32 devices in a mesh: seq: 2 (over core), dp: 16 (over z, y, x).
Axes of the slice: x: 2, y: 2, z: 4, core: 2. Of those that a mesh axis runs over, the one named last changes fastest.
Arguments:
- hidden_in: bfloat16 [2, 16, 768, 768], P(None, 'dp', 'seq'), may hold values from -6 to 6
- encoder_out: bfloat16 [2, 16, 384, 768], P(None, 'dp', 'seq'), may hold values from -6 to 6
- segment_ids: int32 [2, 16, 768], P(None, 'dp', 'seq'), may hold values from 0 to 7, never falling along the last dimension, each value on 1 to 384 neighbouring positions
- passage_counts: int32 [2, 16], P(None, 'dp'), may hold values from 96 to 384, as said below
- cotangent: bfloat16 [2, 16, 768, 768], P(None, 'dp', 'seq'), may hold values from -6 to 6
- w_query: bfloat16 [768, 768], P('dp'), may hold values from -0.0546875 to 0.0546875
- w_key: bfloat16 [768, 768], P('dp'), may hold values from -0.21875 to 0.21875
- w_value: bfloat16 [768, 768], P('dp'), may hold values from -0.21875 to 0.21875
- w_out: bfloat16 [768, 768], P('dp'), may hold values from -0.625 to 0.625
- w_cross_query: bfloat16 [768, 768], P('dp'), may hold values from -0.0546875 to 0.0546875
- w_cross_key: bfloat16 [768, 768], P('dp'), may hold values from -0.21875 to 0.21875
- w_cross_value: bfloat16 [768, 768], P('dp'), may hold values from -0.21875 to 0.21875
- w_cross_out: bfloat16 [768, 768], P('dp'), may hold values from -0.875 to 0.875
- w_ffn_in: bfloat16 [768, 3072], P('dp'), may hold values from -0.21875 to 0.21875
- w_ffn_out: bfloat16 [3072, 768], P('dp'), may hold values from -0.15625 to 0.15625
- gain_self: bfloat16 [768], P('dp'), may hold values from 0.5 to 1.5
- gain_cross: bfloat16 [768], P('dp'), may hold values from 0.5 to 1.5
- gain_ffn: bfloat16 [768], P('dp'), may hold values from 0.5 to 1.5
Outputs:
- out_hidden: bfloat16 [2, 16, 768, 768], P(None, 'dp', 'seq')
- grad_hidden: float32 [2, 16, 768, 768], P(None, 'dp', 'seq')
- grad_encoder: float32 [2, 16, 384, 768], P(None, 'dp', 'seq')
- grad_w_query: float32 [768, 768], P('dp')
- grad_w_key: float32 [768, 768], P('dp')
- grad_w_value: float32 [768, 768], P('dp')
- grad_w_out: float32 [768, 768], P('dp')
- grad_w_cross_query: float32 [768, 768], P('dp')
- grad_w_cross_key: float32 [768, 768], P('dp')
- grad_w_cross_value: float32 [768, 768], P('dp')
- grad_w_cross_out: float32 [768, 768], P('dp')
- grad_w_ffn_in: float32 [768, 3072], P('dp')
- grad_w_ffn_out: float32 [3072, 768], P('dp')
- grad_gain_self: float32 [768], P('dp')
- grad_gain_cross: float32 [768], P('dp')
- grad_gain_ffn: float32 [768], P('dp')
The draws below stay inside these ranges and needn't reach their ends.
Inputs may be any that keep to these rules, and one draw needn't show every extreme that they name: `segment_ids`: within each sequence segment numbers never fall, and each segment has 1 to 384 tokens. `passage_counts`: in every micro-batch some sequence has all 384 encoder tokens valid.
All inputs are finite; a program needn't handle non-finite values.
Results may differ from the reference program's by a relative error of at most 0.025.
The reference program's roundings to bfloat16 on the way count: a program that leaves them out, or rounds other values in their place, can miss the bound.
Values may be sent and summed in bfloat16 or wider, within the bound.
No kernel may reach another device: no remote copies, remote signals or barrier semaphores. Data moves between devices by JAX's collectives and lax.ppermute only.
A program may use at most 192 MiB of HBM per device.

```python
import math
import jax
import jax.numpy as jnp
import numpy as np
from jax import lax

D = 768
HEADS = 12
HEAD_DIM = 64
FF = 3072
MICRO = 2
SEQ_LEN = 768
SEG_COUNT = 8
SEQS = 16
ENC = 384


def draw_passage_counts(key, part):
    first_key, second_key = jax.random.split(key)
    counts = jax.random.randint(first_key, (MICRO, SEQS), ENC // 4, ENC + 1)
    chosen = jax.random.randint(second_key, (MICRO, 1), 0, SEQS)
    places = lax.broadcasted_iota(jnp.int32, (MICRO, SEQS), 1)
    return jnp.where(places == chosen, ENC, counts).astype(jnp.int32)


def levels(rng, extent, cuts, least, high):
    level = 1.0
    for axis_at, parts in cuts:
        heights = jax.random.uniform(jax.random.fold_in(jax.random.fold_in(rng, 6), axis_at), (parts,), jnp.float32, least / len(cuts), high / len(cuts))
        level = level * jnp.repeat(jnp.exp(heights), extent[axis_at] // parts).reshape((-1,) + (1,) * (len(extent) - 1 - axis_at))
    return level


def profile(number_of, total, limit, skew):
    portions = [(1 << 20) // math.isqrt(standing ** skew) + 1 for standing in range(2, number_of + 1)]
    spare, holding = total - limit - (number_of - 1), [1] * (number_of - 1)
    while spare > 0:
        candidates = [i for i in range(number_of - 1) if holding[i] < limit]
        whole, budget = sum([portions[i] for i in candidates]), spare
        for i in candidates:
            addition = min(limit - holding[i], max(1, budget * portions[i] // whole), spare)
            holding[i] = holding[i] + addition
            spare = spare - addition
    return np.array([limit] + holding)


def uneven_parts(rng, number_of, total, limit, lean):
    if number_of == 2:
        one = jax.random.randint(rng, (), max(1, total - limit), min(limit, total - 1) + 1)
        return jnp.stack([one, total - one])
    sizes = jnp.asarray(profile(number_of, total, limit, lean), jnp.int32)
    couples = (number_of - 1) // 2
    giver, sink = sizes[1:1 + 2 * couples:2], sizes[2:2 + 2 * couples:2]
    margin = jnp.minimum(giver - 1, limit - sink)
    passed = jax.random.randint(jax.random.fold_in(rng, 1), (couples,), 0, 1 << 20) % (margin + 1)
    sizes = sizes.at[1:1 + 2 * couples:2].set(giver - passed).at[2:2 + 2 * couples:2].set(sink + passed)
    return sizes[jax.random.permutation(jax.random.fold_in(rng, 2), number_of)]


def centred(own_key, shape, scale, reach, cuts=(), dtype=jnp.bfloat16):
    drawn = scale * jax.random.normal(own_key, shape, jnp.float32)
    if cuts:
        drawn = drawn * levels(own_key, shape, cuts, -0.22, 0.18)
    return jnp.clip(drawn, -reach, reach).astype(dtype)


def setup_inputs(seed: int = 0) -> dict:
    seeds = jax.random.split(jax.random.key(seed), 19)
    hidden_in = centred(seeds[0], (MICRO, SEQS, SEQ_LEN, D), 1.0, 6.0, ((1, 16), (2, 2)))
    encoder_out = centred(seeds[1], (MICRO, SEQS, ENC, D), 1.0, 6.0, ((1, 16), (2, 2)))
    segment_ids = jax.vmap(lambda own: jnp.searchsorted(jnp.cumsum(uneven_parts(own, SEG_COUNT, SEQ_LEN, SEQ_LEN // 2, 2)), jnp.arange(SEQ_LEN), side="right"))(jax.random.split(seeds[2], MICRO * SEQS)).reshape((MICRO, SEQS, SEQ_LEN)).astype(jnp.int32)
    passage_counts = draw_passage_counts(jax.random.fold_in(seeds[18], 71), 0)
    cotangent = centred(seeds[4], (MICRO, SEQS, SEQ_LEN, D), 1.0, 6.0, ((1, 16), (2, 2)))
    w_query = centred(seeds[5], (D, D), (D * HEAD_DIM // 4) ** -0.5, 0.0546875, ((0, 16),))
    w_key = centred(seeds[6], (D, D), D ** -0.5, 0.21875, ((0, 16),))
    w_value = centred(seeds[7], (D, D), D ** -0.5, 0.21875, ((0, 16),))
    w_out = centred(seeds[8], (D, D), (D // 8) ** -0.5, 0.625, ((0, 16),))
    w_cross_query = centred(seeds[9], (D, D), (D * HEAD_DIM // 4) ** -0.5, 0.0546875, ((0, 16),))
    w_cross_key = centred(seeds[10], (D, D), D ** -0.5, 0.21875, ((0, 16),))
    w_cross_value = centred(seeds[11], (D, D), D ** -0.5, 0.21875, ((0, 16),))
    w_cross_out = centred(seeds[12], (D, D), (D // 16) ** -0.5, 0.875, ((0, 16),))
    w_ffn_in = centred(seeds[13], (D, FF), D ** -0.5, 0.21875, ((0, 16),))
    w_ffn_out = centred(seeds[14], (FF, D), (FF // 2) ** -0.5, 0.15625, ((0, 16),))
    gain_self = jnp.clip(1.0 + 0.1 * jax.random.normal(seeds[15], (D,), jnp.float32), 0.5, 1.5).astype(jnp.bfloat16)
    gain_cross = jnp.clip(1.0 + 0.1 * jax.random.normal(seeds[16], (D,), jnp.float32), 0.5, 1.5).astype(jnp.bfloat16)
    gain_ffn = jnp.clip(1.0 + 0.1 * jax.random.normal(seeds[17], (D,), jnp.float32), 0.5, 1.5).astype(jnp.bfloat16)
    return {"hidden_in": hidden_in, "encoder_out": encoder_out, "segment_ids": segment_ids, "passage_counts": passage_counts, "cotangent": cotangent, "w_query": w_query, "w_key": w_key, "w_value": w_value, "w_out": w_out, "w_cross_query": w_cross_query, "w_cross_key": w_cross_key, "w_cross_value": w_cross_value, "w_cross_out": w_cross_out, "w_ffn_in": w_ffn_in, "w_ffn_out": w_ffn_out, "gain_self": gain_self, "gain_cross": gain_cross, "gain_ffn": gain_ffn}


EPS = 1e-06
NEG = -1e+30
EXACT = lax.Precision.HIGHEST
GELU_RATE = 0.7978845608
GELU_CUBIC = 0.044715

@jax.custom_vjp
def low(v):
    return lax.optimization_barrier(v.astype(jnp.bfloat16)).astype(jnp.float32)

@jax.custom_vjp
def low_back(v):
    return v

def low_keep(v):
    return (low(v), None)

def low_pass(kept, grad):
    return (grad,)

def back_keep(v):
    return (v, None)

def back_low(kept, grad):
    return (low(grad),)
low.defvjp(low_keep, low_pass)
low_back.defvjp(back_keep, back_low)

def smooth_act(values):
    return 0.5 * values * (1.0 + jnp.tanh(GELU_RATE * (values + GELU_CUBIC * values * values * values)))

def matmul_exact(left, right):
    return jnp.dot(left, right, precision=EXACT)

def rms_norm(values, gain):
    return values * lax.rsqrt(lax.optimization_barrier(jnp.mean(values * values, axis=-1, keepdims=True)) + EPS) * gain

def attention(queries, key_rows, value_rows, allowed):
    rows = queries.shape[0]
    query_heads = queries.reshape(rows, HEADS, HEAD_DIM)
    key_heads = key_rows.reshape(key_rows.shape[0], HEADS, HEAD_DIM)
    value_heads = value_rows.reshape(value_rows.shape[0], HEADS, HEAD_DIM)
    scores = low_back(jnp.einsum('qhd,khd->hqk', query_heads, key_heads, precision=EXACT))
    scores = jnp.where(allowed[None], scores, NEG)
    row_max = lax.optimization_barrier(jnp.max(scores, axis=-1, keepdims=True))
    exponents = jnp.exp(scores - row_max)
    attn_probs = low(exponents / lax.optimization_barrier(jnp.sum(exponents, axis=-1, keepdims=True)))
    mixed = jnp.einsum('hqk,khd->qhd', attn_probs, value_heads, precision=EXACT)
    return mixed.reshape(rows, HEADS * HEAD_DIM)

def decoder_layer(hidden, encoded, segments, enc_count, weights):
    w_query, w_key, w_value, w_out, w_cross_query, w_cross_key, w_cross_value, w_cross_out, w_ffn_in, w_ffn_out, gain_self, gain_cross, gain_ffn = weights
    length = hidden.shape[0]
    positions = lax.broadcasted_iota(jnp.int32, (length, length), 0)
    key_places = lax.broadcasted_iota(jnp.int32, (length, length), 1)
    self_mask = (key_places <= positions) & (segments[:, None] == segments[None, :])
    enc_places = lax.broadcasted_iota(jnp.int32, (length, encoded.shape[0]), 1)
    cross_mask = enc_places < enc_count
    normed_self = low(rms_norm(hidden, gain_self))
    queries = low_back(low(matmul_exact(normed_self, w_query)))
    key_rows = low_back(low(matmul_exact(normed_self, w_key)))
    value_rows = low_back(low(matmul_exact(normed_self, w_value)))
    attended = low_back(low(attention(queries, key_rows, value_rows, self_mask)))
    after_self = hidden + low_back(matmul_exact(attended, w_out))
    normed_cross = low(rms_norm(after_self, gain_cross))
    cross_queries = low_back(low(matmul_exact(normed_cross, w_cross_query)))
    cross_keys = low_back(low(matmul_exact(encoded, w_cross_key)))
    cross_values = low_back(low(matmul_exact(encoded, w_cross_value)))
    cross_attended = low_back(low(attention(cross_queries, cross_keys, cross_values, cross_mask)))
    after_cross = after_self + low_back(matmul_exact(cross_attended, w_cross_out))
    normed_ffn = low(rms_norm(after_cross, gain_ffn))
    pre_act = low_back(matmul_exact(normed_ffn, w_ffn_in))
    hidden_act = low(smooth_act(pre_act))
    return after_cross + low_back(matmul_exact(hidden_act, w_ffn_out))

def add_terms(left, right):
    return tuple((first_term + second_term for first_term, second_term in zip(left, right)))

def reference(hidden_in, encoder_out, segment_ids, passage_counts, cotangent, w_query, w_key, w_value, w_out, w_cross_query, w_cross_key, w_cross_value, w_cross_out, w_ffn_in, w_ffn_out, gain_self, gain_cross, gain_ffn):
    params = tuple((weight.astype(jnp.float32) for weight in (w_query, w_key, w_value, w_out, w_cross_query, w_cross_key, w_cross_value, w_cross_out, w_ffn_in, w_ffn_out, gain_self, gain_cross, gain_ffn)))
    number = MICRO * SEQS
    inputs = hidden_in.reshape(number, SEQ_LEN, D).astype(jnp.float32)
    encoded_all = encoder_out.reshape(number, ENC, D).astype(jnp.float32)
    segments_all = segment_ids.reshape(number, SEQ_LEN).astype(jnp.int32)
    counts_all = passage_counts.reshape(number).astype(jnp.int32)
    cotangents = cotangent.reshape(number, SEQ_LEN, D).astype(jnp.float32)

    def one_sequence(running, element):
        hidden, encoded, segments, enc_count, d_out = element

        def forward(hidden_rows, enc_rows, weights):
            return decoder_layer(hidden_rows, enc_rows, segments, enc_count, weights)
        result, pullback = jax.vjp(forward, hidden, encoded, params)
        d_hidden, d_encoded, d_params = pullback(d_out)
        return (add_terms(running, d_params), (result.astype(jnp.bfloat16), d_hidden, d_encoded))
    zeros = tuple((jnp.zeros_like(weight) for weight in params))
    sums, outputs = lax.scan(one_sequence, zeros, (inputs, encoded_all, segments_all, counts_all, cotangents))
    results, d_hiddens, d_encodeds = outputs
    grad_query, grad_key, grad_value, grad_out, grad_cross_query, grad_cross_key, grad_cross_value, grad_cross_out, grad_ffn_in, grad_ffn_out, grad_gain_self, grad_gain_cross, grad_gain_ffn = sums
    return (results.reshape(MICRO, SEQS, SEQ_LEN, D), d_hiddens.reshape(MICRO, SEQS, SEQ_LEN, D), d_encodeds.reshape(MICRO, SEQS, ENC, D), grad_query, grad_key, grad_value, grad_out, grad_cross_query, grad_cross_key, grad_cross_value, grad_cross_out, grad_ffn_in, grad_ffn_out, grad_gain_self, grad_gain_cross, grad_gain_ffn)
```

```python
import functools

import jax
import jax.numpy as jnp
from jax import lax
from jax.experimental import pallas as pl
from jax.experimental.pallas import tpu as pltpu
from jax.sharding import PartitionSpec as P

HEAD_DIM = 64
LANES = 128
SEGMENT_LIMIT = 384
QUERY_BLOCK = 256
EPS = 1e-06
NEG = -1e30
GELU_RATE = 0.7978845608
GELU_CUBIC = 0.044715
BF16 = jnp.bfloat16
F32 = jnp.float32
VMEM_LIMIT = 56 << 20


def smooth_act(values):
    return (
        0.5
        * values
        * (1.0 + jnp.tanh(GELU_RATE * (values + GELU_CUBIC * values * values * values)))
    )


def smooth_slope(values):
    bent = jnp.tanh(GELU_RATE * (values + GELU_CUBIC * values * values * values))
    return 0.5 * (1.0 + bent) + 0.5 * values * (1.0 - bent * bent) * GELU_RATE * (
        1.0 + 3.0 * GELU_CUBIC * values * values
    )


def product(left, right):
    return jnp.dot(left, right, preferred_element_type=F32)


def row_outer(left, right):
    return lax.dot_general(left, right, (((0,), (0,)), ((), ())), preferred_element_type=F32)


def right_transposed(left, right):
    return lax.dot_general(left, right, (((1,), (1,)), ((), ())), preferred_element_type=F32)


def inverse_rms(values):
    return lax.rsqrt(jnp.mean(values * values, axis=-1, keepdims=True) + EPS)


def norm_backward(values, scale, gain, d_normed):
    scaled = gain * d_normed
    d_values = scale * scaled - values * (scale * scale * scale) * jnp.mean(
        values * scaled, axis=-1, keepdims=True
    )
    return (d_values, jnp.sum(values * scale * d_normed, axis=0))


def self_blocks(length):
    blocks = []
    for start in range(0, length, QUERY_BLOCK):
        end = min(start + QUERY_BLOCK, length)
        first = max(0, start - SEGMENT_LIMIT + 1) // LANES * LANES
        blocks.append((start, end, first, end))
    return blocks


def cross_blocks(length, keys):
    return [
        (start, min(start + QUERY_BLOCK, length), 0, keys)
        for start in range(0, length, QUERY_BLOCK)
    ]


def of_head(values, head):
    lanes = lax.broadcasted_iota(jnp.int32, values.shape, 1)
    return jnp.where(lanes // HEAD_DIM == head, values, jnp.zeros_like(values))


def pair_forward(blocks, bias_of, q_ref, k_ref, v_ref, o_ref, lse_ref, lse_cols):
    pair = pl.program_id(0)
    lane = lax.broadcasted_iota(jnp.int32, (1, LANES), 1)
    for start, end, first, last in blocks:
        keys = k_ref[first:last, :]
        values = v_ref[first:last, :]
        query_pair = q_ref[start:end, :]
        bias = bias_of(start, end, first, last)
        mixed = []
        columns = lse_cols[start:end, :]
        for head in range(2):
            scores = right_transposed(of_head(query_pair, head), keys) + bias
            row_max = jnp.max(scores, axis=-1, keepdims=True)
            exponents = jnp.exp(scores - row_max)
            totals = jnp.sum(exponents, axis=-1, keepdims=True)
            mixed.append(product(exponents.astype(BF16), values) / totals)
            columns = jnp.where(lane == 2 * pair + head, row_max + jnp.log(totals), columns)
        o_ref[start:end, :] = jnp.where(lane < HEAD_DIM, mixed[0], mixed[1]).astype(BF16)
        lse_cols[start:end, :] = columns

    @pl.when(pair == pl.num_programs(0) - 1)
    def _():
        lse_ref[...] = jnp.transpose(lse_cols[...])[: lse_ref.shape[0], :]


def pair_backward(blocks, bias_of, q_ref, k_ref, v_ref, d_ref, lse_ref, dk_acc, dv_acc):
    pair = pl.program_id(0)
    dk_acc[...] = jnp.zeros_like(dk_acc)
    dv_acc[...] = jnp.zeros_like(dv_acc)
    d_queries = []
    for start, end, first, last in blocks:
        keys = k_ref[first:last, :]
        values = v_ref[first:last, :]
        query_pair = q_ref[start:end, :]
        d_pair = d_ref[start:end, :]
        bias = bias_of(start, end, first, last)
        d_query = None
        for head in range(2):
            query_head = of_head(query_pair, head)
            d_head = of_head(d_pair, head)
            log_totals = lse_ref[pl.ds(2 * pair + head, 1), start:end]
            exact = jnp.exp(right_transposed(keys, query_head) + (bias - log_totals))
            d_probs = right_transposed(values, d_head)
            inner = jnp.sum(exact * d_probs, axis=0, keepdims=True)
            d_scores = (exact * (d_probs - inner)).astype(BF16)
            dv_acc[first:last, :] += product(exact.astype(BF16), d_head)
            dk_acc[first:last, :] += product(d_scores, query_head)
            part = row_outer(d_scores, of_head(keys, head))
            d_query = part if d_query is None else d_query + part
        d_queries.append((start, end, d_query))
    return d_queries


def self_forward_kernel(
    blocks, seg_row, seg_col, q_ref, k_ref, v_ref, o_ref, lse_ref, bias, lse_cols
):
    @pl.when(pl.program_id(0) == 0)
    def _():
        rows = lax.broadcasted_iota(jnp.int32, bias.shape, 0)
        columns = lax.broadcasted_iota(jnp.int32, bias.shape, 1)
        allowed = (columns <= rows) & (seg_col[...] == seg_row[...])
        bias[...] = jnp.where(allowed, 0.0, NEG)
        lse_cols[...] = jnp.zeros_like(lse_cols)

    pair_forward(
        blocks,
        lambda start, end, first, last: bias[start:end, first:last],
        q_ref,
        k_ref,
        v_ref,
        o_ref,
        lse_ref,
        lse_cols,
    )


def self_backward_kernel(
    blocks,
    seg_row,
    seg_col,
    q_ref,
    k_ref,
    v_ref,
    d_ref,
    lse_ref,
    out_ref,
    bias,
    dk_acc,
    dv_acc,
):
    @pl.when(pl.program_id(0) == 0)
    def _():
        rows = lax.broadcasted_iota(jnp.int32, bias.shape, 0)
        columns = lax.broadcasted_iota(jnp.int32, bias.shape, 1)
        allowed = (rows <= columns) & (seg_col[...] == seg_row[...])
        bias[...] = jnp.where(allowed, 0.0, NEG)

    width = out_ref.shape[1] // 3
    d_queries = pair_backward(
        blocks,
        lambda start, end, first, last: bias[first:last, start:end],
        q_ref,
        k_ref,
        v_ref,
        d_ref,
        lse_ref,
        dk_acc,
        dv_acc,
    )
    place = pl.multiple_of(pl.program_id(0) * LANES, LANES)
    for start, end, d_query in d_queries:
        out_ref[start:end, pl.ds(place, LANES)] = d_query.astype(BF16)
    out_ref[:, pl.ds(width + place, LANES)] = dk_acc[...].astype(BF16)
    out_ref[:, pl.ds(2 * width + place, LANES)] = dv_acc[...].astype(BF16)


def cross_forward_kernel(blocks, count, q_ref, k_ref, v_ref, o_ref, lse_ref, lse_cols):
    @pl.when(pl.program_id(0) == 0)
    def _():
        lse_cols[...] = jnp.zeros_like(lse_cols)

    places = lax.broadcasted_iota(jnp.int32, (1, k_ref.shape[0]), 1)
    bias = jnp.where(places < count[0], 0.0, NEG)
    pair_forward(
        blocks,
        lambda start, end, first, last: bias,
        q_ref,
        k_ref,
        v_ref,
        o_ref,
        lse_ref,
        lse_cols,
    )


def cross_backward_kernel(
    blocks,
    count,
    q_ref,
    k_ref,
    v_ref,
    d_ref,
    lse_ref,
    dq_ref,
    dkv_ref,
    dk_acc,
    dv_acc,
):
    places = lax.broadcasted_iota(jnp.int32, (k_ref.shape[0], 1), 0)
    bias = jnp.where(places < count[0], 0.0, NEG)
    width = dkv_ref.shape[1] // 2
    d_queries = pair_backward(
        blocks,
        lambda start, end, first, last: bias,
        q_ref,
        k_ref,
        v_ref,
        d_ref,
        lse_ref,
        dk_acc,
        dv_acc,
    )
    place = pl.multiple_of(pl.program_id(0) * LANES, LANES)
    for start, end, d_query in d_queries:
        dq_ref[start:end, :] = d_query.astype(BF16)
    dkv_ref[:, pl.ds(place, LANES)] = dk_acc[...].astype(BF16)
    dkv_ref[:, pl.ds(width + place, LANES)] = dv_acc[...].astype(BF16)


def columns(rows, offset):
    return pl.BlockSpec((rows, LANES), lambda pair: (0, offset + pair))


def whole(shape):
    return pl.BlockSpec(shape, lambda pair: (0,) * len(shape))


def params():
    return pltpu.CompilerParams(
        dimension_semantics=("arbitrary",), vmem_limit_bytes=VMEM_LIMIT
    )


def self_forward(qkv, seg_row, seg_col):
    length, width = qkv.shape[0], qkv.shape[1] // 3
    pairs = width // LANES
    return pl.pallas_call(
        functools.partial(self_forward_kernel, self_blocks(length)),
        grid=(pairs,),
        in_specs=[
            whole(seg_row.shape),
            whole(seg_col.shape),
            columns(length, 0),
            columns(length, pairs),
            columns(length, 2 * pairs),
        ],
        out_specs=[columns(length, 0), whole((16, length))],
        out_shape=[
            jax.ShapeDtypeStruct((length, width), BF16),
            jax.ShapeDtypeStruct((16, length), F32),
        ],
        scratch_shapes=[
            pltpu.VMEM((length, length), F32),
            pltpu.VMEM((length, LANES), F32),
        ],
        compiler_params=params(),
        cost_estimate=pl.CostEstimate(
            flops=3 * length * length * width,
            bytes_accessed=8 * length * width,
            transcendentals=length * length * width // 128,
        ),
        name="self_forward",
    )(seg_row, seg_col, qkv, qkv, qkv)


def self_backward(qkv, d_mixed, lse, seg_row, seg_col):
    length, width = d_mixed.shape
    pairs = width // LANES
    return pl.pallas_call(
        functools.partial(self_backward_kernel, self_blocks(length)),
        grid=(pairs,),
        in_specs=[
            whole(seg_row.shape),
            whole(seg_col.shape),
            columns(length, 0),
            columns(length, pairs),
            columns(length, 2 * pairs),
            columns(length, 0),
            whole(lse.shape),
        ],
        out_specs=whole(qkv.shape),
        out_shape=jax.ShapeDtypeStruct(qkv.shape, BF16),
        scratch_shapes=[
            pltpu.VMEM((length, length), F32),
            pltpu.VMEM((length, LANES), F32),
            pltpu.VMEM((length, LANES), F32),
        ],
        compiler_params=params(),
        cost_estimate=pl.CostEstimate(
            flops=7 * length * length * width,
            bytes_accessed=14 * length * width,
            transcendentals=length * length * width // 128,
        ),
        name="self_backward",
    )(seg_row, seg_col, qkv, qkv, qkv, d_mixed, lse)


def cross_forward(queries, kv, count):
    length, width = queries.shape
    keys = kv.shape[0]
    pairs = width // LANES
    return pl.pallas_call(
        functools.partial(cross_forward_kernel, cross_blocks(length, keys)),
        grid=(pairs,),
        in_specs=[
            pl.BlockSpec(memory_space=pltpu.SMEM),
            columns(length, 0),
            columns(keys, 0),
            columns(keys, pairs),
        ],
        out_specs=[columns(length, 0), whole((16, length))],
        out_shape=[
            jax.ShapeDtypeStruct((length, width), BF16),
            jax.ShapeDtypeStruct((16, length), F32),
        ],
        scratch_shapes=[pltpu.VMEM((length, LANES), F32)],
        compiler_params=params(),
        cost_estimate=pl.CostEstimate(
            flops=4 * length * keys * width,
            bytes_accessed=6 * length * width,
            transcendentals=length * keys * width // 64,
        ),
        name="cross_forward",
    )(count, queries, kv, kv)


def cross_backward(queries, kv, d_mixed, lse, count):
    length, width = queries.shape
    keys = kv.shape[0]
    pairs = width // LANES
    return pl.pallas_call(
        functools.partial(cross_backward_kernel, cross_blocks(length, keys)),
        grid=(pairs,),
        in_specs=[
            pl.BlockSpec(memory_space=pltpu.SMEM),
            columns(length, 0),
            columns(keys, 0),
            columns(keys, pairs),
            columns(length, 0),
            whole(lse.shape),
        ],
        out_specs=[columns(length, 0), whole(kv.shape)],
        out_shape=[
            jax.ShapeDtypeStruct((length, width), BF16),
            jax.ShapeDtypeStruct(kv.shape, BF16),
        ],
        scratch_shapes=[
            pltpu.VMEM((keys, LANES), F32),
            pltpu.VMEM((keys, LANES), F32),
        ],
        compiler_params=params(),
        cost_estimate=pl.CostEstimate(
            flops=10 * length * keys * width,
            bytes_accessed=10 * length * width,
            transcendentals=length * keys * width // 64,
        ),
        name="cross_backward",
    )(count, queries, kv, kv, d_mixed, lse)


def on_device(
    hidden_in,
    encoder_out,
    segment_ids,
    passage_counts,
    cotangent,
    w_query,
    w_key,
    w_value,
    w_out,
    w_cross_query,
    w_cross_key,
    w_cross_value,
    w_cross_out,
    w_ffn_in,
    w_ffn_out,
    gain_self,
    gain_cross,
    gain_ffn,
):
    cores = lax.axis_size("seq")
    core = lax.axis_index("seq")
    members = cores * lax.axis_size("dp")
    width = hidden_in.shape[-1]
    ratio = w_ffn_in.shape[1] // width
    part = w_query.shape[0] // cores
    joint = ("dp", "seq")

    def own_rows(values):
        rows = values.shape[0] // cores
        return lax.dynamic_slice_in_dim(values, core * rows, rows, 0)

    gains = jnp.stack([gain_self, gain_cross, gain_ffn], axis=1)
    gains = jnp.pad(gains, ((0, 0), (0, LANES - gains.shape[1])))
    attention_rows = jnp.concatenate(
        [
            own_rows(v)
            for v in (
                w_query,
                w_key,
                w_value,
                w_cross_key,
                w_cross_value,
                w_out,
                w_cross_query,
                w_cross_out,
                gains,
            )
        ],
        axis=1,
    )
    ffn_in_rows = (
        own_rows(w_ffn_in).reshape(part, ratio, width).transpose(1, 0, 2).reshape(-1, width)
    )
    ffn_rows = jnp.concatenate([ffn_in_rows, own_rows(w_ffn_out)], axis=1)
    attention_set = lax.all_gather(attention_rows, joint, axis=0, tiled=True)
    ffn_set = lax.all_gather(ffn_rows, joint, axis=0, tiled=True)
    w_qkv = attention_set[:, : 3 * width]
    w_ckv = attention_set[:, 3 * width : 5 * width]
    w_o = attention_set[:, 5 * width : 6 * width]
    w_cq = attention_set[:, 6 * width : 7 * width]
    w_co = attention_set[:, 7 * width : 8 * width]
    g_self, g_cross, g_ffn = (
        attention_set[:, 8 * width + i].astype(F32)[None, :] for i in range(3)
    )
    w_in = (
        ffn_set[:, :width]
        .reshape(members, ratio, part, width)
        .transpose(0, 2, 1, 3)
        .reshape(width, ratio * width)
    )
    w_ff_out = ffn_set[:, width:]

    def dealt(values):
        return lax.all_to_all(values[:, 0], "seq", split_axis=0, concat_axis=1, tiled=True)

    def returned(values):
        values = lax.all_to_all(values, "seq", split_axis=1, concat_axis=0, tiled=True)
        return values[:, None]

    hidden_all = dealt(hidden_in)
    encoded_all = dealt(encoder_out)
    segments_all = dealt(segment_ids)
    cotangent_all = dealt(cotangent)
    turns = hidden_all.shape[0]
    outputs, input_grads, encoder_grads, running = [], [], [], None
    for turn in range(turns):
        count = lax.dynamic_slice_in_dim(passage_counts[:, 0], core * turns + turn, 1, 0)
        hidden = hidden_all[turn].astype(F32)
        encoded = encoded_all[turn]
        seg_row = segments_all[turn][None, :]
        seg_col = segments_all[turn][:, None]
        scale_self = inverse_rms(hidden)
        normed_self = (hidden * scale_self * g_self).astype(BF16)
        qkv = product(normed_self, w_qkv).astype(BF16)
        ckv = product(encoded, w_ckv).astype(BF16)
        attended, self_lse = self_forward(qkv, seg_row, seg_col)
        after_self = hidden + product(attended, w_o)
        scale_cross = inverse_rms(after_self)
        normed_cross = (after_self * scale_cross * g_cross).astype(BF16)
        cross_queries = product(normed_cross, w_cq).astype(BF16)
        cross_attended, cross_lse = cross_forward(cross_queries, ckv, count)
        after_cross = after_self + product(cross_attended, w_co)
        scale_ffn = inverse_rms(after_cross)
        normed_ffn = (after_cross * scale_ffn * g_ffn).astype(BF16)
        pre_act = product(normed_ffn, w_in)
        hidden_act = smooth_act(pre_act).astype(BF16)
        outputs.append((after_cross + product(hidden_act, w_ff_out)).astype(BF16))

        branch_ffn = cotangent_all[turn]
        d_block = branch_ffn.astype(F32)
        grad_ffn_out = row_outer(hidden_act, branch_ffn)
        d_pre = (right_transposed(branch_ffn, w_ff_out) * smooth_slope(pre_act)).astype(BF16)
        grad_ffn_in = row_outer(normed_ffn, d_pre)
        d_norm_ffn, grad_gain_ffn = norm_backward(
            after_cross, scale_ffn, g_ffn, right_transposed(d_pre, w_in)
        )
        d_after_cross = d_block + d_norm_ffn
        branch_cross = d_after_cross.astype(BF16)
        grad_cross_out = row_outer(cross_attended, branch_cross)
        d_cross_att = right_transposed(branch_cross, w_co).astype(BF16)
        dq_cross, dkv_cross = cross_backward(cross_queries, ckv, d_cross_att, cross_lse, count)
        grad_cross_query = row_outer(normed_cross, dq_cross)
        grad_cross_kv = row_outer(encoded, dkv_cross)
        encoder_grads.append(right_transposed(dkv_cross, w_ckv))
        d_norm_cross, grad_gain_cross = norm_backward(
            after_self, scale_cross, g_cross, right_transposed(dq_cross, w_cq)
        )
        d_after_self = d_after_cross + d_norm_cross
        branch_self = d_after_self.astype(BF16)
        grad_out = row_outer(attended, branch_self)
        d_self_att = right_transposed(branch_self, w_o).astype(BF16)
        d_qkv = self_backward(qkv, d_self_att, self_lse, seg_row, seg_col)
        grad_qkv = row_outer(normed_self, d_qkv)
        d_norm_self, grad_gain_self = norm_backward(
            hidden, scale_self, g_self, right_transposed(d_qkv, w_qkv)
        )
        input_grads.append(d_after_self + d_norm_self)
        grads = (
            grad_qkv,
            grad_cross_kv,
            grad_out,
            grad_cross_query,
            grad_cross_out,
            grad_gain_self,
            grad_gain_cross,
            grad_gain_ffn,
            grad_ffn_in,
            grad_ffn_out,
        )
        running = grads if running is None else tuple(a + b for a, b in zip(running, grads))

    gain_grads = jnp.stack(running[5:8], axis=1).astype(BF16)
    gain_grads = jnp.pad(gain_grads, ((0, 0), (0, LANES - gain_grads.shape[1])))
    attention_grads = jnp.concatenate(
        [v.astype(BF16) for v in running[:5]] + [gain_grads], axis=1
    )
    ffn_in_grads = (
        running[8]
        .astype(BF16)
        .reshape(members, part, ratio, width)
        .transpose(0, 2, 1, 3)
        .reshape(ratio * width, width)
    )
    ffn_grads = jnp.concatenate([ffn_in_grads, running[9].astype(BF16)], axis=1)

    def reduced(values):
        rows = lax.psum_scatter(values, joint, scatter_dimension=0, tiled=True)
        return lax.all_gather(rows, "seq", axis=0, tiled=True)

    ffn_sum = reduced(ffn_grads).astype(F32)
    attention_sum = reduced(attention_grads).astype(F32)
    grad_ffn_in = (
        ffn_sum[:, :width]
        .reshape(cores, ratio, part, width)
        .transpose(0, 2, 1, 3)
        .reshape(cores * part, ratio * width)
    )
    grad_ffn_out = ffn_sum[:, width:]

    def column_block(i):
        return attention_sum[:, i * width : (i + 1) * width]

    return (
        returned(jnp.stack(outputs)),
        returned(jnp.stack(input_grads)),
        returned(jnp.stack(encoder_grads)),
        column_block(0),
        column_block(1),
        column_block(2),
        column_block(5),
        column_block(6),
        column_block(3),
        column_block(4),
        column_block(7),
        grad_ffn_in,
        grad_ffn_out,
        attention_sum[:, 8 * width],
        attention_sum[:, 8 * width + 1],
        attention_sum[:, 8 * width + 2],
    )


def solution(mesh):
    tokens = P(None, "dp", "seq", None)
    rows = P("dp", None)
    gain = P("dp")
    return jax.shard_map(
        on_device,
        mesh=mesh,
        in_specs=(tokens, tokens, P(None, "dp", "seq"), P(None, "dp"), tokens)
        + (rows,) * 10
        + (gain,) * 3,
        out_specs=(tokens,) * 3 + (rows,) * 10 + (gain,) * 3,
        check_vma=False,
    )
```

```python
import functools

import jax
import jax.numpy as jnp
from jax import lax
from jax.experimental import pallas as pl
from jax.experimental.pallas import tpu as pltpu
from jax.sharding import PartitionSpec as P

HEAD_DIM = 64
LANES = 128
SEGMENT_LIMIT = 384
QUERY_BLOCK = 256
EPS = 1e-06
NEG = -1e30
GELU_RATE = 0.7978845608
GELU_CUBIC = 0.044715
BF16 = jnp.bfloat16
F32 = jnp.float32
VMEM_LIMIT = 56 << 20


def smooth_act(values):
    return (
        0.5
        * values
        * (1.0 + jnp.tanh(GELU_RATE * (values + GELU_CUBIC * values * values * values)))
    )


def smooth_slope(values):
    bent = jnp.tanh(GELU_RATE * (values + GELU_CUBIC * values * values * values))
    return 0.5 * (1.0 + bent) + 0.5 * values * (1.0 - bent * bent) * GELU_RATE * (
        1.0 + 3.0 * GELU_CUBIC * values * values
    )


def product(left, right):
    return jnp.dot(left, right, preferred_element_type=F32)


def row_outer(left, right):
    return lax.dot_general(left, right, (((0,), (0,)), ((), ())), preferred_element_type=F32)


def right_transposed(left, right):
    return lax.dot_general(left, right, (((1,), (1,)), ((), ())), preferred_element_type=F32)


def inverse_rms(values):
    return lax.rsqrt(jnp.mean(values * values, axis=-1, keepdims=True) + EPS)


def norm_backward(values, scale, gain, d_normed):
    scaled = gain * d_normed
    d_values = scale * scaled - values * (scale * scale * scale) * jnp.mean(
        values * scaled, axis=-1, keepdims=True
    )
    return (d_values, jnp.sum(values * scale * d_normed, axis=0))


def self_blocks(length):
    blocks = []
    for start in range(0, length, QUERY_BLOCK):
        end = min(start + QUERY_BLOCK, length)
        first = max(0, start - SEGMENT_LIMIT + 1) // LANES * LANES
        blocks.append((start, end, first, end))
    return blocks


def cross_blocks(length, keys):
    return [
        (start, min(start + QUERY_BLOCK, length), 0, keys)
        for start in range(0, length, QUERY_BLOCK)
    ]


def of_head(values, head):
    lanes = lax.broadcasted_iota(jnp.int32, values.shape, 1)
    return jnp.where(lanes // HEAD_DIM == head, values, jnp.zeros_like(values))


def pair_forward(blocks, bias_of, q_ref, k_ref, v_ref, o_ref, lse_ref, lse_cols):
    pair = pl.program_id(0)
    lane = lax.broadcasted_iota(jnp.int32, (1, LANES), 1)
    for start, end, first, last in blocks:
        keys = k_ref[first:last, :]
        values = v_ref[first:last, :]
        query_pair = q_ref[start:end, :]
        bias = bias_of(start, end, first, last)
        mixed = []
        columns = lse_cols[start:end, :]
        for head in range(2):
            scores = right_transposed(of_head(query_pair, head), keys) + bias
            row_max = jnp.max(scores, axis=-1, keepdims=True)
            exponents = jnp.exp(scores - row_max)
            totals = jnp.sum(exponents, axis=-1, keepdims=True)
            mixed.append(product(exponents.astype(BF16), values) / totals)
            columns = jnp.where(lane == 2 * pair + head, row_max + jnp.log(totals), columns)
        o_ref[start:end, :] = jnp.where(lane < HEAD_DIM, mixed[0], mixed[1]).astype(BF16)
        lse_cols[start:end, :] = columns

    @pl.when(pair == pl.num_programs(0) - 1)
    def _():
        lse_ref[...] = jnp.transpose(lse_cols[...])[: lse_ref.shape[0], :]


def pair_backward(blocks, bias_of, q_ref, k_ref, v_ref, d_ref, lse_ref, dk_acc, dv_acc):
    pair = pl.program_id(0)
    dk_acc[...] = jnp.zeros_like(dk_acc)
    dv_acc[...] = jnp.zeros_like(dv_acc)
    d_queries = []
    for start, end, first, last in blocks:
        keys = k_ref[first:last, :]
        values = v_ref[first:last, :]
        query_pair = q_ref[start:end, :]
        d_pair = d_ref[start:end, :]
        bias = bias_of(start, end, first, last)
        d_query = None
        for head in range(2):
            query_head = of_head(query_pair, head)
            d_head = of_head(d_pair, head)
            log_totals = lse_ref[pl.ds(2 * pair + head, 1), start:end]
            exact = jnp.exp(right_transposed(keys, query_head) + (bias - log_totals))
            d_probs = right_transposed(values, d_head)
            inner = jnp.sum(exact * d_probs, axis=0, keepdims=True)
            d_scores = (exact * (d_probs - inner)).astype(BF16)
            dv_acc[first:last, :] += product(exact.astype(BF16), d_head)
            dk_acc[first:last, :] += product(d_scores, query_head)
            part = row_outer(d_scores, of_head(keys, head))
            d_query = part if d_query is None else d_query + part
        d_queries.append((start, end, d_query))
    return d_queries


def masked_bias(seg_col, seg_row, keys_first):
    shape = (seg_col.shape[0], seg_row.shape[1])
    rows = lax.broadcasted_iota(jnp.int32, shape, 0)
    lanes = lax.broadcasted_iota(jnp.int32, shape, 1)
    ordered = rows <= lanes if keys_first else lanes <= rows
    return jnp.where(ordered & (seg_col[...] == seg_row[...]), 0.0, NEG)


def project_kernel(hidden, encoded, gains, weight, normed, qkv, ckv, gain_rows):
    step = pl.program_id(0)

    @pl.when(step == 0)
    def _():
        rows = jnp.transpose(gains[...].astype(F32))[: gain_rows.shape[0], :]
        gain_rows[...] = rows
        values = hidden[...].astype(F32)
        normed[...] = (values * inverse_rms(values) * rows[0:1, :]).astype(BF16)

    @pl.when(step < 3)
    def _():
        qkv[...] = product(normed[...], weight[...]).astype(BF16)

    @pl.when(step >= 3)
    def _():
        ckv[...] = product(encoded[...], weight[...]).astype(BF16)


def self_forward_kernel(
    blocks,
    seg_row,
    seg_col,
    hidden,
    gain_rows,
    q_ref,
    k_ref,
    v_ref,
    w_o,
    w_cq,
    attended,
    lse_ref,
    after_self,
    normed_cross,
    cross_queries,
    bias,
    lse_cols,
    mixed,
):
    @pl.when(pl.program_id(0) == 0)
    def _():
        bias[...] = masked_bias(seg_col, seg_row, False)
        lse_cols[...] = jnp.zeros_like(lse_cols)

    pair_forward(
        blocks,
        lambda start, end, first, last: bias[start:end, first:last],
        q_ref,
        k_ref,
        v_ref,
        mixed,
        lse_ref,
        lse_cols,
    )
    place = pl.multiple_of(pl.program_id(0) * LANES, LANES)
    attended[:, pl.ds(place, LANES)] = mixed[...]

    @pl.when(pl.program_id(0) == pl.num_programs(0) - 1)
    def _():
        values = hidden[...].astype(F32) + product(attended[...], w_o[...])
        after_self[...] = values
        normed = (values * inverse_rms(values) * gain_rows[1:2, :]).astype(BF16)
        normed_cross[...] = normed
        cross_queries[...] = product(normed, w_cq[...]).astype(BF16)


def cross_forward_kernel(
    blocks,
    count,
    after_self,
    gain_rows,
    q_ref,
    k_ref,
    v_ref,
    w_co,
    attended,
    lse_ref,
    after_cross,
    normed_ffn,
    lse_cols,
    mixed,
):
    @pl.when(pl.program_id(0) == 0)
    def _():
        lse_cols[...] = jnp.zeros_like(lse_cols)

    places = lax.broadcasted_iota(jnp.int32, (1, k_ref.shape[0]), 1)
    bias = jnp.where(places < count[0], 0.0, NEG)
    pair_forward(
        blocks,
        lambda start, end, first, last: bias,
        q_ref,
        k_ref,
        v_ref,
        mixed,
        lse_ref,
        lse_cols,
    )
    place = pl.multiple_of(pl.program_id(0) * LANES, LANES)
    attended[:, pl.ds(place, LANES)] = mixed[...]

    @pl.when(pl.program_id(0) == pl.num_programs(0) - 1)
    def _():
        values = after_self[...] + product(attended[...], w_co[...])
        after_cross[...] = values
        normed_ffn[...] = (values * inverse_rms(values) * gain_rows[2:3, :]).astype(BF16)


def ffn_kernel(
    normed,
    branch,
    after_cross,
    gain_rows,
    w_in,
    w_out,
    out_hidden,
    d_after_cross,
    gain_grad,
    grad_in,
    grad_out,
    out_acc,
    dn_acc,
    normed_t,
):
    step = pl.program_id(0)

    @pl.when(step == 0)
    def _():
        normed_t[...] = jnp.transpose(normed[...])
        out_acc[...] = after_cross[...]
        dn_acc[...] = jnp.zeros_like(dn_acc)

    width = normed.shape[1]
    up = w_in[...].reshape(width, -1)
    down = w_out[...]
    pre = product(normed[...], up)
    bent = jnp.tanh(GELU_RATE * (pre + GELU_CUBIC * pre * pre * pre))
    half = 0.5 * (1.0 + bent)
    hidden_act = (pre * half).astype(BF16)
    slope = half + 0.5 * pre * (1.0 - bent * bent) * GELU_RATE * (
        1.0 + 3.0 * GELU_CUBIC * pre * pre
    )
    out_acc[...] += product(hidden_act, down)
    d_pre = (right_transposed(branch[...], down) * slope).astype(BF16)
    grad_out[...] = row_outer(hidden_act, branch[...]).astype(BF16)
    grad_in[...] = product(normed_t[...], d_pre).astype(BF16).reshape(grad_in.shape)
    dn_acc[...] += right_transposed(d_pre, up)

    @pl.when(step == pl.num_programs(0) - 1)
    def _():
        out_hidden[...] = out_acc[...].astype(BF16)
        values = after_cross[...]
        d_values, d_gain = norm_backward(
            values, inverse_rms(values), gain_rows[2:3, :], dn_acc[...]
        )
        d_after_cross[...] = branch[...].astype(F32) + d_values
        gain_grad[...] = jnp.broadcast_to(d_gain, gain_grad.shape)


def cross_backward_kernel(
    blocks,
    count,
    q_ref,
    k_ref,
    v_ref,
    lse_ref,
    d_after_cross,
    after_self,
    normed_cross,
    attended,
    encoded,
    gain_rows,
    w_co,
    w_cq,
    w_ck,
    w_cv,
    d_after_self,
    grads,
    grad_encoded,
    gain_grad,
    d_att,
    dq_all,
    dkv_all,
    dk_acc,
    dv_acc,
):
    step = pl.program_id(0)
    width = d_after_cross.shape[1]

    @pl.when(step == 0)
    def _():
        branch = d_after_cross[...].astype(BF16)
        d_mixed = right_transposed(branch, w_co[...]).astype(BF16)
        for pair in range(d_att.shape[0]):
            d_att[pair] = d_mixed[:, pair * LANES : (pair + 1) * LANES]
        grads[:, 3 * width :] = row_outer(attended[...], branch).astype(BF16)

    places = lax.broadcasted_iota(jnp.int32, (k_ref.shape[0], 1), 0)
    bias = jnp.where(places < count[0], 0.0, NEG)
    d_queries = pair_backward(
        blocks,
        lambda start, end, first, last: bias,
        q_ref,
        k_ref,
        v_ref,
        d_att.at[step],
        lse_ref,
        dk_acc,
        dv_acc,
    )
    place = pl.multiple_of(step * LANES, LANES)
    for start, end, d_query in d_queries:
        dq_all[start:end, pl.ds(place, LANES)] = d_query.astype(BF16)
    dkv_all[:, pl.ds(place, LANES)] = dk_acc[...].astype(BF16)
    dkv_all[:, pl.ds(width + place, LANES)] = dv_acc[...].astype(BF16)

    @pl.when(step == pl.num_programs(0) - 1)
    def _():
        dq = dq_all[...]
        grads[:, 2 * width : 3 * width] = row_outer(normed_cross[...], dq).astype(BF16)
        grads[:, : 2 * width] = row_outer(encoded[...], dkv_all[...]).astype(BF16)
        grad_encoded[...] = right_transposed(dkv_all[:, :width], w_ck[...]) + right_transposed(
            dkv_all[:, width:], w_cv[...]
        )
        values = after_self[...]
        d_values, d_gain = norm_backward(
            values,
            inverse_rms(values),
            gain_rows[1:2, :],
            right_transposed(dq, w_cq[...]),
        )
        d_after_self[...] = d_after_cross[...] + d_values
        gain_grad[...] = jnp.broadcast_to(d_gain, gain_grad.shape)


def self_backward_kernel(
    blocks,
    seg_row,
    seg_col,
    q_ref,
    k_ref,
    v_ref,
    lse_ref,
    d_after_self,
    hidden,
    normed_self,
    attended,
    gain_rows,
    w_o,
    w_q,
    w_k,
    w_v,
    grad_hidden,
    grads,
    gain_grad,
    bias,
    d_att,
    d_all,
    dk_acc,
    dv_acc,
):
    step = pl.program_id(0)
    width = d_after_self.shape[1]

    @pl.when(step == 0)
    def _():
        bias[...] = masked_bias(seg_col, seg_row, True)
        branch = d_after_self[...].astype(BF16)
        d_mixed = right_transposed(branch, w_o[...]).astype(BF16)
        for pair in range(d_att.shape[0]):
            d_att[pair] = d_mixed[:, pair * LANES : (pair + 1) * LANES]
        grads[:, 3 * width :] = row_outer(attended[...], branch).astype(BF16)

    d_queries = pair_backward(
        blocks,
        lambda start, end, first, last: bias[first:last, start:end],
        q_ref,
        k_ref,
        v_ref,
        d_att.at[step],
        lse_ref,
        dk_acc,
        dv_acc,
    )
    place = pl.multiple_of(step * LANES, LANES)
    for start, end, d_query in d_queries:
        d_all[start:end, pl.ds(place, LANES)] = d_query.astype(BF16)
    d_all[:, pl.ds(width + place, LANES)] = dk_acc[...].astype(BF16)
    d_all[:, pl.ds(2 * width + place, LANES)] = dv_acc[...].astype(BF16)

    @pl.when(step == pl.num_programs(0) - 1)
    def _():
        grads[:, : 3 * width] = row_outer(normed_self[...], d_all[...]).astype(BF16)
        d_normed = (
            right_transposed(d_all[:, :width], w_q[...])
            + right_transposed(d_all[:, width : 2 * width], w_k[...])
            + right_transposed(d_all[:, 2 * width :], w_v[...])
        )
        values = hidden[...].astype(F32)
        d_values, d_gain = norm_backward(
            values, inverse_rms(values), gain_rows[0:1, :], d_normed
        )
        grad_hidden[...] = d_after_self[...] + d_values
        gain_grad[...] = jnp.broadcast_to(d_gain, gain_grad.shape)


def columns(rows, offset):
    return pl.BlockSpec((rows, LANES), lambda step: (0, offset + step))


def whole(shape, place=None):
    place = (0,) * len(shape) if place is None else place
    return pl.BlockSpec(shape, lambda step: place)


def like(*shapes):
    return [jax.ShapeDtypeStruct(shape, dtype) for shape, dtype in shapes]


def call(kernel, name, steps, in_specs, out_specs, out_shape, scratch, flops, args):
    size = sum(int(a.size) * a.dtype.itemsize for a in args)
    return pl.pallas_call(
        kernel,
        grid=(steps,),
        in_specs=in_specs,
        out_specs=out_specs,
        out_shape=out_shape,
        scratch_shapes=scratch,
        compiler_params=pltpu.CompilerParams(
            dimension_semantics=("arbitrary",), vmem_limit_bytes=VMEM_LIMIT
        ),
        cost_estimate=pl.CostEstimate(flops=flops, bytes_accessed=size, transcendentals=0),
        name=name,
    )(*args)


QUERY, KEY, VALUE, CROSS_KEY, CROSS_VALUE, OUT, CROSS_QUERY, CROSS_OUT = range(8)


def weight(width, place):
    return whole((width, width), (0, place))


def project(hidden, encoded, attention_set):
    length, width = hidden.shape
    keys = encoded.shape[0]
    return call(
        project_kernel,
        "project",
        5,
        [
            whole(hidden.shape),
            whole(encoded.shape),
            whole((width, LANES), (0, 8 * width // LANES)),
            pl.BlockSpec((width, width), lambda step: (0, step)),
        ],
        [
            whole(hidden.shape),
            pl.BlockSpec((length, width), lambda step: (0, jnp.minimum(step, 2))),
            pl.BlockSpec((keys, width), lambda step: (0, jnp.maximum(step - 3, 0))),
            whole((8, width)),
        ],
        like(
            (hidden.shape, BF16),
            ((length, 3 * width), BF16),
            ((keys, 2 * width), BF16),
            ((8, width), F32),
        ),
        [],
        2 * width * width * (3 * length + 2 * keys),
        (hidden, encoded, attention_set, attention_set),
    )


def self_forward(qkv, seg_row, seg_col, hidden, gain_rows, attention_set):
    length, width = hidden.shape
    pairs = width // LANES
    return call(
        functools.partial(self_forward_kernel, self_blocks(length)),
        "self_forward",
        pairs,
        [
            whole(seg_row.shape),
            whole(seg_col.shape),
            whole(hidden.shape),
            whole(gain_rows.shape),
            columns(length, 0),
            columns(length, pairs),
            columns(length, 2 * pairs),
            weight(width, OUT),
            weight(width, CROSS_QUERY),
        ],
        [
            whole(hidden.shape),
            whole((16, length)),
            whole(hidden.shape),
            whole(hidden.shape),
            whole(hidden.shape),
        ],
        like(
            (hidden.shape, BF16),
            ((16, length), F32),
            (hidden.shape, F32),
            (hidden.shape, BF16),
            (hidden.shape, BF16),
        ),
        [
            pltpu.VMEM((length, length), F32),
            pltpu.VMEM((length, LANES), F32),
            pltpu.VMEM((length, LANES), BF16),
        ],
        4 * length * width * (length + width),
        (
            seg_row,
            seg_col,
            hidden,
            gain_rows,
            qkv,
            qkv,
            qkv,
            attention_set,
            attention_set,
        ),
    )


def cross_forward(queries, ckv, count, after_self, gain_rows, attention_set):
    length, width = queries.shape
    keys = ckv.shape[0]
    pairs = width // LANES
    return call(
        functools.partial(cross_forward_kernel, cross_blocks(length, keys)),
        "cross_forward",
        pairs,
        [
            pl.BlockSpec(memory_space=pltpu.SMEM),
            whole(queries.shape),
            whole(gain_rows.shape),
            columns(length, 0),
            columns(keys, 0),
            columns(keys, pairs),
            weight(width, CROSS_OUT),
        ],
        [
            whole(queries.shape),
            whole((16, length)),
            whole(queries.shape),
            whole(queries.shape),
        ],
        like(
            (queries.shape, BF16),
            ((16, length), F32),
            (queries.shape, F32),
            (queries.shape, BF16),
        ),
        [pltpu.VMEM((length, LANES), F32), pltpu.VMEM((length, LANES), BF16)],
        2 * length * width * (2 * keys + width),
        (count, after_self, gain_rows, queries, ckv, ckv, attention_set),
    )


def feed_forward(normed, branch, after_cross, gain_rows, ffn_set, w_in):
    length, width = normed.shape
    groups, steps, rows, _ = w_in.shape
    block = pl.BlockSpec((groups, 1, rows, width), lambda step: (0, step, 0, 0))
    return call(
        ffn_kernel,
        "feed_forward",
        steps,
        [
            whole(normed.shape),
            whole(normed.shape),
            whole(normed.shape),
            whole(gain_rows.shape),
            block,
            pl.BlockSpec((width, width), lambda step: (step, 1)),
        ],
        [
            whole(normed.shape),
            whole(normed.shape),
            whole((8, width)),
            block,
            pl.BlockSpec((width, width), lambda step: (step, 0)),
        ],
        like(
            (normed.shape, BF16),
            (normed.shape, F32),
            ((8, width), F32),
            ((groups, steps, rows, width), BF16),
            ((steps * width, width), BF16),
        ),
        [
            pltpu.VMEM(normed.shape, F32),
            pltpu.VMEM(normed.shape, F32),
            pltpu.VMEM((width, length), BF16),
        ],
        12 * length * width * width * steps,
        (normed, branch, after_cross, gain_rows, w_in, ffn_set),
    )


def cross_backward(
    queries,
    ckv,
    count,
    lse,
    d_after_cross,
    after_self,
    normed_cross,
    attended,
    encoded,
    gain_rows,
    attention_set,
):
    length, width = queries.shape
    keys = ckv.shape[0]
    pairs = width // LANES
    return call(
        functools.partial(cross_backward_kernel, cross_blocks(length, keys)),
        "cross_backward",
        pairs,
        [
            pl.BlockSpec(memory_space=pltpu.SMEM),
            columns(length, 0),
            columns(keys, 0),
            columns(keys, pairs),
            whole(lse.shape),
            whole(queries.shape),
            whole(queries.shape),
            whole(queries.shape),
            whole(queries.shape),
            whole(encoded.shape),
            whole(gain_rows.shape),
            weight(width, CROSS_OUT),
            weight(width, CROSS_QUERY),
            weight(width, CROSS_KEY),
            weight(width, CROSS_VALUE),
        ],
        [
            whole(queries.shape),
            whole((width, 4 * width)),
            whole(encoded.shape),
            whole((8, width)),
        ],
        like(
            (queries.shape, F32),
            ((width, 4 * width), BF16),
            (encoded.shape, F32),
            ((8, width), F32),
        ),
        [
            pltpu.VMEM((pairs, length, LANES), BF16),
            pltpu.VMEM((length, width), BF16),
            pltpu.VMEM((keys, 2 * width), BF16),
            pltpu.VMEM((keys, LANES), F32),
            pltpu.VMEM((keys, LANES), F32),
        ],
        2 * length * width * (5 * keys + 6 * width),
        (
            count,
            queries,
            ckv,
            ckv,
            lse,
            d_after_cross,
            after_self,
            normed_cross,
            attended,
            encoded,
            gain_rows,
            attention_set,
            attention_set,
            attention_set,
            attention_set,
        ),
    )


def self_backward(
    qkv,
    seg_row,
    seg_col,
    lse,
    d_after_self,
    hidden,
    normed_self,
    attended,
    gain_rows,
    attention_set,
):
    length, width = hidden.shape
    pairs = width // LANES
    return call(
        functools.partial(self_backward_kernel, self_blocks(length)),
        "self_backward",
        pairs,
        [
            whole(seg_row.shape),
            whole(seg_col.shape),
            columns(length, 0),
            columns(length, pairs),
            columns(length, 2 * pairs),
            whole(lse.shape),
            whole(hidden.shape),
            whole(hidden.shape),
            whole(hidden.shape),
            whole(hidden.shape),
            whole(gain_rows.shape),
            weight(width, OUT),
            weight(width, QUERY),
            weight(width, KEY),
            weight(width, VALUE),
        ],
        [whole(hidden.shape), whole((width, 4 * width)), whole((8, width))],
        like((hidden.shape, F32), ((width, 4 * width), BF16), ((8, width), F32)),
        [
            pltpu.VMEM((length, length), F32),
            pltpu.VMEM((pairs, length, LANES), BF16),
            pltpu.VMEM((length, 3 * width), BF16),
            pltpu.VMEM((length, LANES), F32),
            pltpu.VMEM((length, LANES), F32),
        ],
        2 * length * width * (4 * length + 8 * width),
        (
            seg_row,
            seg_col,
            qkv,
            qkv,
            qkv,
            lse,
            d_after_self,
            hidden,
            normed_self,
            attended,
            gain_rows,
            attention_set,
            attention_set,
            attention_set,
            attention_set,
        ),
    )


def on_device(
    hidden_in,
    encoder_out,
    segment_ids,
    passage_counts,
    cotangent,
    w_query,
    w_key,
    w_value,
    w_out,
    w_cross_query,
    w_cross_key,
    w_cross_value,
    w_cross_out,
    w_ffn_in,
    w_ffn_out,
    gain_self,
    gain_cross,
    gain_ffn,
):
    cores = lax.axis_size("seq")
    core = lax.axis_index("seq")
    chips = lax.axis_size("dp")
    width = hidden_in.shape[-1]
    ratio = w_ffn_in.shape[1] // width
    rows = w_query.shape[0]
    joint = ("dp", "seq")

    def own_rows(values):
        part = values.shape[0] // cores
        return lax.dynamic_slice_in_dim(values, core * part, part, 0)

    gains = jnp.stack([gain_self, gain_cross, gain_ffn], axis=1)
    gains = jnp.pad(gains, ((0, 0), (0, LANES - gains.shape[1])))
    attention_rows = own_rows(
        jnp.concatenate(
            [
                w_query,
                w_key,
                w_value,
                w_cross_key,
                w_cross_value,
                w_out,
                w_cross_query,
                w_cross_out,
                gains,
            ],
            axis=1,
        )
    )
    ffn_in_rows = jnp.concatenate(
        [w_ffn_in[:, i * width : (i + 1) * width] for i in range(ratio)], axis=0
    )
    ffn_rows = own_rows(jnp.concatenate([ffn_in_rows, w_ffn_out], axis=1))
    attention_set = lax.all_gather(attention_rows, joint, axis=0, tiled=True)
    ffn_rows, _ = lax.optimization_barrier((ffn_rows, attention_set))
    ffn_set = lax.all_gather(ffn_rows, joint, axis=0, tiled=True)
    w_in = ffn_set.reshape(chips, ratio, rows, 2 * width)
    if rows % 16:
        w_in = w_in[:, :, :, :width].transpose(1, 0, 2, 3).reshape(1, ratio, width, width)

    def dealt(values):
        return lax.all_to_all(values[:, 0], "seq", split_axis=0, concat_axis=1, tiled=True)

    def returned(values):
        values = lax.all_to_all(values, "seq", split_axis=1, concat_axis=0, tiled=True)
        return values[:, None]

    hidden_all = dealt(hidden_in)
    encoded_all = dealt(encoder_out)
    segments_all = dealt(segment_ids)
    cotangent_all = dealt(cotangent)
    turns = hidden_all.shape[0]
    outputs, input_grads, encoder_grads, running = [], [], [], None
    for turn in range(turns):
        count = lax.dynamic_slice_in_dim(passage_counts[:, 0], core * turns + turn, 1, 0)
        hidden = hidden_all[turn]
        encoded = encoded_all[turn]
        seg_row = segments_all[turn][None, :]
        seg_col = segments_all[turn][:, None]
        normed_self, qkv, ckv, gain_rows = project(hidden, encoded, attention_set)
        attended, self_lse, after_self, normed_cross, cross_queries = self_forward(
            qkv, seg_row, seg_col, hidden, gain_rows, attention_set
        )
        cross_attended, cross_lse, after_cross, normed_ffn = cross_forward(
            cross_queries, ckv, count, after_self, gain_rows, attention_set
        )
        out_hidden, d_after_cross, gain_grad_ffn, grad_in, grad_out = feed_forward(
            normed_ffn, cotangent_all[turn], after_cross, gain_rows, ffn_set, w_in
        )
        outputs.append(out_hidden)
        d_after_self, cross_grads, grad_encoded, gain_grad_cross = cross_backward(
            cross_queries,
            ckv,
            count,
            cross_lse,
            d_after_cross,
            after_self,
            normed_cross,
            cross_attended,
            encoded,
            gain_rows,
            attention_set,
        )
        encoder_grads.append(grad_encoded)
        grad_hidden, self_grads, gain_grad_self = self_backward(
            qkv,
            seg_row,
            seg_col,
            self_lse,
            d_after_self,
            hidden,
            normed_self,
            attended,
            gain_rows,
            attention_set,
        )
        input_grads.append(grad_hidden)
        gain_grads = jnp.stack(
            [gain_grad_self[0], gain_grad_cross[0], gain_grad_ffn[0]], axis=1
        ).astype(BF16)
        gain_grads = jnp.pad(gain_grads, ((0, 0), (0, LANES - gain_grads.shape[1])))
        if grad_in.shape[0] == 1:
            grad_in = grad_in.reshape(ratio, chips, rows, width).transpose(1, 0, 2, 3)
        grads = (
            jnp.concatenate([self_grads, cross_grads, gain_grads], axis=1),
            jnp.concatenate([grad_in.reshape(ratio * width, width), grad_out], axis=1),
        )
        running = grads if running is None else tuple(a + b for a, b in zip(running, grads))

    def reduced(values):
        own = lax.psum_scatter(values, joint, scatter_dimension=0, tiled=True)
        return lax.all_gather(own, "seq", axis=0, tiled=True).astype(F32)

    ffn_sum = reduced(running[1])
    attention_sum = reduced(running[0])
    grad_ffn_in = jnp.concatenate(
        [ffn_sum[i * rows : (i + 1) * rows, :width] for i in range(ratio)], axis=1
    )

    def block(i):
        return attention_sum[:, i * width : (i + 1) * width]

    return (
        returned(jnp.stack(outputs)),
        returned(jnp.stack(input_grads)),
        returned(jnp.stack(encoder_grads)),
        block(0),
        block(1),
        block(2),
        block(3),
        block(6),
        block(4),
        block(5),
        block(7),
        grad_ffn_in,
        ffn_sum[:, width:],
        attention_sum[:, 8 * width],
        attention_sum[:, 8 * width + 1],
        attention_sum[:, 8 * width + 2],
    )


def solution(mesh):
    tokens = P(None, "dp", "seq", None)
    rows = P("dp", None)
    gain = P("dp")
    return jax.shard_map(
        on_device,
        mesh=mesh,
        in_specs=(tokens, tokens, P(None, "dp", "seq"), P(None, "dp"), tokens)
        + (rows,) * 10
        + (gain,) * 3,
        out_specs=(tokens,) * 3 + (rows,) * 10 + (gain,) * 3,
        check_vma=False,
    )
```

```python
import functools

import jax
import jax.numpy as jnp
from jax import lax
from jax.experimental import pallas as pl
from jax.experimental.pallas import tpu as pltpu
from jax.sharding import PartitionSpec as P

HEAD_DIM = 64
LANES = 128
SEGMENT_LIMIT = 384
QUERY_BLOCK = 256
EPS = 1e-06
NEG = -1e30
GELU_RATE = 0.7978845608
GELU_CUBIC = 0.044715
BF16 = jnp.bfloat16
F32 = jnp.float32


def smooth_act(values):
    return (
        0.5
        * values
        * (1.0 + jnp.tanh(GELU_RATE * (values + GELU_CUBIC * values * values * values)))
    )


def smooth_slope(values):
    bent = jnp.tanh(GELU_RATE * (values + GELU_CUBIC * values * values * values))
    return 0.5 * (1.0 + bent) + 0.5 * values * (1.0 - bent * bent) * GELU_RATE * (
        1.0 + 3.0 * GELU_CUBIC * values * values
    )


def product(left, right):
    return jnp.dot(left, right, preferred_element_type=F32)


def row_outer(left, right):
    return lax.dot_general(left, right, (((0,), (0,)), ((), ())), preferred_element_type=F32)


def right_transposed(left, right):
    return lax.dot_general(left, right, (((1,), (1,)), ((), ())), preferred_element_type=F32)


def inverse_rms(values):
    return lax.rsqrt(jnp.mean(values * values, axis=-1, keepdims=True) + EPS)


def norm_backward(values, scale, gain, d_normed):
    scaled = gain * d_normed
    d_values = scale * scaled - values * (scale * scale * scale) * jnp.mean(
        values * scaled, axis=-1, keepdims=True
    )
    return (d_values, jnp.sum(values * scale * d_normed, axis=0, keepdims=True))


def self_blocks(length):
    blocks = []
    for start in range(0, length, QUERY_BLOCK):
        end = min(start + QUERY_BLOCK, length)
        first = max(0, start - SEGMENT_LIMIT + 1) // LANES * LANES
        blocks.append((start, end, first, end))
    return blocks


def cross_blocks(length, keys):
    return [
        (start, min(start + QUERY_BLOCK, length), 0, keys)
        for start in range(0, length, QUERY_BLOCK)
    ]


def of_head(values, head):
    lanes = lax.broadcasted_iota(jnp.int32, values.shape, 1)
    return jnp.where(lanes // HEAD_DIM == head, values, jnp.zeros_like(values))


def pair_forward(blocks, bias_of, q_ref, k_ref, v_ref, o_ref, lse_ref, lse_cols):
    pair = pl.program_id(0)
    lane = lax.broadcasted_iota(jnp.int32, (1, LANES), 1)
    for start, end, first, last in blocks:
        keys = k_ref[first:last, :]
        values = v_ref[first:last, :]
        query_pair = q_ref[start:end, :]
        bias = bias_of(start, end, first, last)
        mixed = []
        columns = lse_cols[start:end, :]
        for head in range(2):
            scores = right_transposed(of_head(query_pair, head), keys) + bias
            row_max = jnp.max(scores, axis=-1, keepdims=True)
            exponents = jnp.exp(scores - row_max)
            totals = jnp.sum(exponents, axis=-1, keepdims=True)
            mixed.append(product(exponents.astype(BF16), values) / totals)
            columns = jnp.where(lane == 2 * pair + head, row_max + jnp.log(totals), columns)
        o_ref[start:end, :] = jnp.where(lane < HEAD_DIM, mixed[0], mixed[1]).astype(BF16)
        lse_cols[start:end, :] = columns

    @pl.when(pair == pl.num_programs(0) - 1)
    def _():
        lse_ref[...] = jnp.transpose(lse_cols[...])[: lse_ref.shape[0], :]


def pair_backward(
    blocks, bias_of, q_ref, k_ref, v_ref, d_ref, lse_ref, dk_acc, dv_acc, first_pair=0
):
    pair = first_pair + pl.program_id(0)
    dk_acc[...] = jnp.zeros_like(dk_acc)
    dv_acc[...] = jnp.zeros_like(dv_acc)
    d_queries = []
    for start, end, first, last in blocks:
        keys = k_ref[first:last, :]
        values = v_ref[first:last, :]
        query_pair = q_ref[start:end, :]
        d_pair = d_ref[start:end, :]
        bias = bias_of(start, end, first, last)
        d_query = None
        for head in range(2):
            query_head = of_head(query_pair, head)
            d_head = of_head(d_pair, head)
            log_totals = lse_ref[pl.ds(2 * pair + head, 1), start:end]
            exact = jnp.exp(right_transposed(keys, query_head) + (bias - log_totals))
            d_probs = right_transposed(values, d_head)
            inner = jnp.sum(exact * d_probs, axis=0, keepdims=True)
            d_scores = (exact * (d_probs - inner)).astype(BF16)
            dv_acc[first:last, :] += product(exact.astype(BF16), d_head)
            dk_acc[first:last, :] += product(d_scores, query_head)
            part = row_outer(d_scores, of_head(keys, head))
            d_query = part if d_query is None else d_query + part
        d_queries.append((start, end, d_query))
    return d_queries


def store_halves(core, kept, sent, place, value):
    half = value.shape[-1] // 2
    there = slice(place, place + half)

    @pl.when(core == 0)
    def _():
        kept[..., there] = value[..., :half]
        sent[..., there] = value[..., half:]

    @pl.when(core != 0)
    def _():
        kept[..., there] = value[..., half:]
        sent[..., there] = value[..., :half]


def masked_bias(seg_col, seg_row, keys_first):
    shape = (seg_col.shape[0], seg_row.shape[1])
    rows = lax.broadcasted_iota(jnp.int32, shape, 0)
    lanes = lax.broadcasted_iota(jnp.int32, shape, 1)
    ordered = rows <= lanes if keys_first else lanes <= rows
    return jnp.where(ordered & (seg_col[...] == seg_row[...]), 0.0, NEG)


def project_kernel(hidden, encoded, gains, weight, normed, qkv, ckv, gain_rows):
    step = pl.program_id(0)

    @pl.when(step == 0)
    def _():
        rows = jnp.transpose(gains[...].astype(F32))[: gain_rows.shape[0], :]
        gain_rows[...] = rows
        values = hidden[...].astype(F32)
        normed[...] = (values * inverse_rms(values) * rows[0:1, :]).astype(BF16)

    @pl.when(step < 3)
    def _():
        qkv[...] = product(normed[...], weight[...]).astype(BF16)

    @pl.when(step >= 3)
    def _():
        ckv[...] = product(encoded[...], weight[...]).astype(BF16)


def self_forward_kernel(
    blocks,
    seg_row,
    seg_col,
    hidden,
    gain_rows,
    q_ref,
    k_ref,
    v_ref,
    w_o,
    w_cq,
    attended,
    lse_ref,
    after_self,
    normed_cross,
    cross_queries,
    bias,
    lse_cols,
    mixed,
):
    @pl.when(pl.program_id(0) == 0)
    def _():
        bias[...] = masked_bias(seg_col, seg_row, False)
        lse_cols[...] = jnp.zeros_like(lse_cols)

    pair_forward(
        blocks,
        lambda start, end, first, last: bias[start:end, first:last],
        q_ref,
        k_ref,
        v_ref,
        mixed,
        lse_ref,
        lse_cols,
    )
    place = pl.multiple_of(pl.program_id(0) * LANES, LANES)
    attended[:, pl.ds(place, LANES)] = mixed[...]

    @pl.when(pl.program_id(0) == pl.num_programs(0) - 1)
    def _():
        values = hidden[...].astype(F32) + product(attended[...], w_o[...])
        after_self[...] = values
        normed = (values * inverse_rms(values) * gain_rows[1:2, :]).astype(BF16)
        normed_cross[...] = normed
        cross_queries[...] = product(normed, w_cq[...]).astype(BF16)


def cross_forward_kernel(
    blocks,
    count,
    after_self,
    gain_rows,
    q_ref,
    k_ref,
    v_ref,
    w_co,
    attended,
    lse_ref,
    after_cross,
    normed_ffn,
    lse_cols,
    mixed,
):
    @pl.when(pl.program_id(0) == 0)
    def _():
        lse_cols[...] = jnp.zeros_like(lse_cols)

    places = lax.broadcasted_iota(jnp.int32, (1, k_ref.shape[0]), 1)
    bias = jnp.where(places < count[0], 0.0, NEG)
    pair_forward(
        blocks,
        lambda start, end, first, last: bias,
        q_ref,
        k_ref,
        v_ref,
        mixed,
        lse_ref,
        lse_cols,
    )
    place = pl.multiple_of(pl.program_id(0) * LANES, LANES)
    attended[:, pl.ds(place, LANES)] = mixed[...]

    @pl.when(pl.program_id(0) == pl.num_programs(0) - 1)
    def _():
        values = after_self[...] + product(attended[...], w_co[...])
        after_cross[...] = values
        normed_ffn[...] = (values * inverse_rms(values) * gain_rows[2:3, :]).astype(BF16)


def ffn_kernel(
    scalars,
    normed,
    branch,
    after_cross,
    gain_rows,
    w_in,
    w_out,
    out_hidden,
    d_after_cross,
    gain_grad,
    kept_in,
    sent_in,
    kept_out,
    sent_out,
    out_acc,
    dn_acc,
    normed_t,
):
    step = pl.program_id(0)

    @pl.when(step == 0)
    def _():
        normed_t[...] = jnp.transpose(normed[...])
        out_acc[...] = after_cross[...]
        dn_acc[...] = jnp.zeros_like(dn_acc)

    width = normed.shape[1]
    up = w_in[...].reshape(width, -1)
    down = w_out[...]
    pre = product(normed[...], up)
    bent = jnp.tanh(GELU_RATE * (pre + GELU_CUBIC * pre * pre * pre))
    half = 0.5 * (1.0 + bent)
    hidden_act = (pre * half).astype(BF16)
    slope = half + 0.5 * pre * (1.0 - bent * bent) * GELU_RATE * (
        1.0 + 3.0 * GELU_CUBIC * pre * pre
    )
    out_acc[...] += product(hidden_act, down)
    d_pre = (right_transposed(branch[...], down) * slope).astype(BF16)
    grad_out = row_outer(hidden_act, branch[...]).astype(BF16)
    store_halves(scalars[1], kept_out, sent_out, 0, grad_out)
    grad_in = product(normed_t[...], d_pre).astype(BF16)
    grad_in = grad_in.reshape(kept_in.shape[:-1] + (width,))
    store_halves(scalars[1], kept_in, sent_in, 0, grad_in)
    dn_acc[...] += right_transposed(d_pre, up)

    @pl.when(step == pl.num_programs(0) - 1)
    def _():
        out_hidden[...] = out_acc[...].astype(BF16)
        values = after_cross[...]
        d_values, d_gain = norm_backward(
            values, inverse_rms(values), gain_rows[2:3, :], dn_acc[...]
        )
        d_after_cross[...] = branch[...].astype(F32) + d_values
        gain_grad[...] = jnp.broadcast_to(d_gain, gain_grad.shape)


def branch_kernel(scalars, d_after, attended, w_out, d_att, kept, sent):
    branch = d_after[...].astype(BF16)
    d_mixed = right_transposed(branch, w_out[...]).astype(BF16)
    for pair in range(d_att.shape[0]):
        d_att[pair] = d_mixed[:, pair * LANES : (pair + 1) * LANES]
    grad_out = row_outer(attended[...], branch).astype(BF16)
    store_halves(scalars[1], kept, sent, 0, grad_out)


def cross_backward_kernel(
    blocks,
    scalars,
    q_ref,
    k_ref,
    v_ref,
    d_att,
    lse_ref,
    d_after_cross,
    after_self,
    normed_cross,
    encoded,
    gain_rows,
    w_cq,
    w_ck,
    w_cv,
    d_after_self,
    kept,
    sent,
    grad_encoded,
    gain_grad,
    dq_all,
    dkv_all,
    dk_acc,
    dv_acc,
):
    step = pl.program_id(0)
    width = d_after_cross.shape[1]
    half = width // 2
    places = lax.broadcasted_iota(jnp.int32, (k_ref.shape[0], 1), 0)
    bias = jnp.where(places < scalars[0], 0.0, NEG)
    d_queries = pair_backward(
        blocks,
        lambda start, end, first, last: bias,
        q_ref,
        k_ref,
        v_ref,
        d_att.at[0],
        lse_ref,
        dk_acc,
        dv_acc,
    )
    place = pl.multiple_of(step * LANES, LANES)
    for start, end, d_query in d_queries:
        dq_all[start:end, pl.ds(place, LANES)] = d_query.astype(BF16)
    dkv_all[:, pl.ds(place, LANES)] = dk_acc[...].astype(BF16)
    dkv_all[:, pl.ds(width + place, LANES)] = dv_acc[...].astype(BF16)

    @pl.when(step == pl.num_programs(0) - 1)
    def _():
        dq = dq_all[...]
        grad_query = row_outer(normed_cross[...], dq).astype(BF16)
        grad_kv = row_outer(encoded[...], dkv_all[...]).astype(BF16)
        store_halves(scalars[1], kept, sent, 0, grad_query)
        store_halves(scalars[1], kept, sent, half, grad_kv[:, :width])
        store_halves(scalars[1], kept, sent, 2 * half, grad_kv[:, width:])
        grad_encoded[...] = right_transposed(dkv_all[:, :width], w_ck[...]) + right_transposed(
            dkv_all[:, width:], w_cv[...]
        )
        values = after_self[...]
        d_values, d_gain = norm_backward(
            values,
            inverse_rms(values),
            gain_rows[1:2, :],
            right_transposed(dq, w_cq[...]),
        )
        d_after_self[...] = d_after_cross[...] + d_values
        gain_grad[...] = jnp.broadcast_to(d_gain, gain_grad.shape)


def self_backward_pairs(
    blocks, seg_row, seg_col, q_ref, k_ref, v_ref, d_att, lse_ref, d_all, bias, dk_acc, dv_acc, first
):
    @pl.when(pl.program_id(0) == 0)
    def _():
        bias[...] = masked_bias(seg_col, seg_row, True)

    d_queries = pair_backward(
        blocks,
        lambda start, end, first_key, last_key: bias[first_key:last_key, start:end],
        q_ref,
        k_ref,
        v_ref,
        d_att.at[0],
        lse_ref,
        dk_acc,
        dv_acc,
        first,
    )
    place = pl.multiple_of(pl.program_id(0) * LANES, LANES)
    for start, end, d_query in d_queries:
        d_all[0, start:end, pl.ds(place, LANES)] = d_query.astype(BF16)
    d_all[1, :, pl.ds(place, LANES)] = dk_acc[...].astype(BF16)
    d_all[2, :, pl.ds(place, LANES)] = dv_acc[...].astype(BF16)


def self_backward_first_kernel(
    blocks, seg_row, seg_col, q_ref, k_ref, v_ref, d_att, lse_ref, d_all, bias, dk_acc, dv_acc
):
    self_backward_pairs(
        blocks, seg_row, seg_col, q_ref, k_ref, v_ref, d_att, lse_ref, d_all, bias, dk_acc, dv_acc, 0
    )


def self_backward_last_kernel(
    blocks,
    first,
    scalars,
    seg_row,
    seg_col,
    q_ref,
    k_ref,
    v_ref,
    d_att,
    lse_ref,
    d_first,
    d_after_self,
    hidden,
    normed_self,
    gain_rows,
    gain_grad_cross,
    gain_grad_ffn,
    w_q,
    w_k,
    w_v,
    grad_hidden,
    kept,
    sent,
    bias,
    d_all,
    dk_acc,
    dv_acc,
):
    self_backward_pairs(
        blocks,
        seg_row,
        seg_col,
        q_ref,
        k_ref,
        v_ref,
        d_att,
        lse_ref,
        d_all,
        bias,
        dk_acc,
        dv_acc,
        first,
    )
    width = d_after_self.shape[1]

    @pl.when(pl.program_id(0) == pl.num_programs(0) - 1)
    def _():
        d_normed = None
        for i, weight_ref in enumerate((w_q, w_k, w_v)):
            d_out = jnp.concatenate([d_first[i], d_all[i]], axis=1)
            grad = row_outer(normed_self[...], d_out)
            store_halves(scalars[1], kept, sent, i * width // 2, grad.astype(BF16))
            part = right_transposed(d_out, weight_ref[...])
            d_normed = part if d_normed is None else d_normed + part
        values = hidden[...].astype(F32)
        d_values, d_gain = norm_backward(
            values, inverse_rms(values), gain_rows[0:1, :], d_normed
        )
        grad_hidden[...] = d_after_self[...] + d_values
        row = lax.broadcasted_iota(jnp.int32, (LANES, width), 0)
        gain_grads = jnp.where(row == 0, d_gain, 0.0)
        gain_grads = jnp.where(row == 1, gain_grad_cross[0:1, :], gain_grads)
        gain_grads = jnp.where(row == 2, gain_grad_ffn[0:1, :], gain_grads)
        gain_columns = jnp.transpose(gain_grads).astype(BF16)
        kept[:, 3 * width // 2 :] = gain_columns
        sent[:, 3 * width // 2 :] = gain_columns


def columns(rows, offset):
    return pl.BlockSpec((rows, LANES), lambda step: (0, offset + step))


def whole(shape, place=None):
    place = (0,) * len(shape) if place is None else place
    return pl.BlockSpec(shape, lambda step: place)


def like(*shapes):
    return [jax.ShapeDtypeStruct(shape, dtype) for shape, dtype in shapes]


def call(kernel, name, steps, in_specs, out_specs, out_shape, scratch, flops, args, grant=56):
    size = sum(int(a.size) * a.dtype.itemsize for a in args)
    return pl.pallas_call(
        kernel,
        grid=(steps,),
        in_specs=in_specs,
        out_specs=out_specs,
        out_shape=out_shape,
        scratch_shapes=scratch,
        compiler_params=pltpu.CompilerParams(
            dimension_semantics=("arbitrary",), vmem_limit_bytes=grant << 20
        ),
        cost_estimate=pl.CostEstimate(flops=flops, bytes_accessed=size, transcendentals=0),
        name=name,
    )(*args)


QUERY, KEY, VALUE, CROSS_KEY, CROSS_VALUE, OUT, CROSS_QUERY, CROSS_OUT = range(8)


def weight(width, place):
    return whole((width, width), (0, place))


def project(hidden, encoded, attention_set):
    length, width = hidden.shape
    keys = encoded.shape[0]
    return call(
        project_kernel,
        "project",
        5,
        [
            whole(hidden.shape),
            whole(encoded.shape),
            whole((width, LANES), (0, 8 * width // LANES)),
            pl.BlockSpec((width, width), lambda step: (0, step)),
        ],
        [
            whole(hidden.shape),
            pl.BlockSpec((length, width), lambda step: (0, jnp.minimum(step, 2))),
            pl.BlockSpec((keys, width), lambda step: (0, jnp.maximum(step - 3, 0))),
            whole((8, width)),
        ],
        like(
            (hidden.shape, BF16),
            ((length, 3 * width), BF16),
            ((keys, 2 * width), BF16),
            ((8, width), F32),
        ),
        [],
        2 * width * width * (3 * length + 2 * keys),
        (hidden, encoded, attention_set, attention_set),
    )


def self_forward(qkv, seg_row, seg_col, hidden, gain_rows, attention_set):
    length, width = hidden.shape
    pairs = width // LANES
    return call(
        functools.partial(self_forward_kernel, self_blocks(length)),
        "self_forward",
        pairs,
        [
            whole(seg_row.shape),
            whole(seg_col.shape),
            whole(hidden.shape),
            whole(gain_rows.shape),
            columns(length, 0),
            columns(length, pairs),
            columns(length, 2 * pairs),
            weight(width, OUT),
            weight(width, CROSS_QUERY),
        ],
        [
            whole(hidden.shape),
            whole((16, length)),
            whole(hidden.shape),
            whole(hidden.shape),
            whole(hidden.shape),
        ],
        like(
            (hidden.shape, BF16),
            ((16, length), F32),
            (hidden.shape, F32),
            (hidden.shape, BF16),
            (hidden.shape, BF16),
        ),
        [
            pltpu.VMEM((length, length), F32),
            pltpu.VMEM((length, LANES), F32),
            pltpu.VMEM((length, LANES), BF16),
        ],
        4 * length * width * (length + width),
        (
            seg_row,
            seg_col,
            hidden,
            gain_rows,
            qkv,
            qkv,
            qkv,
            attention_set,
            attention_set,
        ),
    )


def cross_forward(queries, ckv, count, after_self, gain_rows, attention_set):
    length, width = queries.shape
    keys = ckv.shape[0]
    pairs = width // LANES
    return call(
        functools.partial(cross_forward_kernel, cross_blocks(length, keys)),
        "cross_forward",
        pairs,
        [
            pl.BlockSpec(memory_space=pltpu.SMEM),
            whole(queries.shape),
            whole(gain_rows.shape),
            columns(length, 0),
            columns(keys, 0),
            columns(keys, pairs),
            weight(width, CROSS_OUT),
        ],
        [
            whole(queries.shape),
            whole((16, length)),
            whole(queries.shape),
            whole(queries.shape),
        ],
        like(
            (queries.shape, BF16),
            ((16, length), F32),
            (queries.shape, F32),
            (queries.shape, BF16),
        ),
        [pltpu.VMEM((length, LANES), F32), pltpu.VMEM((length, LANES), BF16)],
        2 * length * width * (2 * keys + width),
        (count, after_self, gain_rows, queries, ckv, ckv, attention_set),
    )


def feed_forward(scalars, normed, branch, after_cross, gain_rows, ffn_set, w_in):
    length, width = normed.shape
    groups, steps, rows, _ = w_in.shape
    block = pl.BlockSpec((groups, 1, rows, width), lambda step: (0, step, 0, 0))
    half_block = pl.BlockSpec((groups, 1, rows, width // 2), lambda step: (0, step, 0, 0))
    half_rows = pl.BlockSpec((width, width // 2), lambda step: (step, 0))
    half_in = ((groups, steps, rows, width // 2), BF16)
    half_out = ((steps * width, width // 2), BF16)
    return call(
        ffn_kernel,
        "feed_forward",
        steps,
        [
            pl.BlockSpec(memory_space=pltpu.SMEM),
            whole(normed.shape),
            whole(normed.shape),
            whole(normed.shape),
            whole(gain_rows.shape),
            block,
            pl.BlockSpec((width, width), lambda step: (step, 1)),
        ],
        [
            whole(normed.shape),
            whole(normed.shape),
            whole((8, width)),
            half_block,
            half_block,
            half_rows,
            half_rows,
        ],
        like(
            (normed.shape, BF16),
            (normed.shape, F32),
            ((8, width), F32),
            half_in,
            half_in,
            half_out,
            half_out,
        ),
        [
            pltpu.VMEM(normed.shape, F32),
            pltpu.VMEM(normed.shape, F32),
            pltpu.VMEM((width, length), BF16),
        ],
        12 * length * width * width * steps,
        (scalars, normed, branch, after_cross, gain_rows, w_in, ffn_set),
        grant=56,
    )


def branch_backward(scalars, d_after, attended, attention_set, place):
    length, width = d_after.shape
    pairs = width // LANES
    halves = (width, width // 2)
    return call(
        branch_kernel,
        "branch_backward",
        1,
        [
            pl.BlockSpec(memory_space=pltpu.SMEM),
            whole(d_after.shape),
            whole(attended.shape),
            weight(width, place),
        ],
        [whole((pairs, length, LANES)), whole(halves), whole(halves)],
        like(((pairs, length, LANES), BF16), (halves, BF16), (halves, BF16)),
        [],
        4 * length * width * width,
        (scalars, d_after, attended, attention_set),
    )


def pair_block(length, first):
    return pl.BlockSpec((1, length, LANES), lambda step: (first + step, 0, 0))


def cross_backward(
    scalars,
    queries,
    ckv,
    d_att,
    lse,
    d_after_cross,
    after_self,
    normed_cross,
    encoded,
    gain_rows,
    attention_set,
):
    length, width = queries.shape
    keys = ckv.shape[0]
    pairs = width // LANES
    halves = (width, 3 * width // 2)
    return call(
        functools.partial(cross_backward_kernel, cross_blocks(length, keys)),
        "cross_backward",
        pairs,
        [
            pl.BlockSpec(memory_space=pltpu.SMEM),
            columns(length, 0),
            columns(keys, 0),
            columns(keys, pairs),
            pair_block(length, 0),
            whole(lse.shape),
            whole(queries.shape),
            whole(queries.shape),
            whole(queries.shape),
            whole(encoded.shape),
            whole(gain_rows.shape),
            weight(width, CROSS_QUERY),
            weight(width, CROSS_KEY),
            weight(width, CROSS_VALUE),
        ],
        [
            whole(queries.shape),
            whole(halves),
            whole(halves),
            whole(encoded.shape),
            whole((8, width)),
        ],
        like(
            (queries.shape, F32),
            (halves, BF16),
            (halves, BF16),
            (encoded.shape, F32),
            ((8, width), F32),
        ),
        [
            pltpu.VMEM((length, width), BF16),
            pltpu.VMEM((keys, 2 * width), BF16),
            pltpu.VMEM((keys, LANES), F32),
            pltpu.VMEM((keys, LANES), F32),
        ],
        2 * length * width * (5 * keys + 4 * width),
        (
            scalars,
            queries,
            ckv,
            ckv,
            d_att,
            lse,
            d_after_cross,
            after_self,
            normed_cross,
            encoded,
            gain_rows,
            attention_set,
            attention_set,
            attention_set,
        ),
    )


def self_backward_first(seg_row, seg_col, qkv, d_att, lse):
    length, width = qkv.shape[0], qkv.shape[1] // 3
    pairs = width // LANES
    done = 2 * pairs // 3
    return call(
        functools.partial(self_backward_first_kernel, self_blocks(length)),
        "self_backward_first",
        done,
        [
            whole(seg_row.shape),
            whole(seg_col.shape),
            columns(length, 0),
            columns(length, pairs),
            columns(length, 2 * pairs),
            pair_block(length, 0),
            whole(lse.shape),
        ],
        whole((3, length, done * LANES)),
        jax.ShapeDtypeStruct((3, length, done * LANES), BF16),
        [
            pltpu.VMEM((length, length), F32),
            pltpu.VMEM((length, LANES), F32),
            pltpu.VMEM((length, LANES), F32),
        ],
        4 * length * width * length,
        (seg_row, seg_col, qkv, qkv, qkv, d_att, lse),
    )


def self_backward_last(
    scalars,
    seg_row,
    seg_col,
    qkv,
    d_att,
    lse,
    d_first,
    d_after_self,
    hidden,
    normed_self,
    gain_rows,
    gain_grad_cross,
    gain_grad_ffn,
    attention_set,
):
    length, width = hidden.shape
    pairs = width // LANES
    done = 2 * pairs // 3
    halves = (width, 3 * width // 2 + LANES)
    return call(
        functools.partial(self_backward_last_kernel, self_blocks(length), done),
        "self_backward_last",
        pairs - done,
        [
            pl.BlockSpec(memory_space=pltpu.SMEM),
            whole(seg_row.shape),
            whole(seg_col.shape),
            columns(length, done),
            columns(length, pairs + done),
            columns(length, 2 * pairs + done),
            pair_block(length, done),
            whole(lse.shape),
            whole(d_first.shape),
            whole(hidden.shape),
            whole(hidden.shape),
            whole(hidden.shape),
            whole(gain_rows.shape),
            whole(gain_rows.shape),
            whole(gain_rows.shape),
            weight(width, QUERY),
            weight(width, KEY),
            weight(width, VALUE),
        ],
        [whole(hidden.shape), whole(halves), whole(halves)],
        like((hidden.shape, F32), (halves, BF16), (halves, BF16)),
        [
            pltpu.VMEM((length, length), F32),
            pltpu.VMEM((3, length, (pairs - done) * LANES), BF16),
            pltpu.VMEM((length, LANES), F32),
            pltpu.VMEM((length, LANES), F32),
        ],
        2 * length * width * (2 * length + 6 * width),
        (
            scalars,
            seg_row,
            seg_col,
            qkv,
            qkv,
            qkv,
            d_att,
            lse,
            d_first,
            d_after_self,
            hidden,
            normed_self,
            gain_rows,
            gain_grad_cross,
            gain_grad_ffn,
            attention_set,
            attention_set,
            attention_set,
        ),
    )


def grid_of(chips):
    side = 1
    while 2 * side**3 < chips:
        side += 1
    return (2 * side, side, side) if 2 * side**3 == chips else (1, 1, chips)


def axis_stride(grid, axis):
    stride = 1
    for extent in grid[axis + 1 :]:
        stride *= extent
    return stride


def coordinate(grid, axis):
    return lax.axis_index("dp") // axis_stride(grid, axis) % grid[axis]


def shifted(values, grid, axis, shift):
    stride, extent = axis_stride(grid, axis), grid[axis]
    chips = grid[0] * grid[1] * grid[2]
    pairs = []
    for chip in range(chips):
        at = chip // stride % extent
        pairs.append((chip, chip + ((at + shift) % extent - at) * stride))
    return lax.ppermute(values, "dp", pairs)


def swapped(values):
    cores = lax.axis_size("seq")
    return lax.ppermute(values, "seq", [(i, (i + 1) % cores) for i in range(cores)])


def total(parts):
    result = parts[0].astype(F32)
    for part in parts[1:]:
        result = result + part.astype(F32)
    return result


def pieces_kernel(plan, *refs):
    outputs = refs[len(refs) - len(plan) :]
    at = 1
    for output, sources in zip(outputs, plan):
        for start, end, count in sources:
            value = total([refs[at + i][:, 0] for i in range(count)])
            output[:, :, :, start:end] = value.astype(BF16)
            at += count


def pieces(groups):
    outers = []
    for sources, dim, _ in groups:
        outer = 1
        for n in sources[0][0][0].shape[:dim]:
            outer *= n
        outers.append(outer)
    steps = 1 if any(outer % 2 for outer in outers) else 2
    plan, args, in_specs, out_specs, out_shape, finals, all_places = [], [], [], [], [], [], []
    size = 0
    for (sources, dim, places), outer in zip(groups, outers):
        shape = sources[0][0][0].shape
        before, extent, after, rows = shape[:dim], shape[dim], shape[dim + 1 : -2], shape[-2]
        inner = 1
        for n in after:
            inner *= n
        lead = outer // steps
        for place in places:
            width, spans = 0, []
            for parts, columns_, block in sources:
                spans.append((width, width + columns_, len(parts)))
                width += columns_
                for part in parts:
                    args.append(part.reshape(outer, extent, inner, rows, part.shape[-1]))
                    in_specs.append(
                        pl.BlockSpec(
                            (lead, 1, inner, rows, columns_),
                            lambda g, at, o=len(all_places), block=block: (g, at[o], 0, 0, block),
                        )
                    )
                    size += outer * inner * rows * columns_
            plan.append(spans)
            all_places.append(place)
            out_specs.append(
                pl.BlockSpec((lead, inner, rows, width), lambda g, at: (g, 0, 0, 0))
            )
            out_shape.append(jax.ShapeDtypeStruct((outer, inner, rows, width), BF16))
            finals.append(before + after + (rows, width))
            size += outer * inner * rows * width
    result = pl.pallas_call(
        functools.partial(pieces_kernel, plan),
        grid_spec=pltpu.PrefetchScalarGridSpec(
            num_scalar_prefetch=1, grid=(steps,), in_specs=in_specs, out_specs=out_specs
        ),
        out_shape=out_shape,
        compiler_params=pltpu.CompilerParams(
            dimension_semantics=("arbitrary",), vmem_limit_bytes=max(16 << 20, 6 * size)
        ),
        cost_estimate=pl.CostEstimate(flops=0, bytes_accessed=2 * size, transcendentals=0),
        name="pieces",
    )(jnp.stack(all_places).astype(jnp.int32), *args)
    return [r.reshape(final) for r, final in zip(result, finals)]


def scattered(grid, *groups):
    wanted = []
    for sources, axis, dim in groups:
        here, extent = coordinate(grid, axis), grid[axis]
        wanted.append((sources, dim, [(here + shift) % extent for shift in range(extent)]))
    taken = pieces(wanted)
    results = []
    for _, axis, _ in groups:
        own, *others = taken[: grid[axis]]
        taken = taken[grid[axis] :]
        results.append(
            [own]
            + [shifted(other, grid, axis, shift) for shift, other in enumerate(others, start=1)]
        )
    return results


def on_device(
    hidden_in,
    encoder_out,
    segment_ids,
    passage_counts,
    cotangent,
    w_query,
    w_key,
    w_value,
    w_out,
    w_cross_query,
    w_cross_key,
    w_cross_value,
    w_cross_out,
    w_ffn_in,
    w_ffn_out,
    gain_self,
    gain_cross,
    gain_ffn,
):
    cores = lax.axis_size("seq")
    core = lax.axis_index("seq")
    chips = lax.axis_size("dp")
    grid = grid_of(chips)
    width = hidden_in.shape[-1]
    half = width // 2
    ratio = w_ffn_in.shape[1] // width
    rows = w_query.shape[0]
    joint = ("dp", "seq")

    def own_rows(values):
        part = values.shape[0] // cores
        return lax.dynamic_slice_in_dim(values, core * part, part, 0)

    def in_order(mine, other, axis):
        first = jnp.where(core == 0, mine, other)
        second = jnp.where(core == 0, other, mine)
        return jnp.concatenate([first, second], axis=axis)

    gains = jnp.stack([gain_self, gain_cross, gain_ffn], axis=1)
    gains = jnp.pad(gains, ((0, 0), (0, LANES - gains.shape[1])))
    attention_rows = own_rows(
        jnp.concatenate(
            [
                w_query,
                w_key,
                w_value,
                w_cross_key,
                w_cross_value,
                w_out,
                w_cross_query,
                w_cross_out,
                gains,
            ],
            axis=1,
        )
    )
    ffn_in_rows = jnp.concatenate(
        [w_ffn_in[:, i * width : (i + 1) * width] for i in range(ratio)], axis=0
    )
    ffn_rows = own_rows(jnp.concatenate([ffn_in_rows, w_ffn_out], axis=1))
    attention_set = lax.all_gather(attention_rows, joint, axis=0, tiled=True)

    def dealt(values):
        mine = lax.dynamic_index_in_dim(values[:, 0], core, 0, keepdims=False)
        theirs = lax.dynamic_index_in_dim(values[:, 0], 1 - core, 0, keepdims=False)
        return in_order(mine, swapped(theirs), 0)

    def returned(values):
        length = values.shape[0] // cores
        mine = lax.dynamic_slice_in_dim(values, core * length, length, 0)
        theirs = lax.dynamic_slice_in_dim(values, (1 - core) * length, length, 0)
        return in_order(mine[None, None], swapped(theirs)[None, None], 0)

    hidden = dealt(hidden_in)
    encoded = dealt(encoder_out)
    segments = dealt(segment_ids)
    branch_ffn = dealt(cotangent)
    hidden, encoded, segments, branch_ffn, ffn_rows = lax.optimization_barrier(
        (hidden, encoded, segments, branch_ffn, ffn_rows)
    )
    ffn_set = lax.all_gather(ffn_rows, joint, axis=0, tiled=True)
    w_in = ffn_set.reshape(chips, ratio, rows, 2 * width)
    if rows % 16:
        w_in = w_in[:, :, :, :width].transpose(1, 0, 2, 3).reshape(1, ratio, width, width)

    count = lax.dynamic_index_in_dim(passage_counts[:, 0], core, 0, keepdims=False)
    scalars = jnp.stack([count, core.astype(jnp.int32)])
    seg_row = segments[None, :]
    seg_col = segments[:, None]
    normed_self, qkv, ckv, gain_rows = project(hidden, encoded, attention_set)
    attended, self_lse, after_self, normed_cross, cross_queries = self_forward(
        qkv, seg_row, seg_col, hidden, gain_rows, attention_set
    )
    cross_attended, cross_lse, after_cross, normed_ffn = cross_forward(
        cross_queries, ckv, scalars, after_self, gain_rows, attention_set
    )
    out_hidden, d_after_cross, gain_grad_ffn, kept_in, sent_in, kept_out, sent_out = feed_forward(
        scalars, normed_ffn, branch_ffn, after_cross, gain_rows, ffn_set, w_in
    )

    def by_chip(values):
        if values.shape[0] == 1:
            values = values[0].reshape(ratio, chips, rows, -1).transpose(1, 0, 2, 3)
        return values.reshape(grid + (-1, values.shape[-1]))

    def whole_source(parts):
        return (parts, parts[0].shape[-1], 0)

    def along_first(first, second):
        return scattered(grid, (first, 2, 2), (second, 1, 1))

    def along_second(first, second):
        return scattered(grid, ([whole_source(first)], 1, 1), ([whole_source(second)], 2, 1))

    def along_z(first, second):
        return scattered(grid, ([whole_source(first), whole_source(second)], 0, 0))[0]

    def tied(value, others):
        return lax.optimization_barrier((value, others))

    ffn_in = [by_chip(kept_in), by_chip(swapped(sent_in))]
    ffn_out = [by_chip(kept_out), by_chip(swapped(sent_out))]
    d_att, kept_co, sent_co = branch_backward(
        scalars, d_after_cross, cross_attended, attention_set, CROSS_OUT
    )
    d_att, (ffn_in, ffn_out) = tied(d_att, (ffn_in, ffn_out))
    ffn_first, ffn_second = along_first([(ffn_in, half, 0)], [(ffn_out, half, 0)])
    cross_o = [by_chip(kept_co), by_chip(swapped(sent_co))]
    d_after_self, kept_c, sent_c, grad_encoded, gain_grad_cross = cross_backward(
        scalars,
        cross_queries,
        ckv,
        d_att,
        cross_lse,
        d_after_cross,
        after_self,
        normed_cross,
        encoded,
        gain_rows,
        attention_set,
    )
    d_after_self, (ffn_first, ffn_second) = tied(d_after_self, (ffn_first, ffn_second))
    ffn_first, ffn_second = along_second(ffn_first, ffn_second)
    d_after_self, _ = tied(d_after_self, (ffn_first[0], ffn_second[0]))
    cross_qkv = [by_chip(kept_c), by_chip(swapped(sent_c))]
    d_att, kept_o, sent_o = branch_backward(
        scalars, d_after_self, attended, attention_set, OUT
    )
    self_o = [by_chip(kept_o), by_chip(swapped(sent_o))]
    cross_first, cross_second = along_first(
        [(cross_o, half, 0), (cross_qkv, half, 0), (self_o, half, 0)],
        [(cross_qkv, half, 1), (cross_qkv, half, 2)],
    )
    (ffn_first, ffn_second), _ = tied((ffn_first, ffn_second), (cross_first[0], cross_second[0]))
    ffn_parts = along_z(ffn_first, ffn_second)
    d_att, _ = tied(d_att, (cross_first[0], cross_second[0], ffn_parts[0]))
    d_first = self_backward_first(seg_row, seg_col, qkv, d_att, self_lse)
    d_first, (cross_first, cross_second) = tied(d_first, (cross_first, cross_second))
    cross_first, cross_second = along_second(cross_first, cross_second)
    d_first, _ = tied(d_first, (cross_first[0], cross_second[0]))
    grad_hidden, kept_s, sent_s = self_backward_last(
        scalars,
        seg_row,
        seg_col,
        qkv,
        d_att,
        self_lse,
        d_first,
        d_after_self,
        hidden,
        normed_self,
        gain_rows,
        gain_grad_cross,
        gain_grad_ffn,
        attention_set,
    )
    sent_s, (ffn_parts, cross_first, cross_second) = tied(
        sent_s, (ffn_parts, cross_first, cross_second)
    )
    self_qkv = [by_chip(kept_s), by_chip(swapped(sent_s))]
    self_first, self_second = along_first(
        [(self_qkv, half, 0), (self_qkv, 2 * LANES, half // LANES)],
        [
            (self_qkv, half, 1),
            (self_qkv, LANES, 3 * half // LANES - 1),
            (self_qkv, LANES, 3 * half // LANES),
        ],
    )
    ffn_sum = total(ffn_parts)
    (cross_first, cross_second), (self_first, self_second) = tied(
        (cross_first, cross_second), (self_first, self_second)
    )
    self_first, self_second = along_second(self_first, self_second)
    (cross_first, cross_second), _ = tied(
        (cross_first, cross_second), (self_first[0], self_second[0])
    )
    cross_parts = along_z(cross_first, cross_second)
    (self_first, self_second), _ = tied((self_first, self_second), cross_parts[0])
    self_parts = along_z(self_first, self_second)
    cross_parts, _ = tied(cross_parts, self_parts[0])
    cross_sum = total(cross_parts)
    self_sum = total(self_parts)

    ffn_other, cross_other, self_other = swapped(ffn_sum), swapped(cross_sum), swapped(self_sum)

    def matrix(mine, other, i):
        there = slice(i * half, (i + 1) * half)
        return in_order(mine[:, there], other[:, there], 1)

    ffn_sum = ffn_sum.reshape(ratio, rows, 2 * half)
    ffn_other = ffn_other.reshape(ratio, rows, 2 * half)
    grad_ffn_in = jnp.concatenate(
        [matrix(ffn_sum[i], ffn_other[i], 0) for i in range(ratio)], axis=1
    )
    grad_ffn_out = jnp.concatenate(
        [matrix(ffn_sum[i], ffn_other[i], 1) for i in range(ratio)], axis=0
    )
    def value_columns(values):
        split = half + 2 * LANES
        return jnp.concatenate(
            [values[:, half:split], values[:, split + half : 3 * half]], axis=1
        )

    split = half + 2 * LANES
    gain_grads = self_sum[:, 3 * half :]
    return (
        returned(out_hidden),
        returned(grad_hidden),
        returned(grad_encoded),
        matrix(self_sum, self_other, 0),
        in_order(self_sum[:, split : split + half], self_other[:, split : split + half], 1),
        in_order(value_columns(self_sum), value_columns(self_other), 1),
        matrix(cross_sum, cross_other, 2),
        matrix(cross_sum, cross_other, 1),
        matrix(cross_sum, cross_other, 3),
        matrix(cross_sum, cross_other, 4),
        matrix(cross_sum, cross_other, 0),
        grad_ffn_in,
        grad_ffn_out,
        gain_grads[:, 0],
        gain_grads[:, 1],
        gain_grads[:, 2],
    )


def solution(mesh):
    tokens = P(None, "dp", "seq", None)
    rows = P("dp", None)
    gain = P("dp")
    return jax.shard_map(
        on_device,
        mesh=mesh,
        in_specs=(tokens, tokens, P(None, "dp", "seq"), P(None, "dp"), tokens)
        + (rows,) * 10
        + (gain,) * 3,
        out_specs=(tokens,) * 3 + (rows,) * 10 + (gain,) * 3,
        check_vma=False,
    )
```

```python
import functools

import jax
import jax.numpy as jnp
from jax import lax
from jax.experimental import pallas as pl
from jax.experimental.pallas import tpu as pltpu
from jax.sharding import PartitionSpec as P

HEAD_DIM = 64
LANES = 128
SEGMENT_LIMIT = 384
QUERY_BLOCK = 256
EPS = 1e-06
NEG = -1e30
GELU_RATE = 0.7978845608
GELU_CUBIC = 0.044715
BF16 = jnp.bfloat16
F32 = jnp.float32


def smooth_act(values):
    return (
        0.5
        * values
        * (1.0 + jnp.tanh(GELU_RATE * (values + GELU_CUBIC * values * values * values)))
    )


def smooth_slope(values):
    bent = jnp.tanh(GELU_RATE * (values + GELU_CUBIC * values * values * values))
    return 0.5 * (1.0 + bent) + 0.5 * values * (1.0 - bent * bent) * GELU_RATE * (
        1.0 + 3.0 * GELU_CUBIC * values * values
    )


def product(left, right):
    return jnp.dot(left, right, preferred_element_type=F32)


def row_outer(left, right):
    return lax.dot_general(left, right, (((0,), (0,)), ((), ())), preferred_element_type=F32)


def right_transposed(left, right):
    return lax.dot_general(left, right, (((1,), (1,)), ((), ())), preferred_element_type=F32)


def inverse_rms(values):
    return lax.rsqrt(jnp.mean(values * values, axis=-1, keepdims=True) + EPS)


def norm_backward(values, scale, gain, d_normed):
    scaled = gain * d_normed
    d_values = scale * scaled - values * (scale * scale * scale) * jnp.mean(
        values * scaled, axis=-1, keepdims=True
    )
    return (d_values, jnp.sum(values * scale * d_normed, axis=0, keepdims=True))


def self_blocks(length):
    blocks = []
    for start in range(0, length, QUERY_BLOCK):
        end = min(start + QUERY_BLOCK, length)
        first = max(0, start - SEGMENT_LIMIT + 1) // LANES * LANES
        blocks.append((start, end, first, end))
    return blocks


def cross_blocks(length, keys):
    return [
        (start, min(start + QUERY_BLOCK, length), 0, keys)
        for start in range(0, length, QUERY_BLOCK)
    ]


def of_head(values, head):
    lanes = lax.broadcasted_iota(jnp.int32, values.shape, 1)
    return jnp.where(lanes // HEAD_DIM == head, values, jnp.zeros_like(values))


def pair_forward(blocks, bias_of, q_ref, k_ref, v_ref, o_ref, lse_ref, lse_cols):
    pair = pl.program_id(0)
    lane = lax.broadcasted_iota(jnp.int32, (1, LANES), 1)
    for start, end, first, last in blocks:
        keys = k_ref[first:last, :]
        values = v_ref[first:last, :]
        query_pair = q_ref[start:end, :]
        bias = bias_of(start, end, first, last)
        mixed = []
        columns = lse_cols[start:end, :]
        for head in range(2):
            scores = right_transposed(of_head(query_pair, head), keys) + bias
            row_max = jnp.max(scores, axis=-1, keepdims=True)
            exponents = jnp.exp(scores - row_max)
            totals = jnp.sum(exponents, axis=-1, keepdims=True)
            mixed.append(product(exponents.astype(BF16), values) / totals)
            columns = jnp.where(lane == 2 * pair + head, row_max + jnp.log(totals), columns)
        o_ref[start:end, :] = jnp.where(lane < HEAD_DIM, mixed[0], mixed[1]).astype(BF16)
        lse_cols[start:end, :] = columns

    @pl.when(pair == pl.num_programs(0) - 1)
    def _():
        lse_ref[...] = jnp.transpose(lse_cols[...])[: lse_ref.shape[0], :]


def pair_backward(
    blocks, bias_of, q_ref, k_ref, v_ref, d_ref, lse_ref, dk_acc, dv_acc, first_pair=0
):
    pair = first_pair + pl.program_id(0)
    dk_acc[...] = jnp.zeros_like(dk_acc)
    dv_acc[...] = jnp.zeros_like(dv_acc)
    d_queries = []
    for start, end, first, last in blocks:
        keys = k_ref[first:last, :]
        values = v_ref[first:last, :]
        query_pair = q_ref[start:end, :]
        d_pair = d_ref[start:end, :]
        bias = bias_of(start, end, first, last)
        d_query = None
        for head in range(2):
            query_head = of_head(query_pair, head)
            d_head = of_head(d_pair, head)
            log_totals = lse_ref[pl.ds(2 * pair + head, 1), start:end]
            exact = jnp.exp(right_transposed(keys, query_head) + (bias - log_totals))
            d_probs = right_transposed(values, d_head)
            inner = jnp.sum(exact * d_probs, axis=0, keepdims=True)
            d_scores = (exact * (d_probs - inner)).astype(BF16)
            dv_acc[first:last, :] += product(exact.astype(BF16), d_head)
            dk_acc[first:last, :] += product(d_scores, query_head)
            part = row_outer(d_scores, of_head(keys, head))
            d_query = part if d_query is None else d_query + part
        d_queries.append((start, end, d_query))
    return d_queries


def store_halves(core, kept, sent, place, value):
    half = value.shape[-1] // 2
    there = slice(place, place + half)

    @pl.when(core == 0)
    def _():
        kept[..., there] = value[..., :half]
        sent[..., there] = value[..., half:]

    @pl.when(core != 0)
    def _():
        kept[..., there] = value[..., half:]
        sent[..., there] = value[..., :half]


def masked_bias(seg_col, seg_row, keys_first):
    shape = (seg_col.shape[0], seg_row.shape[1])
    rows = lax.broadcasted_iota(jnp.int32, shape, 0)
    lanes = lax.broadcasted_iota(jnp.int32, shape, 1)
    ordered = rows <= lanes if keys_first else lanes <= rows
    return jnp.where(ordered & (seg_col[...] == seg_row[...]), 0.0, NEG)


def put_together(core, both, theirs, whole_rows):
    length = theirs.shape[0]

    @pl.when(core == 0)
    def _():
        whole_rows[:length, :] = both[0]
        whole_rows[length:, :] = theirs[...]

    @pl.when(core != 0)
    def _():
        whole_rows[:length, :] = theirs[...]
        whole_rows[length:, :] = both[1]


def project_kernel(scalars, both, theirs, gains, weight, hidden, normed, qkv, gain_rows):
    @pl.when(pl.program_id(0) == 0)
    def _():
        put_together(scalars[1], both, theirs, hidden)
        rows = jnp.transpose(gains[...].astype(F32))[: gain_rows.shape[0], :]
        gain_rows[...] = rows
        values = hidden[...].astype(F32)
        normed[...] = (values * inverse_rms(values) * rows[0:1, :]).astype(BF16)

    qkv[...] = product(normed[...], weight[...]).astype(BF16)


def project_cross_kernel(
    scalars, both, theirs, normed_cross, weight, encoded, ckv, cross_queries
):
    step = pl.program_id(0)

    @pl.when(step == 0)
    def _():
        put_together(scalars[1], both, theirs, encoded)

    @pl.when(step == 1)
    def _():
        cross_queries[...] = product(normed_cross[...], weight[...]).astype(BF16)

    @pl.when(step != 1)
    def _():
        ckv[...] = product(encoded[...], weight[...]).astype(BF16)


def self_forward_kernel(
    blocks,
    seg_row,
    seg_col,
    hidden,
    gain_rows,
    q_ref,
    k_ref,
    v_ref,
    w_o,
    attended,
    lse_ref,
    after_self,
    normed_cross,
    bias,
    lse_cols,
    mixed,
):
    @pl.when(pl.program_id(0) == 0)
    def _():
        bias[...] = masked_bias(seg_col, seg_row, False)
        lse_cols[...] = jnp.zeros_like(lse_cols)

    pair_forward(
        blocks,
        lambda start, end, first, last: bias[start:end, first:last],
        q_ref,
        k_ref,
        v_ref,
        mixed,
        lse_ref,
        lse_cols,
    )
    place = pl.multiple_of(pl.program_id(0) * LANES, LANES)
    attended[:, pl.ds(place, LANES)] = mixed[...]

    @pl.when(pl.program_id(0) == pl.num_programs(0) - 1)
    def _():
        values = hidden[...].astype(F32) + product(attended[...], w_o[...])
        after_self[...] = values
        normed_cross[...] = (values * inverse_rms(values) * gain_rows[1:2, :]).astype(BF16)


def cross_forward_kernel(
    blocks,
    count,
    after_self,
    gain_rows,
    q_ref,
    k_ref,
    v_ref,
    w_co,
    attended,
    lse_ref,
    after_cross,
    normed_ffn,
    lse_cols,
    mixed,
):
    @pl.when(pl.program_id(0) == 0)
    def _():
        lse_cols[...] = jnp.zeros_like(lse_cols)

    places = lax.broadcasted_iota(jnp.int32, (1, k_ref.shape[0]), 1)
    bias = jnp.where(places < count[0], 0.0, NEG)
    pair_forward(
        blocks,
        lambda start, end, first, last: bias,
        q_ref,
        k_ref,
        v_ref,
        mixed,
        lse_ref,
        lse_cols,
    )
    place = pl.multiple_of(pl.program_id(0) * LANES, LANES)
    attended[:, pl.ds(place, LANES)] = mixed[...]

    @pl.when(pl.program_id(0) == pl.num_programs(0) - 1)
    def _():
        values = after_self[...] + product(attended[...], w_co[...])
        after_cross[...] = values
        normed_ffn[...] = (values * inverse_rms(values) * gain_rows[2:3, :]).astype(BF16)


def ffn_kernel(
    scalars,
    normed,
    both,
    theirs,
    after_cross,
    gain_rows,
    w_in,
    w_out,
    out_hidden,
    d_after_cross,
    gain_grad,
    kept_in,
    sent_in,
    kept_out,
    sent_out,
    out_acc,
    dn_acc,
    normed_t,
    branch,
):
    step = pl.program_id(0)

    @pl.when(step == 0)
    def _():
        put_together(scalars[1], both, theirs, branch)
        normed_t[...] = jnp.transpose(normed[...])
        out_acc[...] = after_cross[...]
        dn_acc[...] = jnp.zeros_like(dn_acc)

    width = normed.shape[1]
    up = w_in[...].reshape(width, -1)
    down = w_out[...]
    pre = product(normed[...], up)
    bent = jnp.tanh(GELU_RATE * (pre + GELU_CUBIC * pre * pre * pre))
    half = 0.5 * (1.0 + bent)
    hidden_act = (pre * half).astype(BF16)
    slope = half + 0.5 * pre * (1.0 - bent * bent) * GELU_RATE * (
        1.0 + 3.0 * GELU_CUBIC * pre * pre
    )
    out_acc[...] += product(hidden_act, down)
    d_pre = (right_transposed(branch[...], down) * slope).astype(BF16)
    grad_out = row_outer(hidden_act, branch[...]).astype(BF16)
    store_halves(scalars[1], kept_out, sent_out, 0, grad_out)
    grad_in = product(normed_t[...], d_pre).astype(BF16)
    grad_in = grad_in.reshape(kept_in.shape[:-1] + (width,))
    store_halves(scalars[1], kept_in, sent_in, 0, grad_in)
    dn_acc[...] += right_transposed(d_pre, up)

    @pl.when(step == pl.num_programs(0) - 1)
    def _():
        out_hidden[...] = out_acc[...].astype(BF16)
        values = after_cross[...]
        d_values, d_gain = norm_backward(
            values, inverse_rms(values), gain_rows[2:3, :], dn_acc[...]
        )
        d_after_cross[...] = branch[...].astype(F32) + d_values
        gain_grad[...] = jnp.broadcast_to(d_gain, gain_grad.shape)


def branch_kernel(scalars, d_after, attended, w_out, d_att, kept, sent):
    branch = d_after[...].astype(BF16)
    d_mixed = right_transposed(branch, w_out[...]).astype(BF16)
    for pair in range(d_att.shape[0]):
        d_att[pair] = d_mixed[:, pair * LANES : (pair + 1) * LANES]
    grad_out = row_outer(attended[...], branch).astype(BF16)
    store_halves(scalars[1], kept, sent, 0, grad_out)


def cross_backward_kernel(
    blocks,
    scalars,
    q_ref,
    k_ref,
    v_ref,
    d_att,
    lse_ref,
    d_after_cross,
    after_self,
    normed_cross,
    encoded,
    gain_rows,
    w_cq,
    w_ck,
    w_cv,
    d_after_self,
    kept,
    sent,
    grad_encoded,
    gain_grad,
    dq_all,
    dkv_all,
    dk_acc,
    dv_acc,
):
    step = pl.program_id(0)
    width = d_after_cross.shape[1]
    half = width // 2
    places = lax.broadcasted_iota(jnp.int32, (k_ref.shape[0], 1), 0)
    bias = jnp.where(places < scalars[0], 0.0, NEG)
    d_queries = pair_backward(
        blocks,
        lambda start, end, first, last: bias,
        q_ref,
        k_ref,
        v_ref,
        d_att.at[0],
        lse_ref,
        dk_acc,
        dv_acc,
    )
    place = pl.multiple_of(step * LANES, LANES)
    for start, end, d_query in d_queries:
        dq_all[start:end, pl.ds(place, LANES)] = d_query.astype(BF16)
    dkv_all[:, pl.ds(place, LANES)] = dk_acc[...].astype(BF16)
    dkv_all[:, pl.ds(width + place, LANES)] = dv_acc[...].astype(BF16)

    @pl.when(step == pl.num_programs(0) - 1)
    def _():
        dq = dq_all[...]
        grad_query = row_outer(normed_cross[...], dq).astype(BF16)
        grad_kv = row_outer(encoded[...], dkv_all[...]).astype(BF16)
        store_halves(scalars[1], kept, sent, 0, grad_query)
        store_halves(scalars[1], kept, sent, half, grad_kv[:, :width])
        store_halves(scalars[1], kept, sent, 2 * half, grad_kv[:, width:])
        grad_encoded[...] = right_transposed(dkv_all[:, :width], w_ck[...]) + right_transposed(
            dkv_all[:, width:], w_cv[...]
        )
        values = after_self[...]
        d_values, d_gain = norm_backward(
            values,
            inverse_rms(values),
            gain_rows[1:2, :],
            right_transposed(dq, w_cq[...]),
        )
        d_after_self[...] = d_after_cross[...] + d_values
        gain_grad[...] = jnp.broadcast_to(d_gain, gain_grad.shape)


def self_backward_pairs(
    blocks, seg_row, seg_col, q_ref, k_ref, v_ref, d_att, lse_ref, d_all, bias, dk_acc, dv_acc, first
):
    @pl.when(pl.program_id(0) == 0)
    def _():
        bias[...] = masked_bias(seg_col, seg_row, True)

    d_queries = pair_backward(
        blocks,
        lambda start, end, first_key, last_key: bias[first_key:last_key, start:end],
        q_ref,
        k_ref,
        v_ref,
        d_att.at[0],
        lse_ref,
        dk_acc,
        dv_acc,
        first,
    )
    place = pl.multiple_of(pl.program_id(0) * LANES, LANES)
    for start, end, d_query in d_queries:
        d_all[0, start:end, pl.ds(place, LANES)] = d_query.astype(BF16)
    d_all[1, :, pl.ds(place, LANES)] = dk_acc[...].astype(BF16)
    d_all[2, :, pl.ds(place, LANES)] = dv_acc[...].astype(BF16)


def self_backward_first_kernel(
    blocks, seg_row, seg_col, q_ref, k_ref, v_ref, d_att, lse_ref, d_all, bias, dk_acc, dv_acc
):
    self_backward_pairs(
        blocks, seg_row, seg_col, q_ref, k_ref, v_ref, d_att, lse_ref, d_all, bias, dk_acc, dv_acc, 0
    )


def self_backward_last_kernel(
    blocks,
    first,
    scalars,
    seg_row,
    seg_col,
    q_ref,
    k_ref,
    v_ref,
    d_att,
    lse_ref,
    d_first,
    d_after_self,
    hidden,
    normed_self,
    gain_rows,
    gain_grad_cross,
    gain_grad_ffn,
    w_q,
    w_k,
    w_v,
    grad_hidden,
    kept,
    sent,
    bias,
    d_all,
    dk_acc,
    dv_acc,
):
    self_backward_pairs(
        blocks,
        seg_row,
        seg_col,
        q_ref,
        k_ref,
        v_ref,
        d_att,
        lse_ref,
        d_all,
        bias,
        dk_acc,
        dv_acc,
        first,
    )
    width = d_after_self.shape[1]

    @pl.when(pl.program_id(0) == pl.num_programs(0) - 1)
    def _():
        d_normed = None
        for i, weight_ref in enumerate((w_q, w_k, w_v)):
            d_out = jnp.concatenate([d_first[i], d_all[i]], axis=1)
            grad = row_outer(normed_self[...], d_out)
            store_halves(scalars[1], kept, sent, i * width // 2, grad.astype(BF16))
            part = right_transposed(d_out, weight_ref[...])
            d_normed = part if d_normed is None else d_normed + part
        values = hidden[...].astype(F32)
        d_values, d_gain = norm_backward(
            values, inverse_rms(values), gain_rows[0:1, :], d_normed
        )
        grad_hidden[...] = d_after_self[...] + d_values
        row = lax.broadcasted_iota(jnp.int32, (LANES, width), 0)
        gain_grads = jnp.where(row == 0, d_gain, 0.0)
        gain_grads = jnp.where(row == 1, gain_grad_cross[0:1, :], gain_grads)
        gain_grads = jnp.where(row == 2, gain_grad_ffn[0:1, :], gain_grads)
        gain_columns = jnp.transpose(gain_grads).astype(BF16)
        kept[:, 3 * width // 2 :] = gain_columns
        sent[:, 3 * width // 2 :] = gain_columns


def columns(rows, offset):
    return pl.BlockSpec((rows, LANES), lambda step: (0, offset + step))


def whole(shape, place=None):
    place = (0,) * len(shape) if place is None else place
    return pl.BlockSpec(shape, lambda step: place)


def like(*shapes):
    return [jax.ShapeDtypeStruct(shape, dtype) for shape, dtype in shapes]


def call(kernel, name, steps, in_specs, out_specs, out_shape, scratch, flops, args, grant=56):
    size = sum(int(a.size) * a.dtype.itemsize for a in args)
    return pl.pallas_call(
        kernel,
        grid=(steps,),
        in_specs=in_specs,
        out_specs=out_specs,
        out_shape=out_shape,
        scratch_shapes=scratch,
        compiler_params=pltpu.CompilerParams(
            dimension_semantics=("arbitrary",), vmem_limit_bytes=grant << 20
        ),
        cost_estimate=pl.CostEstimate(flops=flops, bytes_accessed=size, transcendentals=0),
        name=name,
    )(*args)


QUERY, VALUE, KEY, OUT = range(4)
CROSS_KEY, CROSS_QUERY, CROSS_VALUE, CROSS_OUT = range(4)


def weight(width, place):
    return pl.BlockSpec((None, width, width), lambda step: (place, 0, 0))


def project(scalars, both, theirs, gains, self_set):
    cores, half_length, width = both.shape
    length = cores * half_length
    shape = (length, width)
    return call(
        project_kernel,
        "project",
        3,
        [
            pl.BlockSpec(memory_space=pltpu.SMEM),
            whole(both.shape),
            whole(theirs.shape),
            whole(gains.shape),
            pl.BlockSpec((None, width, width), lambda step: (2 * step % 3, 0, 0)),
        ],
        [
            whole(shape),
            whole(shape),
            pl.BlockSpec((length, width), lambda step: (0, step)),
            whole((8, width)),
        ],
        like((shape, BF16), (shape, BF16), ((length, 3 * width), BF16), ((8, width), F32)),
        [],
        6 * length * width * width,
        (scalars, both, theirs, gains, self_set),
    )


def project_cross(scalars, both, theirs, normed_cross, cross_set):
    length, width = normed_cross.shape
    keys = both.shape[0] * both.shape[1]
    return call(
        project_cross_kernel,
        "project_cross",
        3,
        [
            pl.BlockSpec(memory_space=pltpu.SMEM),
            whole(both.shape),
            whole(theirs.shape),
            whole(normed_cross.shape),
            pl.BlockSpec((None, width, width), lambda step: (step, 0, 0)),
        ],
        [
            whole((keys, width)),
            pl.BlockSpec((keys, width), lambda step: (0, step // 2)),
            whole(normed_cross.shape),
        ],
        like(((keys, width), BF16), ((keys, 2 * width), BF16), (normed_cross.shape, BF16)),
        [],
        2 * width * width * (length + 2 * keys),
        (scalars, both, theirs, normed_cross, cross_set),
    )


def self_forward(qkv, seg_row, seg_col, hidden, gain_rows, self_set):
    length, width = hidden.shape
    pairs = width // LANES
    return call(
        functools.partial(self_forward_kernel, self_blocks(length)),
        "self_forward",
        pairs,
        [
            whole(seg_row.shape),
            whole(seg_col.shape),
            whole(hidden.shape),
            whole(gain_rows.shape),
            columns(length, 0),
            columns(length, pairs),
            columns(length, 2 * pairs),
            weight(width, OUT),
        ],
        [
            whole(hidden.shape),
            whole((16, length)),
            whole(hidden.shape),
            whole(hidden.shape),
        ],
        like(
            (hidden.shape, BF16),
            ((16, length), F32),
            (hidden.shape, F32),
            (hidden.shape, BF16),
        ),
        [
            pltpu.VMEM((length, length), F32),
            pltpu.VMEM((length, LANES), F32),
            pltpu.VMEM((length, LANES), BF16),
        ],
        4 * length * width * (length + width),
        (
            seg_row,
            seg_col,
            hidden,
            gain_rows,
            qkv,
            qkv,
            qkv,
            self_set,
        ),
    )


def cross_forward(queries, ckv, count, after_self, gain_rows, cross_set):
    length, width = queries.shape
    keys = ckv.shape[0]
    pairs = width // LANES
    return call(
        functools.partial(cross_forward_kernel, cross_blocks(length, keys)),
        "cross_forward",
        pairs,
        [
            pl.BlockSpec(memory_space=pltpu.SMEM),
            whole(queries.shape),
            whole(gain_rows.shape),
            columns(length, 0),
            columns(keys, 0),
            columns(keys, pairs),
            weight(width, CROSS_OUT),
        ],
        [
            whole(queries.shape),
            whole((16, length)),
            whole(queries.shape),
            whole(queries.shape),
        ],
        like(
            (queries.shape, BF16),
            ((16, length), F32),
            (queries.shape, F32),
            (queries.shape, BF16),
        ),
        [pltpu.VMEM((length, LANES), F32), pltpu.VMEM((length, LANES), BF16)],
        2 * length * width * (2 * keys + width),
        (count, after_self, gain_rows, queries, ckv, ckv, cross_set),
    )


def feed_forward(scalars, normed, both, theirs, after_cross, gain_rows, ffn_set, w_in):
    length, width = normed.shape
    groups, steps, rows, _ = w_in.shape
    block = pl.BlockSpec((groups, 1, rows, width), lambda step: (0, step, 0, 0))
    half_block = pl.BlockSpec((groups, 1, rows, width // 2), lambda step: (0, step, 0, 0))
    half_rows = pl.BlockSpec((width, width // 2), lambda step: (step, 0))
    half_in = ((groups, steps, rows, width // 2), BF16)
    half_out = ((steps * width, width // 2), BF16)
    return call(
        ffn_kernel,
        "feed_forward",
        steps,
        [
            pl.BlockSpec(memory_space=pltpu.SMEM),
            whole(normed.shape),
            whole(both.shape),
            whole(theirs.shape),
            whole(normed.shape),
            whole(gain_rows.shape),
            block,
            pl.BlockSpec((width, width), lambda step: (step, 1)),
        ],
        [
            whole(normed.shape),
            whole(normed.shape),
            whole((8, width)),
            half_block,
            half_block,
            half_rows,
            half_rows,
        ],
        like(
            (normed.shape, BF16),
            (normed.shape, F32),
            ((8, width), F32),
            half_in,
            half_in,
            half_out,
            half_out,
        ),
        [
            pltpu.VMEM(normed.shape, F32),
            pltpu.VMEM(normed.shape, F32),
            pltpu.VMEM((width, length), BF16),
            pltpu.VMEM((length, width), BF16),
        ],
        12 * length * width * width * steps,
        (scalars, normed, both, theirs, after_cross, gain_rows, w_in, ffn_set),
        grant=56,
    )


def branch_backward(scalars, d_after, attended, weight_set, place):
    length, width = d_after.shape
    pairs = width // LANES
    halves = (width, width // 2)
    return call(
        branch_kernel,
        "branch_backward",
        1,
        [
            pl.BlockSpec(memory_space=pltpu.SMEM),
            whole(d_after.shape),
            whole(attended.shape),
            weight(width, place),
        ],
        [whole((pairs, length, LANES)), whole(halves), whole(halves)],
        like(((pairs, length, LANES), BF16), (halves, BF16), (halves, BF16)),
        [],
        4 * length * width * width,
        (scalars, d_after, attended, weight_set),
    )


def pair_block(length, first):
    return pl.BlockSpec((1, length, LANES), lambda step: (first + step, 0, 0))


def cross_backward(
    scalars,
    queries,
    ckv,
    d_att,
    lse,
    d_after_cross,
    after_self,
    normed_cross,
    encoded,
    gain_rows,
    cross_set,
):
    length, width = queries.shape
    keys = ckv.shape[0]
    pairs = width // LANES
    halves = (width, 3 * width // 2)
    return call(
        functools.partial(cross_backward_kernel, cross_blocks(length, keys)),
        "cross_backward",
        pairs,
        [
            pl.BlockSpec(memory_space=pltpu.SMEM),
            columns(length, 0),
            columns(keys, 0),
            columns(keys, pairs),
            pair_block(length, 0),
            whole(lse.shape),
            whole(queries.shape),
            whole(queries.shape),
            whole(queries.shape),
            whole(encoded.shape),
            whole(gain_rows.shape),
            weight(width, CROSS_QUERY),
            weight(width, CROSS_KEY),
            weight(width, CROSS_VALUE),
        ],
        [
            whole(queries.shape),
            whole(halves),
            whole(halves),
            whole(encoded.shape),
            whole((8, width)),
        ],
        like(
            (queries.shape, F32),
            (halves, BF16),
            (halves, BF16),
            (encoded.shape, F32),
            ((8, width), F32),
        ),
        [
            pltpu.VMEM((length, width), BF16),
            pltpu.VMEM((keys, 2 * width), BF16),
            pltpu.VMEM((keys, LANES), F32),
            pltpu.VMEM((keys, LANES), F32),
        ],
        2 * length * width * (5 * keys + 4 * width),
        (
            scalars,
            queries,
            ckv,
            ckv,
            d_att,
            lse,
            d_after_cross,
            after_self,
            normed_cross,
            encoded,
            gain_rows,
            cross_set,
            cross_set,
            cross_set,
        ),
    )


def self_backward_first(seg_row, seg_col, qkv, d_att, lse):
    length, width = qkv.shape[0], qkv.shape[1] // 3
    pairs = width // LANES
    done = 2 * pairs // 3
    return call(
        functools.partial(self_backward_first_kernel, self_blocks(length)),
        "self_backward_first",
        done,
        [
            whole(seg_row.shape),
            whole(seg_col.shape),
            columns(length, 0),
            columns(length, pairs),
            columns(length, 2 * pairs),
            pair_block(length, 0),
            whole(lse.shape),
        ],
        whole((3, length, done * LANES)),
        jax.ShapeDtypeStruct((3, length, done * LANES), BF16),
        [
            pltpu.VMEM((length, length), F32),
            pltpu.VMEM((length, LANES), F32),
            pltpu.VMEM((length, LANES), F32),
        ],
        4 * length * width * length,
        (seg_row, seg_col, qkv, qkv, qkv, d_att, lse),
    )


def self_backward_last(
    scalars,
    seg_row,
    seg_col,
    qkv,
    d_att,
    lse,
    d_first,
    d_after_self,
    hidden,
    normed_self,
    gain_rows,
    gain_grad_cross,
    gain_grad_ffn,
    self_set,
):
    length, width = hidden.shape
    pairs = width // LANES
    done = 2 * pairs // 3
    halves = (width, 3 * width // 2 + LANES)
    return call(
        functools.partial(self_backward_last_kernel, self_blocks(length), done),
        "self_backward_last",
        pairs - done,
        [
            pl.BlockSpec(memory_space=pltpu.SMEM),
            whole(seg_row.shape),
            whole(seg_col.shape),
            columns(length, done),
            columns(length, pairs + done),
            columns(length, 2 * pairs + done),
            pair_block(length, done),
            whole(lse.shape),
            whole(d_first.shape),
            whole(hidden.shape),
            whole(hidden.shape),
            whole(hidden.shape),
            whole(gain_rows.shape),
            whole(gain_rows.shape),
            whole(gain_rows.shape),
            weight(width, QUERY),
            weight(width, KEY),
            weight(width, VALUE),
        ],
        [whole(hidden.shape), whole(halves), whole(halves)],
        like((hidden.shape, F32), (halves, BF16), (halves, BF16)),
        [
            pltpu.VMEM((length, length), F32),
            pltpu.VMEM((3, length, (pairs - done) * LANES), BF16),
            pltpu.VMEM((length, LANES), F32),
            pltpu.VMEM((length, LANES), F32),
        ],
        2 * length * width * (2 * length + 6 * width),
        (
            scalars,
            seg_row,
            seg_col,
            qkv,
            qkv,
            qkv,
            d_att,
            lse,
            d_first,
            d_after_self,
            hidden,
            normed_self,
            gain_rows,
            gain_grad_cross,
            gain_grad_ffn,
            self_set,
            self_set,
            self_set,
        ),
    )


def grid_of(chips):
    side = 1
    while 2 * side**3 < chips:
        side += 1
    return (2 * side, side, side) if 2 * side**3 == chips else (1, 1, chips)


def axis_stride(grid, axis):
    stride = 1
    for extent in grid[axis + 1 :]:
        stride *= extent
    return stride


def coordinate(grid, axis):
    return lax.axis_index("dp") // axis_stride(grid, axis) % grid[axis]


def shifted(values, grid, axis, shift):
    stride, extent = axis_stride(grid, axis), grid[axis]
    chips = grid[0] * grid[1] * grid[2]
    pairs = []
    for chip in range(chips):
        at = chip // stride % extent
        pairs.append((chip, chip + ((at + shift) % extent - at) * stride))
    return lax.ppermute(values, "dp", pairs)


def swapped(values):
    cores = lax.axis_size("seq")
    return lax.ppermute(values, "seq", [(i, (i + 1) % cores) for i in range(cores)])


def total(parts):
    result = parts[0].astype(F32)
    for part in parts[1:]:
        result = result + part.astype(F32)
    return result


def pieces_kernel(plan, *refs):
    outputs = refs[len(refs) - len(plan) :]
    at = 1
    for output, sources in zip(outputs, plan):
        for start, end, count in sources:
            value = total([refs[at + i][:, 0] for i in range(count)])
            output[:, :, :, start:end] = value.astype(BF16)
            at += count


def pieces(groups):
    outers = []
    for sources, dim, _ in groups:
        outer = 1
        for n in sources[0][0][0].shape[:dim]:
            outer *= n
        outers.append(outer)
    steps = 1 if any(outer % 2 for outer in outers) else 2
    plan, args, in_specs, out_specs, out_shape, finals, all_places = [], [], [], [], [], [], []
    size = 0
    for (sources, dim, places), outer in zip(groups, outers):
        shape = sources[0][0][0].shape
        before, extent, after, rows = shape[:dim], shape[dim], shape[dim + 1 : -2], shape[-2]
        inner = 1
        for n in after:
            inner *= n
        lead = outer // steps
        for place in places:
            width, spans = 0, []
            for parts, columns_, block in sources:
                spans.append((width, width + columns_, len(parts)))
                width += columns_
                for part in parts:
                    args.append(part.reshape(outer, extent, inner, rows, part.shape[-1]))
                    in_specs.append(
                        pl.BlockSpec(
                            (lead, 1, inner, rows, columns_),
                            lambda g, at, o=len(all_places), block=block: (g, at[o], 0, 0, block),
                        )
                    )
                    size += outer * inner * rows * columns_
            plan.append(spans)
            all_places.append(place)
            out_specs.append(
                pl.BlockSpec((lead, inner, rows, width), lambda g, at: (g, 0, 0, 0))
            )
            out_shape.append(jax.ShapeDtypeStruct((outer, inner, rows, width), BF16))
            finals.append(before + after + (rows, width))
            size += outer * inner * rows * width
    result = pl.pallas_call(
        functools.partial(pieces_kernel, plan),
        grid_spec=pltpu.PrefetchScalarGridSpec(
            num_scalar_prefetch=1, grid=(steps,), in_specs=in_specs, out_specs=out_specs
        ),
        out_shape=out_shape,
        compiler_params=pltpu.CompilerParams(
            dimension_semantics=("arbitrary",), vmem_limit_bytes=max(16 << 20, 6 * size)
        ),
        cost_estimate=pl.CostEstimate(flops=0, bytes_accessed=2 * size, transcendentals=0),
        name="pieces",
    )(jnp.stack(all_places).astype(jnp.int32), *args)
    return [r.reshape(final) for r, final in zip(result, finals)]


def scattered(grid, *groups):
    wanted = []
    for sources, axis, dim in groups:
        here, extent = coordinate(grid, axis), grid[axis]
        wanted.append((sources, dim, [(here + shift) % extent for shift in range(extent)]))
    taken = pieces(wanted)
    results = []
    for _, axis, _ in groups:
        own, *others = taken[: grid[axis]]
        taken = taken[grid[axis] :]
        results.append(
            [own]
            + [shifted(other, grid, axis, shift) for shift, other in enumerate(others, start=1)]
        )
    return results


def assemble_kernel(count, chips, *refs):
    inputs, (weights, gains) = refs[: 2 * 2 * count], refs[2 * 2 * count :]
    core = chips[chips.shape[0] - 1]
    width = weights.shape[-1]
    for which in range(2):
        place = core if which == 0 else 1 - core
        at = 0
        for number in range(2 * count):
            source = inputs[which * 2 * count + number]
            second = number >= count
            for i in range(source.shape[0]):
                for k in range(source.shape[1]):
                    chip = chips[at]
                    at += 1
                    if second:
                        weights[2 + place, chip] = source[i, k, :, :width]
                        if which == 0 and gains is not None:
                            gains[chip] = source[i, k, :, width:]
                    else:
                        weights[place, chip] = source[i, k]


def along(values, grid, axis):
    return [values] + [shifted(values, grid, axis, shift) for shift in range(1, grid[axis])]


def gather_z(matrices, grid):
    every = along(jnp.concatenate(matrices, axis=1), grid, 0)
    stacked, at = [], 0
    for matrix in matrices:
        end = at + matrix.shape[1]
        stacked.append(jnp.stack([values[:, at:end] for values in every]))
        at = end
    return stacked


def gather_near(first, second, grid):
    return jnp.stack(along(first, grid, 1)), jnp.stack(along(second, grid, 2))


def gather_far(first, second, grid):
    return along(first, grid, 2), along(second, grid, 1)


def gather_end(mine, other, grid):
    first_sets, second_sets = mine
    mine, other = first_sets + second_sets, other[0] + other[1]
    rows, width = first_sets[0].shape[-2:]
    chips = grid[0] * grid[1] * grid[2]
    here = [coordinate(grid, axis) for axis in range(3)]
    places = []
    for outer, inner in ((2, 1), (1, 2)):
        for far in range(grid[outer]):
            for near in range(grid[inner]):
                for deep in range(grid[0]):
                    at = [None, None, None]
                    at[outer] = (here[outer] - far) % grid[outer]
                    at[inner] = (here[inner] - near) % grid[inner]
                    at[0] = (here[0] - deep) % grid[0]
                    places.append((at[0] * grid[1] + at[1]) * grid[2] + at[2])
    places.append(lax.axis_index("seq"))
    assert len(first_sets) == len(second_sets)
    extra = second_sets[0].shape[-1] - width
    out_shape = [pltpu.HBM((4, chips, rows, width), BF16)]
    if extra:
        out_shape.append(pltpu.HBM((chips, rows, extra), BF16))
    in_vmem = pl.BlockSpec(memory_space=pltpu.VMEM)

    def kernel(places, *refs):
        assemble_kernel(len(first_sets), places, *(refs if extra else refs + (None,)))

    result = pl.pallas_call(
        kernel,
        in_specs=[pl.BlockSpec(memory_space=pltpu.SMEM)] + [in_vmem] * (2 * len(mine)),
        out_specs=[in_vmem] * len(out_shape),
        out_shape=out_shape,
        compiler_params=pltpu.CompilerParams(vmem_limit_bytes=48 << 20),
        cost_estimate=pl.CostEstimate(
            flops=0, bytes_accessed=16 * chips * rows * width, transcendentals=0
        ),
        name="assemble",
    )(jnp.stack(places).astype(jnp.int32), *mine, *other)
    weights = result[0].reshape(4, chips * rows, width)
    return weights, result[1].reshape(chips * rows, extra) if extra else None


def on_device(
    hidden_in,
    encoder_out,
    segment_ids,
    passage_counts,
    cotangent,
    w_query,
    w_key,
    w_value,
    w_out,
    w_cross_query,
    w_cross_key,
    w_cross_value,
    w_cross_out,
    w_ffn_in,
    w_ffn_out,
    gain_self,
    gain_cross,
    gain_ffn,
):
    cores = lax.axis_size("seq")
    core = lax.axis_index("seq")
    chips = lax.axis_size("dp")
    grid = grid_of(chips)
    width = hidden_in.shape[-1]
    half = width // 2
    ratio = w_ffn_in.shape[1] // width
    rows = w_query.shape[0]
    joint = ("dp", "seq")

    def own_rows(values):
        part = values.shape[0] // cores
        return lax.dynamic_slice_in_dim(values, core * part, part, 0)

    def in_order(mine, other, axis):
        first = jnp.where(core == 0, mine, other)
        second = jnp.where(core == 0, other, mine)
        return jnp.concatenate([first, second], axis=axis)

    ffn_in_rows = jnp.concatenate(
        [w_ffn_in[:, i * width : (i + 1) * width] for i in range(ratio)], axis=0
    )
    ffn_rows = own_rows(jnp.concatenate([ffn_in_rows, w_ffn_out], axis=1))
    gains = jnp.stack([gain_self, gain_cross, gain_ffn], axis=1)
    gains = jnp.pad(gains, ((0, 0), (0, LANES - gains.shape[1])))

    def by_core(here, there):
        return jnp.where(core == 0, here, there)

    def tied(value, others):
        return lax.optimization_barrier((value, others))

    def sent(values):
        return swapped(lax.dynamic_index_in_dim(values, 1 - core, 0, keepdims=False))

    def returned(values):
        length = values.shape[0] // cores
        mine = lax.dynamic_slice_in_dim(values, core * length, length, 0)
        theirs = lax.dynamic_slice_in_dim(values, (1 - core) * length, length, 0)
        return in_order(mine[None, None], swapped(theirs)[None, None], 0)

    def exchanged(sets):
        return tuple([swapped(values) for values in one] for one in sets)

    hidden_both, encoded_both, branch_both = hidden_in[:, 0], encoder_out[:, 0], cotangent[:, 0]
    hidden_theirs, encoded_theirs, branch_theirs = (
        sent(hidden_both),
        sent(encoded_both),
        sent(branch_both),
    )
    segments = in_order(
        lax.dynamic_index_in_dim(segment_ids[:, 0], core, 0, keepdims=False),
        sent(segment_ids[:, 0]),
        0,
    )
    count = lax.dynamic_index_in_dim(passage_counts[:, 0], core, 0, keepdims=False)
    scalars = jnp.stack([count, core.astype(jnp.int32)])
    seg_row = segments[None, :]
    seg_col = segments[:, None]

    stacked = gather_z(
        [
            by_core(w_query, w_value),
            jnp.concatenate([by_core(w_key, w_out), gains], axis=1),
            by_core(w_cross_key, w_cross_query),
            by_core(w_cross_value, w_cross_out),
        ],
        grid,
    )
    self_rows, cross_rows = stacked[:2], stacked[2:]
    ffn_rows, self_rows = tied(ffn_rows, self_rows)
    ffn_set = lax.all_gather(ffn_rows, joint, axis=0, tiled=True)
    self_rows = gather_near(*self_rows, grid)
    self_near = [[values] for values in self_rows]
    self_far = [values[1:] for values in gather_far(*self_rows, grid)]
    self_other = exchanged(self_near)
    self_far, _ = tied(self_far, (self_other, scalars, seg_row, seg_col, hidden_theirs))
    cross_rows, self_far = tied(cross_rows, self_far)
    self_set, gains = gather_end(
        [near + far for near, far in zip(self_near, self_far)],
        [near + far for near, far in zip(self_other, exchanged(self_far))],
        grid,
    )
    cross_rows = along(cross_rows[0], grid, 1), along(cross_rows[1], grid, 2)

    w_in = ffn_set.reshape(chips, ratio, rows, 2 * width)
    if rows % 16:
        w_in = w_in[:, :, :, :width].transpose(1, 0, 2, 3).reshape(1, ratio, width, width)

    hidden, normed_self, qkv, gain_rows = project(
        scalars, hidden_both, hidden_theirs, gains, self_set
    )
    cross_rows, qkv = tied(cross_rows, qkv)
    cross_rows = [jnp.stack(values) for values in cross_rows]
    cross_near = [[values] for values in cross_rows]
    cross_far = [values[1:] for values in gather_far(*cross_rows, grid)]
    cross_other = exchanged(cross_near)
    qkv, (cross_near, cross_other) = tied(qkv, (cross_near, cross_other))
    attended, self_lse, after_self, normed_cross = self_forward(
        qkv, seg_row, seg_col, hidden, gain_rows, self_set
    )
    normed_cross, cross_far = tied(normed_cross, cross_far)
    cross_set, _ = gather_end(
        [near + far for near, far in zip(cross_near, cross_far)],
        [near + far for near, far in zip(cross_other, exchanged(cross_far))],
        grid,
    )
    encoded, ckv, cross_queries = project_cross(
        scalars, encoded_both, encoded_theirs, normed_cross, cross_set
    )
    cross_attended, cross_lse, after_cross, normed_ffn = cross_forward(
        cross_queries, ckv, scalars, after_self, gain_rows, cross_set
    )
    out_hidden, d_after_cross, gain_grad_ffn, kept_in, sent_in, kept_out, sent_out = feed_forward(
        scalars, normed_ffn, branch_both, branch_theirs, after_cross, gain_rows, ffn_set, w_in
    )

    def by_chip(values):
        if values.shape[0] == 1:
            values = values[0].reshape(ratio, chips, rows, -1).transpose(1, 0, 2, 3)
        return values.reshape(grid + (-1, values.shape[-1]))

    def whole_source(parts):
        return (parts, parts[0].shape[-1], 0)

    def along_first(first, second):
        return scattered(grid, (first, 2, 2), (second, 1, 1))

    def along_second(first, second):
        return scattered(grid, ([whole_source(first)], 1, 1), ([whole_source(second)], 2, 1))

    def along_z(first, second):
        return scattered(grid, ([whole_source(first), whole_source(second)], 0, 0))[0]

    ffn_in = [by_chip(kept_in), by_chip(swapped(sent_in))]
    ffn_out = [by_chip(kept_out), by_chip(swapped(sent_out))]
    d_att, kept_co, sent_co = branch_backward(
        scalars, d_after_cross, cross_attended, cross_set, CROSS_OUT
    )
    d_att, (ffn_in, ffn_out) = tied(d_att, (ffn_in, ffn_out))
    ffn_first, ffn_second = along_first([(ffn_in, half, 0)], [(ffn_out, half, 0)])
    cross_o = [by_chip(kept_co), by_chip(swapped(sent_co))]
    d_after_self, kept_c, sent_c, grad_encoded, gain_grad_cross = cross_backward(
        scalars,
        cross_queries,
        ckv,
        d_att,
        cross_lse,
        d_after_cross,
        after_self,
        normed_cross,
        encoded,
        gain_rows,
        cross_set,
    )
    d_after_self, (ffn_first, ffn_second) = tied(d_after_self, (ffn_first, ffn_second))
    ffn_first, ffn_second = along_second(ffn_first, ffn_second)
    d_after_self, _ = tied(d_after_self, (ffn_first[0], ffn_second[0]))
    cross_qkv = [by_chip(kept_c), by_chip(swapped(sent_c))]
    d_att, kept_o, sent_o = branch_backward(
        scalars, d_after_self, attended, self_set, OUT
    )
    self_o = [by_chip(kept_o), by_chip(swapped(sent_o))]
    cross_first, cross_second = along_first(
        [(cross_o, half, 0), (cross_qkv, half, 0), (self_o, half, 0)],
        [(cross_qkv, half, 1), (cross_qkv, half, 2)],
    )
    (ffn_first, ffn_second), _ = tied((ffn_first, ffn_second), (cross_first[0], cross_second[0]))
    ffn_parts = along_z(ffn_first, ffn_second)
    d_att, _ = tied(d_att, (cross_first[0], cross_second[0], ffn_parts[0]))
    d_first = self_backward_first(seg_row, seg_col, qkv, d_att, self_lse)
    d_first, (cross_first, cross_second) = tied(d_first, (cross_first, cross_second))
    cross_first, cross_second = along_second(cross_first, cross_second)
    d_first, _ = tied(d_first, (cross_first[0], cross_second[0]))
    grad_hidden, kept_s, sent_s = self_backward_last(
        scalars,
        seg_row,
        seg_col,
        qkv,
        d_att,
        self_lse,
        d_first,
        d_after_self,
        hidden,
        normed_self,
        gain_rows,
        gain_grad_cross,
        gain_grad_ffn,
        self_set,
    )
    sent_s, (ffn_parts, cross_first, cross_second) = tied(
        sent_s, (ffn_parts, cross_first, cross_second)
    )
    self_qkv = [by_chip(kept_s), by_chip(swapped(sent_s))]
    self_first, self_second = along_first(
        [(self_qkv, half, 0), (self_qkv, 2 * LANES, half // LANES)],
        [
            (self_qkv, half, 1),
            (self_qkv, LANES, 3 * half // LANES - 1),
            (self_qkv, LANES, 3 * half // LANES),
        ],
    )
    ffn_sum = total(ffn_parts)
    (cross_first, cross_second), (self_first, self_second) = tied(
        (cross_first, cross_second), (self_first, self_second)
    )
    self_first, self_second = along_second(self_first, self_second)
    (cross_first, cross_second), _ = tied(
        (cross_first, cross_second), (self_first[0], self_second[0])
    )
    cross_parts = along_z(cross_first, cross_second)
    (self_first, self_second), _ = tied((self_first, self_second), cross_parts[0])
    self_parts = along_z(self_first, self_second)
    cross_parts, _ = tied(cross_parts, self_parts[0])
    cross_sum = total(cross_parts)
    self_sum = total(self_parts)

    ffn_other, cross_other, self_other = swapped(ffn_sum), swapped(cross_sum), swapped(self_sum)

    def matrix(mine, other, i):
        there = slice(i * half, (i + 1) * half)
        return in_order(mine[:, there], other[:, there], 1)

    ffn_sum = ffn_sum.reshape(ratio, rows, 2 * half)
    ffn_other = ffn_other.reshape(ratio, rows, 2 * half)
    grad_ffn_in = jnp.concatenate(
        [matrix(ffn_sum[i], ffn_other[i], 0) for i in range(ratio)], axis=1
    )
    grad_ffn_out = jnp.concatenate(
        [matrix(ffn_sum[i], ffn_other[i], 1) for i in range(ratio)], axis=0
    )
    def value_columns(values):
        split = half + 2 * LANES
        return jnp.concatenate(
            [values[:, half:split], values[:, split + half : 3 * half]], axis=1
        )

    split = half + 2 * LANES
    gain_grads = self_sum[:, 3 * half :]
    return (
        returned(out_hidden),
        returned(grad_hidden),
        returned(grad_encoded),
        matrix(self_sum, self_other, 0),
        in_order(self_sum[:, split : split + half], self_other[:, split : split + half], 1),
        in_order(value_columns(self_sum), value_columns(self_other), 1),
        matrix(cross_sum, cross_other, 2),
        matrix(cross_sum, cross_other, 1),
        matrix(cross_sum, cross_other, 3),
        matrix(cross_sum, cross_other, 4),
        matrix(cross_sum, cross_other, 0),
        grad_ffn_in,
        grad_ffn_out,
        gain_grads[:, 0],
        gain_grads[:, 1],
        gain_grads[:, 2],
    )


def solution(mesh):
    tokens = P(None, "dp", "seq", None)
    rows = P("dp", None)
    gain = P("dp")
    return jax.shard_map(
        on_device,
        mesh=mesh,
        in_specs=(tokens, tokens, P(None, "dp", "seq"), P(None, "dp"), tokens)
        + (rows,) * 10
        + (gain,) * 3,
        out_specs=(tokens,) * 3 + (rows,) * 10 + (gain,) * 3,
        check_vma=False,
    )
```

```python
import functools

import jax
import jax.numpy as jnp
from jax import lax
from jax.experimental import pallas as pl
from jax.experimental.pallas import tpu as pltpu
from jax.sharding import PartitionSpec as P

HEAD_DIM = 64
LANES = 128
SEGMENT_LIMIT = 384
QUERY_BLOCK = 256
EPS = 1e-06
NEG = -1e30
GELU_RATE = 0.7978845608
GELU_CUBIC = 0.044715
BF16 = jnp.bfloat16
F32 = jnp.float32


def product(left, right):
    return jnp.dot(left, right, preferred_element_type=F32)


def row_outer(left, right):
    return lax.dot_general(left, right, (((0,), (0,)), ((), ())), preferred_element_type=F32)


def right_transposed(left, right):
    return lax.dot_general(left, right, (((1,), (1,)), ((), ())), preferred_element_type=F32)


def inverse_rms(values):
    return lax.rsqrt(jnp.mean(values * values, axis=-1, keepdims=True) + EPS)


def norm_backward(values, scale, gain, d_normed):
    scaled = gain * d_normed
    d_values = scale * scaled - values * (scale * scale * scale) * jnp.mean(
        values * scaled, axis=-1, keepdims=True
    )
    return d_values


def self_blocks(length):
    blocks = []
    for start in range(0, length, QUERY_BLOCK):
        end = min(start + QUERY_BLOCK, length)
        first = max(0, start - SEGMENT_LIMIT + 1) // LANES * LANES
        blocks.append((start, end, first, end))
    return blocks


def cross_blocks(length, keys):
    return [
        (start, min(start + QUERY_BLOCK, length), 0, keys)
        for start in range(0, length, QUERY_BLOCK)
    ]


def of_head(values, head):
    lanes = lax.broadcasted_iota(jnp.int32, values.shape, 1)
    return jnp.where(lanes // HEAD_DIM == head, values, jnp.zeros_like(values))


def pair_forward(blocks, bias_of, q_ref, k_ref, v_ref, o_ref, lse_ref, lse_cols):
    pair = pl.program_id(0)
    lane = lax.broadcasted_iota(jnp.int32, (1, LANES), 1)
    for start, end, first, last in blocks:
        keys = k_ref[first:last, :]
        values = v_ref[first:last, :]
        query_pair = q_ref[start:end, :]
        bias = bias_of(start, end, first, last)
        mixed = []
        columns = lse_cols[start:end, :]
        for head in range(2):
            scores = right_transposed(of_head(query_pair, head), keys) + bias
            row_max = jnp.max(scores, axis=-1, keepdims=True)
            exponents = jnp.exp(scores - row_max)
            totals = jnp.sum(exponents, axis=-1, keepdims=True)
            mixed.append(product(exponents.astype(BF16), values) / totals)
            columns = jnp.where(lane == 2 * pair + head, row_max + jnp.log(totals), columns)
        o_ref[start:end, :] = jnp.where(lane < HEAD_DIM, mixed[0], mixed[1]).astype(BF16)
        lse_cols[start:end, :] = columns

    @pl.when(pair == pl.num_programs(0) - 1)
    def _():
        lse_ref[...] = jnp.transpose(lse_cols[...])[: lse_ref.shape[0], :]


def pair_backward(
    blocks, bias_of, q_ref, k_ref, v_ref, d_ref, lse_ref, dk_acc, dv_acc, first_pair=0
):
    pair = first_pair + pl.program_id(0)
    dk_acc[...] = jnp.zeros_like(dk_acc)
    dv_acc[...] = jnp.zeros_like(dv_acc)
    d_queries = []
    for start, end, first, last in blocks:
        keys = k_ref[first:last, :]
        values = v_ref[first:last, :]
        query_pair = q_ref[start:end, :]
        d_pair = d_ref[start:end, :]
        bias = bias_of(start, end, first, last)
        d_query = None
        for head in range(2):
            query_head = of_head(query_pair, head)
            d_head = of_head(d_pair, head)
            log_totals = lse_ref[pl.ds(2 * pair + head, 1), start:end]
            exact = jnp.exp(right_transposed(keys, query_head) + (bias - log_totals))
            d_probs = right_transposed(values, d_head)
            inner = jnp.sum(exact * d_probs, axis=0, keepdims=True)
            d_scores = (exact * (d_probs - inner)).astype(BF16)
            dv_acc[first:last, :] += product(exact.astype(BF16), d_head)
            dk_acc[first:last, :] += product(d_scores, query_head)
            part = row_outer(d_scores, of_head(keys, head))
            d_query = part if d_query is None else d_query + part
        d_queries.append((start, end, d_query))
    return d_queries


def store_halves(core, kept, sent, place, value):
    half = value.shape[-1] // 2
    there = slice(place, place + half)

    @pl.when(core == 0)
    def _():
        kept[..., there] = value[..., :half]
        sent[..., there] = value[..., half:]

    @pl.when(core != 0)
    def _():
        kept[..., there] = value[..., half:]
        sent[..., there] = value[..., :half]


def store_rows(core, mine, theirs, value):
    length = mine.shape[0]

    @pl.when(core == 0)
    def _():
        mine[...] = value[:length, :]
        theirs[...] = value[length:, :]

    @pl.when(core != 0)
    def _():
        mine[...] = value[length:, :]
        theirs[...] = value[:length, :]


def masked_bias(seg_col, seg_row, keys_first):
    shape = (seg_col.shape[0], seg_row.shape[1])
    rows = lax.broadcasted_iota(jnp.int32, shape, 0)
    lanes = lax.broadcasted_iota(jnp.int32, shape, 1)
    ordered = rows <= lanes if keys_first else lanes <= rows
    return jnp.where(ordered & (seg_col[...] == seg_row[...]), 0.0, NEG)


def put_together(core, both, theirs, whole_rows):
    length = theirs.shape[0]

    @pl.when(core == 0)
    def _():
        whole_rows[:length, :] = both[0]
        whole_rows[length:, :] = theirs[...]

    @pl.when(core != 0)
    def _():
        whole_rows[:length, :] = theirs[...]
        whole_rows[length:, :] = both[1]


def project_kernel(scalars, both, theirs, gains, weight, hidden, normed, qkv, gain_rows):
    @pl.when(pl.program_id(0) == 0)
    def _():
        put_together(scalars[1], both, theirs, hidden)
        rows = jnp.transpose(gains[...].astype(F32))[: gain_rows.shape[0], :]
        gain_rows[...] = rows
        values = hidden[...].astype(F32)
        normed[...] = (values * inverse_rms(values) * rows[0:1, :]).astype(BF16)

    qkv[...] = product(normed[...], weight[...]).astype(BF16)


def project_cross_kernel(
    scalars, both, theirs, normed_cross, weight, encoded, ckv, cross_queries
):
    step = pl.program_id(0)

    @pl.when(step == 0)
    def _():
        put_together(scalars[1], both, theirs, encoded)

    @pl.when(step == 1)
    def _():
        cross_queries[...] = product(normed_cross[...], weight[...]).astype(BF16)

    @pl.when(step != 1)
    def _():
        ckv[...] = product(encoded[...], weight[...]).astype(BF16)


def self_forward_kernel(
    blocks,
    seg_row,
    seg_col,
    hidden,
    gain_rows,
    q_ref,
    k_ref,
    v_ref,
    w_o,
    attended,
    lse_ref,
    after_self,
    normed_cross,
    bias,
    lse_cols,
    mixed,
):
    @pl.when(pl.program_id(0) == 0)
    def _():
        bias[...] = masked_bias(seg_col, seg_row, False)
        lse_cols[...] = jnp.zeros_like(lse_cols)

    pair_forward(
        blocks,
        lambda start, end, first, last: bias[start:end, first:last],
        q_ref,
        k_ref,
        v_ref,
        mixed,
        lse_ref,
        lse_cols,
    )
    place = pl.multiple_of(pl.program_id(0) * LANES, LANES)
    attended[:, pl.ds(place, LANES)] = mixed[...]

    @pl.when(pl.program_id(0) == pl.num_programs(0) - 1)
    def _():
        values = hidden[...].astype(F32) + product(attended[...], w_o[...])
        after_self[...] = values
        normed_cross[...] = (values * inverse_rms(values) * gain_rows[1:2, :]).astype(BF16)


def cross_forward_kernel(
    blocks,
    count,
    after_self,
    gain_rows,
    q_ref,
    k_ref,
    v_ref,
    w_co,
    attended,
    lse_ref,
    after_cross,
    normed_ffn,
    lse_cols,
    mixed,
):
    @pl.when(pl.program_id(0) == 0)
    def _():
        lse_cols[...] = jnp.zeros_like(lse_cols)

    places = lax.broadcasted_iota(jnp.int32, (1, k_ref.shape[0]), 1)
    bias = jnp.where(places < count[0], 0.0, NEG)
    pair_forward(
        blocks,
        lambda start, end, first, last: bias,
        q_ref,
        k_ref,
        v_ref,
        mixed,
        lse_ref,
        lse_cols,
    )
    place = pl.multiple_of(pl.program_id(0) * LANES, LANES)
    attended[:, pl.ds(place, LANES)] = mixed[...]

    @pl.when(pl.program_id(0) == pl.num_programs(0) - 1)
    def _():
        values = after_self[...] + product(attended[...], w_co[...])
        after_cross[...] = values
        normed_ffn[...] = (values * inverse_rms(values) * gain_rows[2:3, :]).astype(BF16)


def ffn_kernel(
    scalars,
    normed,
    both,
    theirs,
    after_cross,
    gain_rows,
    w_in,
    w_out,
    out_mine,
    out_theirs,
    d_after_cross,
    grad_in,
    kept_out,
    sent_out,
    out_acc,
    dn_acc,
    normed_t,
    branch,
):
    step = pl.program_id(0)

    @pl.when(step == 0)
    def _():
        put_together(scalars[1], both, theirs, branch)
        normed_t[...] = jnp.transpose(normed[...])
        out_acc[...] = after_cross[...]
        dn_acc[...] = jnp.zeros_like(dn_acc)

    width = normed.shape[1]
    up = w_in[...].reshape(width, -1)
    down = w_out[...]
    pre = product(normed[...], up)
    bent = jnp.tanh(GELU_RATE * (pre + GELU_CUBIC * pre * pre * pre))
    half = 0.5 * (1.0 + bent)
    hidden_act = (pre * half).astype(BF16)
    slope = half + 0.5 * pre * (1.0 - bent * bent) * GELU_RATE * (
        1.0 + 3.0 * GELU_CUBIC * pre * pre
    )
    out_acc[...] += product(hidden_act, down)
    d_pre = (right_transposed(branch[...], down) * slope).astype(BF16)
    grad_out = row_outer(hidden_act, branch[...]).astype(BF16)
    store_halves(scalars[1], kept_out, sent_out, 0, grad_out)
    grad_in[...] = product(normed_t[...], d_pre).astype(BF16)
    dn_acc[...] += right_transposed(d_pre, up)

    @pl.when(step == pl.num_programs(0) - 1)
    def _():
        store_rows(scalars[1], out_mine, out_theirs, out_acc[...].astype(BF16))
        values = after_cross[...]
        d_values = norm_backward(values, inverse_rms(values), gain_rows[2:3, :], dn_acc[...])
        d_after_cross[...] = branch[...].astype(F32) + d_values


def attended_gradient(branch, w_out, d_att):
    d_mixed = right_transposed(branch, w_out[...]).astype(BF16)
    for pair in range(d_att.shape[0]):
        d_att[pair] = d_mixed[:, pair * LANES : (pair + 1) * LANES]


def cross_branch_kernel(d_after, w_out, d_att):
    attended_gradient(d_after[...].astype(BF16), w_out, d_att)


def cross_backward_kernel(
    blocks,
    scalars,
    q_ref,
    k_ref,
    v_ref,
    d_att,
    lse_ref,
    d_after_cross,
    after_self,
    normed_cross,
    cross_attended,
    self_attended,
    encoded,
    gain_rows,
    w_cq,
    w_ck,
    w_cv,
    w_o,
    d_after_self,
    d_att_self,
    kept,
    sent,
    encoded_mine,
    encoded_theirs,
    dq_all,
    dkv_all,
    dk_acc,
    dv_acc,
):
    step = pl.program_id(0)
    width = d_after_cross.shape[1]
    half = width // 2
    places = lax.broadcasted_iota(jnp.int32, (k_ref.shape[0], 1), 0)
    bias = jnp.where(places < scalars[0], 0.0, NEG)
    d_queries = pair_backward(
        blocks,
        lambda start, end, first, last: bias,
        q_ref,
        k_ref,
        v_ref,
        d_att.at[0],
        lse_ref,
        dk_acc,
        dv_acc,
    )
    place = pl.multiple_of(step * LANES, LANES)
    for start, end, d_query in d_queries:
        dq_all[start:end, pl.ds(place, LANES)] = d_query.astype(BF16)
    dkv_all[:, pl.ds(place, LANES)] = dk_acc[...].astype(BF16)
    dkv_all[:, pl.ds(width + place, LANES)] = dv_acc[...].astype(BF16)

    @pl.when(step == pl.num_programs(0) - 1)
    def _():
        dq = dq_all[...]
        grad_query = row_outer(normed_cross[...], dq).astype(BF16)
        grad_kv = row_outer(encoded[...], dkv_all[...]).astype(BF16)
        store_halves(scalars[1], kept, sent, 0, grad_query)
        store_halves(scalars[1], kept, sent, half, grad_kv[:, :width])
        store_halves(scalars[1], kept, sent, 2 * half, grad_kv[:, width:])
        grad_out = row_outer(cross_attended[...], d_after_cross[...].astype(BF16))
        store_halves(scalars[1], kept, sent, 3 * half, grad_out.astype(BF16))
        grad_encoded = right_transposed(dkv_all[:, :width], w_ck[...]) + right_transposed(
            dkv_all[:, width:], w_cv[...]
        )
        store_rows(scalars[1], encoded_mine, encoded_theirs, grad_encoded)
        values = after_self[...]
        d_values = norm_backward(
            values,
            inverse_rms(values),
            gain_rows[1:2, :],
            right_transposed(dq, w_cq[...]),
        )
        d_values = d_after_cross[...] + d_values
        d_after_self[...] = d_values
        branch = d_values.astype(BF16)
        attended_gradient(branch, w_o, d_att_self)
        grad_out = row_outer(self_attended[...], branch)
        store_halves(scalars[1], kept, sent, 4 * half, grad_out.astype(BF16))


def self_backward_pairs(
    blocks, seg_row, seg_col, q_ref, k_ref, v_ref, d_att, lse_ref, d_all, bias, dk_acc, dv_acc, first
):
    @pl.when(pl.program_id(0) == 0)
    def _():
        bias[...] = masked_bias(seg_col, seg_row, True)

    d_queries = pair_backward(
        blocks,
        lambda start, end, first_key, last_key: bias[first_key:last_key, start:end],
        q_ref,
        k_ref,
        v_ref,
        d_att.at[0],
        lse_ref,
        dk_acc,
        dv_acc,
        first,
    )
    place = pl.multiple_of(pl.program_id(0) * LANES, LANES)
    for start, end, d_query in d_queries:
        d_all[0, start:end, pl.ds(place, LANES)] = d_query.astype(BF16)
    d_all[1, :, pl.ds(place, LANES)] = dk_acc[...].astype(BF16)
    d_all[2, :, pl.ds(place, LANES)] = dv_acc[...].astype(BF16)


def self_backward_first_kernel(
    blocks, seg_row, seg_col, q_ref, k_ref, v_ref, d_att, lse_ref, d_all, bias, dk_acc, dv_acc
):
    self_backward_pairs(
        blocks, seg_row, seg_col, q_ref, k_ref, v_ref, d_att, lse_ref, d_all, bias, dk_acc, dv_acc, 0
    )


def self_backward_last_kernel(
    blocks,
    first,
    scalars,
    seg_row,
    seg_col,
    q_ref,
    k_ref,
    v_ref,
    d_att,
    lse_ref,
    d_first,
    normed_self,
    kept_q,
    kept_k,
    kept_v,
    sent_q,
    sent_k,
    sent_v,
    d_last,
    bias,
    dk_acc,
    dv_acc,
):
    self_backward_pairs(
        blocks,
        seg_row,
        seg_col,
        q_ref,
        k_ref,
        v_ref,
        d_att,
        lse_ref,
        d_last,
        bias,
        dk_acc,
        dv_acc,
        first,
    )

    @pl.when(pl.program_id(0) == pl.num_programs(0) - 1)
    def _():
        normed_t = jnp.transpose(normed_self[...])
        for i, (kept, sent) in enumerate(
            ((kept_q, sent_q), (kept_k, sent_k), (kept_v, sent_v))
        ):
            grad = product(normed_t, jnp.concatenate([d_first[i], d_last[i]], axis=1))
            store_halves(scalars[1], kept, sent, 0, grad.astype(BF16))


def self_input_kernel(
    scalars, d_first, d_last, d_after_self, hidden, gain_rows, w_q, w_k, w_v, mine, theirs
):
    d_normed = None
    for i, weight_ref in enumerate((w_q, w_k, w_v)):
        d_out = jnp.concatenate([d_first[i], d_last[i]], axis=1)
        part = right_transposed(d_out, weight_ref[...])
        d_normed = part if d_normed is None else d_normed + part
    values = hidden[...].astype(F32)
    d_values = norm_backward(values, inverse_rms(values), gain_rows[0:1, :], d_normed)
    store_rows(scalars[1], mine, theirs, d_after_self[...] + d_values)


def columns(rows, offset):
    return pl.BlockSpec((rows, LANES), lambda step: (0, offset + step))


def whole(shape, place=None):
    place = (0,) * len(shape) if place is None else place
    return pl.BlockSpec(shape, lambda step: place)


def like(*shapes):
    return [jax.ShapeDtypeStruct(shape, dtype) for shape, dtype in shapes]


def call(kernel, name, steps, in_specs, out_specs, out_shape, scratch, flops, args, grant=56):
    size = sum(int(a.size) * a.dtype.itemsize for a in args)
    return pl.pallas_call(
        kernel,
        grid=(steps,),
        in_specs=in_specs,
        out_specs=out_specs,
        out_shape=out_shape,
        scratch_shapes=scratch,
        compiler_params=pltpu.CompilerParams(
            dimension_semantics=("arbitrary",), vmem_limit_bytes=grant << 20
        ),
        cost_estimate=pl.CostEstimate(flops=flops, bytes_accessed=size, transcendentals=0),
        name=name,
    )(*args)


QUERY, VALUE, KEY, OUT = range(4)
CROSS_KEY, CROSS_QUERY, CROSS_VALUE, CROSS_OUT = range(4)


def weight(width, place):
    return pl.BlockSpec((None, width, width), lambda step: (place, 0, 0))


def project(scalars, both, theirs, gains, self_set):
    cores, half_length, width = both.shape
    length = cores * half_length
    shape = (length, width)
    return call(
        project_kernel,
        "project",
        3,
        [
            pl.BlockSpec(memory_space=pltpu.SMEM),
            whole(both.shape),
            whole(theirs.shape),
            whole(gains.shape),
            pl.BlockSpec((None, width, width), lambda step: (2 * step % 3, 0, 0)),
        ],
        [
            whole(shape),
            whole(shape),
            pl.BlockSpec((length, width), lambda step: (0, step)),
            whole((8, width)),
        ],
        like((shape, BF16), (shape, BF16), ((length, 3 * width), BF16), ((8, width), F32)),
        [],
        6 * length * width * width,
        (scalars, both, theirs, gains, self_set),
    )


def project_cross(scalars, both, theirs, normed_cross, cross_set):
    length, width = normed_cross.shape
    keys = both.shape[0] * both.shape[1]
    return call(
        project_cross_kernel,
        "project_cross",
        3,
        [
            pl.BlockSpec(memory_space=pltpu.SMEM),
            whole(both.shape),
            whole(theirs.shape),
            whole(normed_cross.shape),
            pl.BlockSpec((None, width, width), lambda step: (step, 0, 0)),
        ],
        [
            whole((keys, width)),
            pl.BlockSpec((keys, width), lambda step: (0, step // 2)),
            whole(normed_cross.shape),
        ],
        like(((keys, width), BF16), ((keys, 2 * width), BF16), (normed_cross.shape, BF16)),
        [],
        2 * width * width * (length + 2 * keys),
        (scalars, both, theirs, normed_cross, cross_set),
    )


def self_forward(qkv, seg_row, seg_col, hidden, gain_rows, self_set):
    length, width = hidden.shape
    pairs = width // LANES
    return call(
        functools.partial(self_forward_kernel, self_blocks(length)),
        "self_forward",
        pairs,
        [
            whole(seg_row.shape),
            whole(seg_col.shape),
            whole(hidden.shape),
            whole(gain_rows.shape),
            columns(length, 0),
            columns(length, pairs),
            columns(length, 2 * pairs),
            weight(width, OUT),
        ],
        [
            whole(hidden.shape),
            whole((16, length)),
            whole(hidden.shape),
            whole(hidden.shape),
        ],
        like(
            (hidden.shape, BF16),
            ((16, length), F32),
            (hidden.shape, F32),
            (hidden.shape, BF16),
        ),
        [
            pltpu.VMEM((length, length), F32),
            pltpu.VMEM((length, LANES), F32),
            pltpu.VMEM((length, LANES), BF16),
        ],
        4 * length * width * (length + width),
        (
            seg_row,
            seg_col,
            hidden,
            gain_rows,
            qkv,
            qkv,
            qkv,
            self_set,
        ),
    )


def cross_forward(queries, ckv, count, after_self, gain_rows, cross_set):
    length, width = queries.shape
    keys = ckv.shape[0]
    pairs = width // LANES
    return call(
        functools.partial(cross_forward_kernel, cross_blocks(length, keys)),
        "cross_forward",
        pairs,
        [
            pl.BlockSpec(memory_space=pltpu.SMEM),
            whole(queries.shape),
            whole(gain_rows.shape),
            columns(length, 0),
            columns(keys, 0),
            columns(keys, pairs),
            weight(width, CROSS_OUT),
        ],
        [
            whole(queries.shape),
            whole((16, length)),
            whole(queries.shape),
            whole(queries.shape),
        ],
        like(
            (queries.shape, BF16),
            ((16, length), F32),
            (queries.shape, F32),
            (queries.shape, BF16),
        ),
        [pltpu.VMEM((length, LANES), F32), pltpu.VMEM((length, LANES), BF16)],
        2 * length * width * (2 * keys + width),
        (count, after_self, gain_rows, queries, ckv, ckv, cross_set),
    )


def feed_forward(scalars, normed, both, theirs, after_cross, gain_rows, ffn_set, w_in):
    length, width = normed.shape
    groups, steps, rows, _ = w_in.shape
    block = pl.BlockSpec((groups, 1, rows, width), lambda step: (0, step, 0, 0))
    half_rows = pl.BlockSpec((width, width // 2), lambda step: (step, 0))
    half_out = ((steps * width, width // 2), BF16)
    half_length = (length // both.shape[0], width)
    return call(
        ffn_kernel,
        "feed_forward",
        steps,
        [
            pl.BlockSpec(memory_space=pltpu.SMEM),
            whole(normed.shape),
            whole(both.shape),
            whole(theirs.shape),
            whole(normed.shape),
            whole(gain_rows.shape),
            block,
            pl.BlockSpec((width, width), lambda step: (step, 1)),
        ],
        [
            whole(half_length),
            whole(half_length),
            whole(normed.shape),
            pl.BlockSpec((width, width), lambda step: (0, step)),
            half_rows,
            half_rows,
        ],
        like(
            (half_length, BF16),
            (half_length, BF16),
            (normed.shape, F32),
            ((width, steps * width), BF16),
            half_out,
            half_out,
        ),
        [
            pltpu.VMEM(normed.shape, F32),
            pltpu.VMEM(normed.shape, F32),
            pltpu.VMEM((width, length), BF16),
            pltpu.VMEM((length, width), BF16),
        ],
        12 * length * width * width * steps,
        (scalars, normed, both, theirs, after_cross, gain_rows, w_in, ffn_set),
        grant=56,
    )


def cross_branch(d_after, cross_set):
    length, width = d_after.shape
    shape = (width // LANES, length, LANES)
    return call(
        cross_branch_kernel,
        "cross_branch",
        1,
        [whole(d_after.shape), weight(width, CROSS_OUT)],
        whole(shape),
        jax.ShapeDtypeStruct(shape, BF16),
        [],
        2 * length * width * width,
        (d_after, cross_set),
    )


def pair_block(length, first):
    return pl.BlockSpec((1, length, LANES), lambda step: (first + step, 0, 0))


def cross_backward(
    scalars,
    queries,
    ckv,
    d_att,
    lse,
    d_after_cross,
    after_self,
    normed_cross,
    cross_attended,
    self_attended,
    encoded,
    gain_rows,
    cross_set,
    self_set,
):
    length, width = queries.shape
    keys = ckv.shape[0]
    pairs = width // LANES
    halves = (width, 5 * width // 2)
    half_keys = (keys // 2, width)
    return call(
        functools.partial(cross_backward_kernel, cross_blocks(length, keys)),
        "cross_backward",
        pairs,
        [
            pl.BlockSpec(memory_space=pltpu.SMEM),
            columns(length, 0),
            columns(keys, 0),
            columns(keys, pairs),
            pair_block(length, 0),
            whole(lse.shape),
            whole(queries.shape),
            whole(queries.shape),
            whole(queries.shape),
            whole(queries.shape),
            whole(queries.shape),
            whole(encoded.shape),
            whole(gain_rows.shape),
            weight(width, CROSS_QUERY),
            weight(width, CROSS_KEY),
            weight(width, CROSS_VALUE),
            weight(width, OUT),
        ],
        [
            whole(queries.shape),
            whole((pairs, length, LANES)),
            whole(halves),
            whole(halves),
            whole(half_keys),
            whole(half_keys),
        ],
        like(
            (queries.shape, F32),
            ((pairs, length, LANES), BF16),
            (halves, BF16),
            (halves, BF16),
            (half_keys, F32),
            (half_keys, F32),
        ),
        [
            pltpu.VMEM((length, width), BF16),
            pltpu.VMEM((keys, 2 * width), BF16),
            pltpu.VMEM((keys, LANES), F32),
            pltpu.VMEM((keys, LANES), F32),
        ],
        2 * length * width * (5 * keys + 7 * width),
        (
            scalars,
            queries,
            ckv,
            ckv,
            d_att,
            lse,
            d_after_cross,
            after_self,
            normed_cross,
            cross_attended,
            self_attended,
            encoded,
            gain_rows,
            cross_set,
            cross_set,
            cross_set,
            self_set,
        ),
    )


def self_backward_first(seg_row, seg_col, qkv, d_att, lse):
    length, width = qkv.shape[0], qkv.shape[1] // 3
    pairs = width // LANES
    done = pairs // 2
    return call(
        functools.partial(self_backward_first_kernel, self_blocks(length)),
        "self_backward_first",
        done,
        [
            whole(seg_row.shape),
            whole(seg_col.shape),
            columns(length, 0),
            columns(length, pairs),
            columns(length, 2 * pairs),
            pair_block(length, 0),
            whole(lse.shape),
        ],
        whole((3, length, done * LANES)),
        jax.ShapeDtypeStruct((3, length, done * LANES), BF16),
        [
            pltpu.VMEM((length, length), F32),
            pltpu.VMEM((length, LANES), F32),
            pltpu.VMEM((length, LANES), F32),
        ],
        120 * length * width * length,
        (seg_row, seg_col, qkv, qkv, qkv, d_att, lse),
    )


def self_backward_last(scalars, seg_row, seg_col, qkv, d_att, lse, d_first, normed_self):
    length, width = normed_self.shape
    pairs = width // LANES
    done = d_first.shape[2] // LANES
    halves = (width, width // 2)
    d_last = (3, length, (pairs - done) * LANES)
    return call(
        functools.partial(self_backward_last_kernel, self_blocks(length), done),
        "self_backward_last",
        pairs - done,
        [
            pl.BlockSpec(memory_space=pltpu.SMEM),
            whole(seg_row.shape),
            whole(seg_col.shape),
            columns(length, done),
            columns(length, pairs + done),
            columns(length, 2 * pairs + done),
            pair_block(length, done),
            whole(lse.shape),
            whole(d_first.shape),
            whole(normed_self.shape),
        ],
        [whole(halves)] * 6 + [whole(d_last)],
        like(*[(halves, BF16)] * 6, (d_last, BF16)),
        [
            pltpu.VMEM((length, length), F32),
            pltpu.VMEM((length, LANES), F32),
            pltpu.VMEM((length, LANES), F32),
        ],
        2 * length * width * (length + 3 * width),
        (scalars, seg_row, seg_col, qkv, qkv, qkv, d_att, lse, d_first, normed_self),
    )


def self_input(scalars, d_first, d_last, d_after_self, hidden, gain_rows, self_set):
    length, width = hidden.shape
    half_length = (length // 2, width)
    return call(
        self_input_kernel,
        "self_input",
        1,
        [
            pl.BlockSpec(memory_space=pltpu.SMEM),
            whole(d_first.shape),
            whole(d_last.shape),
            whole(hidden.shape),
            whole(hidden.shape),
            whole(gain_rows.shape),
            weight(width, QUERY),
            weight(width, KEY),
            weight(width, VALUE),
        ],
        [whole(half_length), whole(half_length)],
        like((half_length, F32), (half_length, F32)),
        [],
        6 * length * width * width,
        (scalars, d_first, d_last, d_after_self, hidden, gain_rows)
        + (self_set, self_set, self_set),
    )


def grid_of(chips):
    side = 1
    while 2 * side**3 < chips:
        side += 1
    return (2 * side, side, side) if 2 * side**3 == chips else (1, 1, chips)


def axis_stride(grid, axis):
    stride = 1
    for extent in grid[axis + 1 :]:
        stride *= extent
    return stride


def coordinate(grid, axis):
    return lax.axis_index("dp") // axis_stride(grid, axis) % grid[axis]


def shifted(values, grid, axis, shift):
    stride, extent = axis_stride(grid, axis), grid[axis]
    chips = grid[0] * grid[1] * grid[2]
    pairs = []
    for chip in range(chips):
        at = chip // stride % extent
        pairs.append((chip, chip + ((at + shift) % extent - at) * stride))
    return lax.ppermute(values, "dp", pairs)


def swapped(values):
    cores = lax.axis_size("seq")
    return lax.ppermute(values, "seq", [(i, (i + 1) % cores) for i in range(cores)])


def total(parts):
    result = parts[0].astype(F32)
    for part in parts[1:]:
        result = result + part.astype(F32)
    return result


def pieces_kernel(plan, *refs):
    outputs = refs[len(refs) - len(plan) :]
    at = 1
    for output, sources in zip(outputs, plan):
        for start, end, count in sources:
            value = total([refs[at + i][:, 0] for i in range(count)])
            output[:, :, :, start:end] = value.astype(BF16)
            at += count


def pieces(groups):
    outers = []
    for sources, dim, _, _ in groups:
        outer = 1
        for n in sources[0][0][0].shape[:dim]:
            outer *= n
        outers.append(outer)
    steps = 1 if any(outer % 2 for outer in outers) else 2
    plan, args, in_specs, out_specs, out_shape, finals, all_places = [], [], [], [], [], [], []
    size = 0
    for (sources, dim, places, (share, shares)), outer in zip(groups, outers):
        shape = sources[0][0][0].shape
        before, extent, after = shape[:dim], shape[dim], shape[dim + 1 : -2]
        rows = shape[-2] // shares
        inner = 1
        for n in after:
            inner *= n
        lead = outer // steps
        for place in places:
            width, spans = 0, []
            for parts, columns_, block in sources:
                spans.append((width, width + columns_, len(parts)))
                width += columns_
                for part in parts:
                    args.append(part.reshape(outer, extent, inner, *part.shape[-2:]))
                    in_specs.append(
                        pl.BlockSpec(
                            (lead, 1, inner, rows, columns_),
                            lambda g, at, o=len(all_places), share=share, block=block: (
                                g,
                                at[o],
                                0,
                                share,
                                block,
                            ),
                        )
                    )
                    size += outer * inner * rows * columns_
            plan.append(spans)
            all_places.append(place)
            out_specs.append(
                pl.BlockSpec((lead, inner, rows, width), lambda g, at: (g, 0, 0, 0))
            )
            out_shape.append(jax.ShapeDtypeStruct((outer, inner, rows, width), BF16))
            finals.append(before + after + (rows, width))
            size += outer * inner * rows * width
    result = pl.pallas_call(
        functools.partial(pieces_kernel, plan),
        grid_spec=pltpu.PrefetchScalarGridSpec(
            num_scalar_prefetch=1, grid=(steps,), in_specs=in_specs, out_specs=out_specs
        ),
        out_shape=out_shape,
        compiler_params=pltpu.CompilerParams(
            dimension_semantics=("arbitrary",), vmem_limit_bytes=max(16 << 20, 6 * size)
        ),
        cost_estimate=pl.CostEstimate(flops=0, bytes_accessed=2 * size, transcendentals=0),
        name="pieces",
    )(jnp.stack(all_places).astype(jnp.int32), *args)
    return [r.reshape(final) for r, final in zip(result, finals)]


def scattered(grid, *groups):
    wanted = []
    for sources, axis, dim, share in groups:
        here, extent = coordinate(grid, axis), grid[axis]
        wanted.append((sources, dim, [(here + shift) % extent for shift in range(extent)], share))
    taken = pieces(wanted)
    results = []
    for _, axis, _, _ in groups:
        own, *others = taken[: grid[axis]]
        taken = taken[grid[axis] :]
        results.append(
            [own]
            + [shifted(other, grid, axis, shift) for shift, other in enumerate(others, start=1)]
        )
    return results


def assemble_kernel(count, chips, *refs):
    inputs, (weights, gains) = refs[: 2 * 2 * count], refs[2 * 2 * count :]
    core = chips[chips.shape[0] - 1]
    width = weights.shape[-1]
    for which in range(2):
        place = core if which == 0 else 1 - core
        at = 0
        for number in range(2 * count):
            source = inputs[which * 2 * count + number]
            second = number >= count
            for i in range(source.shape[0]):
                for k in range(source.shape[1]):
                    chip = chips[at]
                    at += 1
                    if second:
                        weights[2 + place, chip] = source[i, k, :, :width]
                        if which == 0 and gains is not None:
                            gains[chip] = source[i, k, :, width:]
                    else:
                        weights[place, chip] = source[i, k]


def along(values, grid, axis):
    return [values] + [shifted(values, grid, axis, shift) for shift in range(1, grid[axis])]


def gather_z(matrices, grid):
    every = along(jnp.concatenate(matrices, axis=1), grid, 0)
    stacked, at = [], 0
    for matrix in matrices:
        end = at + matrix.shape[1]
        stacked.append(jnp.stack([values[:, at:end] for values in every]))
        at = end
    return stacked


def gather_near(first, second, grid):
    return jnp.stack(along(first, grid, 1)), jnp.stack(along(second, grid, 2))


def gather_far(first, second, grid):
    return along(first, grid, 2), along(second, grid, 1)


def gather_end(mine, other, grid):
    first_sets, second_sets = mine
    mine, other = first_sets + second_sets, other[0] + other[1]
    rows, width = first_sets[0].shape[-2:]
    chips = grid[0] * grid[1] * grid[2]
    here = [coordinate(grid, axis) for axis in range(3)]
    places = []
    for outer, inner in ((2, 1), (1, 2)):
        for far in range(grid[outer]):
            for near in range(grid[inner]):
                for deep in range(grid[0]):
                    at = [None, None, None]
                    at[outer] = (here[outer] - far) % grid[outer]
                    at[inner] = (here[inner] - near) % grid[inner]
                    at[0] = (here[0] - deep) % grid[0]
                    places.append((at[0] * grid[1] + at[1]) * grid[2] + at[2])
    places.append(lax.axis_index("seq"))
    assert len(first_sets) == len(second_sets)
    extra = second_sets[0].shape[-1] - width
    out_shape = [pltpu.HBM((4, chips, rows, width), BF16)]
    if extra:
        out_shape.append(pltpu.HBM((chips, rows, extra), BF16))
    in_vmem = pl.BlockSpec(memory_space=pltpu.VMEM)

    def kernel(places, *refs):
        assemble_kernel(len(first_sets), places, *(refs if extra else refs + (None,)))

    result = pl.pallas_call(
        kernel,
        in_specs=[pl.BlockSpec(memory_space=pltpu.SMEM)] + [in_vmem] * (2 * len(mine)),
        out_specs=[in_vmem] * len(out_shape),
        out_shape=out_shape,
        compiler_params=pltpu.CompilerParams(vmem_limit_bytes=48 << 20),
        cost_estimate=pl.CostEstimate(
            flops=0, bytes_accessed=16 * chips * rows * width, transcendentals=0
        ),
        name="assemble",
    )(jnp.stack(places).astype(jnp.int32), *mine, *other)
    weights = result[0].reshape(4, chips * rows, width)
    return weights, result[1].reshape(chips * rows, extra) if extra else None


def on_device(
    hidden_in,
    encoder_out,
    segment_ids,
    passage_counts,
    cotangent,
    w_query,
    w_key,
    w_value,
    w_out,
    w_cross_query,
    w_cross_key,
    w_cross_value,
    w_cross_out,
    w_ffn_in,
    w_ffn_out,
    gain_self,
    gain_cross,
    gain_ffn,
):
    cores = lax.axis_size("seq")
    core = lax.axis_index("seq")
    chips = lax.axis_size("dp")
    grid = grid_of(chips)
    width = hidden_in.shape[-1]
    half = width // 2
    ratio = w_ffn_in.shape[1] // width
    rows = w_query.shape[0]
    joint = ("dp", "seq")

    def own_rows(values):
        part = values.shape[0] // cores
        return lax.dynamic_slice_in_dim(values, core * part, part, 0)

    def in_order(mine, other, axis):
        first = jnp.where(core == 0, mine, other)
        second = jnp.where(core == 0, other, mine)
        return jnp.concatenate([first, second], axis=axis)

    ffn_in_rows = jnp.concatenate(
        [w_ffn_in[:, i * width : (i + 1) * width] for i in range(ratio)], axis=0
    )
    ffn_rows = own_rows(jnp.concatenate([ffn_in_rows, w_ffn_out], axis=1))
    gains = jnp.stack([gain_self, gain_cross, gain_ffn], axis=1)
    gains = jnp.pad(gains, ((0, 0), (0, LANES - gains.shape[1])))

    def by_core(here, there):
        return jnp.where(core == 0, here, there)

    def tied(value, others):
        return lax.optimization_barrier((value, others))

    def sent(values):
        return swapped(lax.dynamic_index_in_dim(values, 1 - core, 0, keepdims=False))

    def returned(mine, theirs):
        return in_order(mine[None, None], theirs[None, None], 0)

    def exchanged(sets):
        return tuple([swapped(values) for values in one] for one in sets)

    hidden_both, encoded_both, branch_both = hidden_in[:, 0], encoder_out[:, 0], cotangent[:, 0]
    hidden_theirs, encoded_theirs, branch_theirs = (
        sent(hidden_both),
        sent(encoded_both),
        sent(branch_both),
    )
    segments = in_order(
        lax.dynamic_index_in_dim(segment_ids[:, 0], core, 0, keepdims=False),
        sent(segment_ids[:, 0]),
        0,
    )
    count = lax.dynamic_index_in_dim(passage_counts[:, 0], core, 0, keepdims=False)
    scalars = jnp.stack([count, core.astype(jnp.int32)])
    seg_row = segments[None, :]
    seg_col = segments[:, None]

    stacked = gather_z(
        [
            by_core(w_query, w_value),
            jnp.concatenate([by_core(w_key, w_out), gains], axis=1),
            by_core(w_cross_key, w_cross_query),
            by_core(w_cross_value, w_cross_out),
        ],
        grid,
    )
    self_rows, cross_rows = stacked[:2], stacked[2:]
    ffn_rows, self_rows = tied(ffn_rows, self_rows)
    ffn_set = lax.all_gather(ffn_rows, joint, axis=0, tiled=True)
    self_rows = gather_near(*self_rows, grid)
    self_near = [[values] for values in self_rows]
    self_far = [values[1:] for values in gather_far(*self_rows, grid)]
    self_other = exchanged(self_near)
    self_far, _ = tied(self_far, (self_other, scalars, seg_row, seg_col, hidden_theirs))
    cross_rows, self_far = tied(cross_rows, self_far)
    self_set, gains = gather_end(
        [near + far for near, far in zip(self_near, self_far)],
        [near + far for near, far in zip(self_other, exchanged(self_far))],
        grid,
    )
    cross_rows = along(cross_rows[0], grid, 1), along(cross_rows[1], grid, 2)

    w_in = ffn_set.reshape(chips, ratio, rows, 2 * width)
    if rows % 16:
        w_in = w_in[:, :, :, :width].transpose(1, 0, 2, 3).reshape(1, ratio, width, width)

    hidden, normed_self, qkv, gain_rows = project(
        scalars, hidden_both, hidden_theirs, gains, self_set
    )
    cross_rows, qkv = tied(cross_rows, qkv)
    cross_rows = [jnp.stack(values) for values in cross_rows]
    cross_near = [[values] for values in cross_rows]
    cross_far = [values[1:] for values in gather_far(*cross_rows, grid)]
    cross_other = exchanged(cross_near)
    qkv, (cross_near, cross_other) = tied(qkv, (cross_near, cross_other))
    attended, self_lse, after_self, normed_cross = self_forward(
        qkv, seg_row, seg_col, hidden, gain_rows, self_set
    )
    normed_cross, cross_far = tied(normed_cross, cross_far)
    cross_set, _ = gather_end(
        [near + far for near, far in zip(cross_near, cross_far)],
        [near + far for near, far in zip(cross_other, exchanged(cross_far))],
        grid,
    )
    encoded, ckv, cross_queries = project_cross(
        scalars, encoded_both, encoded_theirs, normed_cross, cross_set
    )
    cross_attended, cross_lse, after_cross, normed_ffn = cross_forward(
        cross_queries, ckv, scalars, after_self, gain_rows, cross_set
    )
    out_mine, out_theirs, d_after_cross, grad_in, kept_out, sent_out = feed_forward(
        scalars, normed_ffn, branch_both, branch_theirs, after_cross, gain_rows, ffn_set, w_in
    )
    grad_in = lax.psum_scatter(grad_in, joint, scatter_dimension=0, tiled=True)

    def by_chip(values):
        return values.reshape(grid + (-1, values.shape[-1]))

    def pair_parts(kept, sent):
        return [by_chip(kept), by_chip(swapped(sent))]

    def whole_source(parts):
        return (parts, parts[0].shape[-1], 0)

    every = (0, 1)

    def along_first(first, second, first_share=every, second_share=every):
        return scattered(grid, (first, 2, 2, first_share), (second, 1, 1, second_share))

    def along_second(first, second):
        return scattered(
            grid, ([whole_source(first)], 1, 1, every), ([whole_source(second)], 2, 1, every)
        )

    def along_z(first, second):
        return scattered(grid, ([whole_source(first), whole_source(second)], 0, 0, every))[0]

    ffn_out = pair_parts(kept_out, sent_out)
    d_att = cross_branch(d_after_cross, cross_set)
    d_att, ffn_out = tied(d_att, ffn_out)
    by_rows = ratio * rows // 2 % 16 == 0
    if by_rows:
        ffn_first, ffn_second = along_first(
            [(ffn_out, half, 0)], [(ffn_out, half, 0)], (0, 2), (1, 2)
        )
    else:
        ffn_first, ffn_second = along_first(
            [(ffn_out, 2 * LANES, 0)], [(ffn_out, half - 2 * LANES, 2)]
        )
    d_att, _ = tied(d_att, (ffn_first[0], ffn_second[0]))
    d_after_self, d_att, kept_c, sent_c, encoded_mine, encoded_their = cross_backward(
        scalars,
        cross_queries,
        ckv,
        d_att,
        cross_lse,
        d_after_cross,
        after_self,
        normed_cross,
        cross_attended,
        attended,
        encoded,
        gain_rows,
        cross_set,
        self_set,
    )
    d_att, (ffn_first, ffn_second) = tied(d_att, (ffn_first, ffn_second))
    ffn_first, ffn_second = along_second(ffn_first, ffn_second)
    d_att, _ = tied(d_att, (ffn_first[0], ffn_second[0]))
    cross_all = pair_parts(kept_c, sent_c)
    d_first = self_backward_first(seg_row, seg_col, qkv, d_att, self_lse)
    out_theirs, encoded_their = swapped(out_theirs), swapped(encoded_their)
    d_first, (ffn_first, ffn_second, cross_all, out_theirs, encoded_their) = tied(
        d_first, (ffn_first, ffn_second, cross_all, out_theirs, encoded_their)
    )
    cross_first, cross_second = along_first(
        [(cross_all, half, 3), (cross_all, half, 0), (cross_all, half, 4)],
        [(cross_all, half, 1), (cross_all, half, 2)],
    )
    ffn_parts = along_z(ffn_first, ffn_second)
    d_first, _ = tied(d_first, (ffn_parts[0], cross_first[0], cross_second[0]))
    *self_grads, d_last = self_backward_last(
        scalars, seg_row, seg_col, qkv, d_att, self_lse, d_first, normed_self
    )
    self_grads, ffn_parts = tied(self_grads, ffn_parts)
    self_qkv = [pair_parts(self_grads[i], self_grads[3 + i]) for i in range(3)]
    d_last, (cross_first, cross_second) = tied(d_last, (cross_first, cross_second))
    cross_first, cross_second = along_second(cross_first, cross_second)
    self_qkv, _ = tied(self_qkv, (cross_first[0], cross_second[0]))
    self_first, self_second = along_first(
        [(self_qkv[0], half, 0), (self_qkv[2], 2 * LANES, 0)],
        [(self_qkv[1], half, 0), (self_qkv[2], half - 2 * LANES, 2)],
    )
    d_last, _ = tied(d_last, (self_first[0], self_second[0]))
    hidden_mine, hidden_their = self_input(
        scalars, d_first, d_last, d_after_self, hidden, gain_rows, self_set
    )
    def matrices(mine, places):
        other = swapped(mine)
        results = []
        for spans in places:
            halves = [
                jnp.concatenate([values[:, start:end] for start, end in spans], axis=1)
                for values in (mine, other)
            ]
            results.append(in_order(*halves, 1))
        return results

    def gain_gradient(gain, *pairs):
        weighed = [weight_rows.astype(F32) * grad for weight_rows, grad in pairs]
        return jnp.sum(total(weighed), axis=1) / gain.astype(F32)

    hidden_their, (self_first, self_second, cross_first, cross_second) = tied(
        hidden_their, (self_first, self_second, cross_first, cross_second)
    )
    ffn_sum = total(ffn_parts)
    if by_rows:
        ffn_sum = jnp.concatenate([ffn_sum[:, :half], ffn_sum[:, half:]], axis=0)
    (grad_ffn_out,) = matrices(ffn_sum, [[(0, half)]])
    (cross_first, cross_second), grad_ffn_out = tied((cross_first, cross_second), grad_ffn_out)
    cross_parts = along_z(cross_first, cross_second)
    (self_first, self_second), _ = tied((self_first, self_second), cross_parts[0])
    self_first, self_second = along_second(self_first, self_second)
    (cross_parts, hidden_their, grad_in), _ = tied(
        (cross_parts, hidden_their, grad_in), (self_first[0], self_second[0])
    )
    self_parts = along_z(self_first, self_second)
    cross_grads = matrices(total(cross_parts), [[(i * half, (i + 1) * half)] for i in range(5)])
    grad_co, grad_cq, grad_o, grad_ck, grad_cv = cross_grads
    grad_in = lax.all_gather(grad_in, "seq", axis=0, tiled=True).astype(F32)
    done = (
        returned(out_mine, out_theirs),
        returned(hidden_mine, swapped(hidden_their)),
        returned(encoded_mine, encoded_their),
        gain_gradient(gain_cross, (w_cross_query, grad_cq)),
        gain_gradient(gain_ffn, (w_ffn_in, grad_in)),
    )
    self_parts, (done, cross_grads, grad_in) = tied(self_parts, (done, cross_grads, grad_in))
    grad_co, grad_cq, grad_o, grad_ck, grad_cv = cross_grads
    split = half + 2 * LANES
    grad_q, grad_k, grad_v = matrices(
        total(self_parts),
        [
            [(0, half)],
            [(split, split + half)],
            [(half, split), (split + half, 3 * half)],
        ],
    )
    return done[:3] + (
        grad_q,
        grad_k,
        grad_v,
        grad_o,
        grad_cq,
        grad_ck,
        grad_cv,
        grad_co,
        grad_in,
        grad_ffn_out,
        gain_gradient(gain_self, (w_query, grad_q), (w_key, grad_k), (w_value, grad_v)),
    ) + done[3:]


def solution(mesh):
    tokens = P(None, "dp", "seq", None)
    rows = P("dp", None)
    gain = P("dp")
    return jax.shard_map(
        on_device,
        mesh=mesh,
        in_specs=(tokens, tokens, P(None, "dp", "seq"), P(None, "dp"), tokens)
        + (rows,) * 10
        + (gain,) * 3,
        out_specs=(tokens,) * 3 + (rows,) * 10 + (gain,) * 3,
        check_vma=False,
    )
```

```python
import functools

import jax
import jax.numpy as jnp
from jax import lax
from jax.experimental import pallas as pl
from jax.experimental.pallas import tpu as pltpu
from jax.sharding import PartitionSpec as P

HEAD_DIM = 64
LANES = 128
SEGMENT_LIMIT = 384
SELF_BLOCK = 256
CROSS_BLOCK = 768
EPS = 1e-06
NEG = -1e30
GELU_RATE = 0.7978845608
GELU_CUBIC = 0.044715
BF16 = jnp.bfloat16
F32 = jnp.float32


def product(left, right):
    return jnp.dot(left, right, preferred_element_type=F32)


def row_outer(left, right):
    return lax.dot_general(left, right, (((0,), (0,)), ((), ())), preferred_element_type=F32)


def right_transposed(left, right):
    return lax.dot_general(left, right, (((1,), (1,)), ((), ())), preferred_element_type=F32)


def inverse_rms(values):
    return lax.rsqrt(jnp.mean(values * values, axis=-1, keepdims=True) + EPS)


def norm_backward(values, scale, gain, d_normed):
    scaled = gain * d_normed
    d_values = scale * scaled - values * (scale * scale * scale) * jnp.mean(
        values * scaled, axis=-1, keepdims=True
    )
    return d_values


def self_blocks(length):
    blocks = []
    for start in range(0, length, SELF_BLOCK):
        end = min(start + SELF_BLOCK, length)
        first = max(0, start - SEGMENT_LIMIT + 1) // LANES * LANES
        blocks.append((start, end, first, end))
    return blocks


def cross_blocks(length, keys):
    return [
        (start, min(start + CROSS_BLOCK, length), 0, keys)
        for start in range(0, length, CROSS_BLOCK)
    ]


def of_head(values, head):
    lanes = lax.broadcasted_iota(jnp.int32, values.shape, 1)
    return jnp.where(lanes // HEAD_DIM == head, values, jnp.zeros_like(values))


def ahead(first_step, items):
    coming = first_step(*items[0])
    for at, item in enumerate(items):
        result = coming
        if at + 1 < len(items):
            coming = first_step(*items[at + 1])
        yield item, result


def pair_forward(blocks, bias_of, q_ref, k_ref, v_ref, o_ref, lse_ref, lse_cols):
    pair = pl.program_id(0)
    lane = lax.broadcasted_iota(jnp.int32, (1, LANES), 1)

    def scores_of(block, head):
        start, end, first, last = block
        query_head = of_head(q_ref[start:end, :], head)
        return right_transposed(query_head, k_ref[first:last, :]) + bias_of(*block)

    mixed = []
    items = [(block, head) for block in blocks for head in range(2)]
    for ((start, end, first, last), head), scores in ahead(scores_of, items):
        row_max = jnp.max(scores, axis=-1, keepdims=True)
        exponents = jnp.exp(scores - row_max)
        totals = jnp.sum(exponents, axis=-1, keepdims=True)
        mixed.append(product(exponents.astype(BF16), v_ref[first:last, :]) / totals)
        lse_cols[start:end, :] = jnp.where(
            lane == 2 * pair + head, row_max + jnp.log(totals), lse_cols[start:end, :]
        )
        if head == 1:
            o_ref[start:end, :] = jnp.where(lane < HEAD_DIM, mixed[-2], mixed[-1]).astype(BF16)

    @pl.when(pair == pl.num_programs(0) - 1)
    def _():
        lse_ref[...] = jnp.transpose(lse_cols[...])[: lse_ref.shape[0], :]


def pair_backward(
    blocks, bias_of, q_ref, k_ref, v_ref, d_ref, lse_ref, dk_acc, dv_acc, first_pair=0
):
    pair = first_pair + pl.program_id(0)

    def products_of(block, head):
        start, end, first, last = block
        query_head = of_head(q_ref[start:end, :], head)
        d_head = of_head(d_ref[start:end, :], head)
        scores = right_transposed(k_ref[first:last, :], query_head)
        d_probs = right_transposed(v_ref[first:last, :], d_head)
        return query_head, d_head, scores, d_probs

    dk_acc[...] = jnp.zeros_like(dk_acc)
    dv_acc[...] = jnp.zeros_like(dv_acc)
    d_queries, rows = [], []
    items = [(block, head) for block in blocks for head in range(2)]
    for (block, head), (query_head, d_head, scores, d_probs) in ahead(products_of, items):
        start, end, first, last = block
        log_totals = lse_ref[pl.ds(2 * pair + head, 1), start:end]
        exact = jnp.exp(scores + (bias_of(*block) - log_totals))
        inner = jnp.sum(exact * d_probs, axis=0, keepdims=True)
        d_scores = (exact * (d_probs - inner)).astype(BF16)
        dv_acc[first:last, :] += product(exact.astype(BF16), d_head)
        dk_acc[first:last, :] += product(d_scores, query_head)
        rows.append(row_outer(d_scores, of_head(k_ref[first:last, :], head)))
        if head == 1:
            d_queries.append((start, end, rows[-2] + rows[-1]))
    return d_queries


def store_halves(core, kept, sent, place, value):
    half = value.shape[-1] // 2
    there = slice(place, place + half)

    @pl.when(core == 0)
    def _():
        kept[..., there] = value[..., :half]
        sent[..., there] = value[..., half:]

    @pl.when(core != 0)
    def _():
        kept[..., there] = value[..., half:]
        sent[..., there] = value[..., :half]


def store_rows(core, mine, theirs, value):
    length = mine.shape[0]

    @pl.when(core == 0)
    def _():
        mine[...] = value[:length, :]
        theirs[...] = value[length:, :]

    @pl.when(core != 0)
    def _():
        mine[...] = value[length:, :]
        theirs[...] = value[:length, :]


def masked_bias(seg_col, seg_row, keys_first):
    shape = (seg_col.shape[0], seg_row.shape[1])
    rows = lax.broadcasted_iota(jnp.int32, shape, 0)
    lanes = lax.broadcasted_iota(jnp.int32, shape, 1)
    ordered = rows <= lanes if keys_first else lanes <= rows
    return jnp.where(ordered & (seg_col[...] == seg_row[...]), 0.0, NEG)


def put_together(core, both, theirs, whole_rows):
    length = theirs.shape[0]

    @pl.when(core == 0)
    def _():
        whole_rows[:length, :] = both[0]
        whole_rows[length:, :] = theirs[...]

    @pl.when(core != 0)
    def _():
        whole_rows[:length, :] = theirs[...]
        whole_rows[length:, :] = both[1]


def project_kernel(scalars, both, theirs, gains, weight, hidden, normed, qkv, gain_rows):
    @pl.when(pl.program_id(0) == 0)
    def _():
        put_together(scalars[1], both, theirs, hidden)
        rows = jnp.transpose(gains[...].astype(F32))[: gain_rows.shape[0], :]
        gain_rows[...] = rows
        values = hidden[...].astype(F32)
        normed[...] = (values * inverse_rms(values) * rows[0:1, :]).astype(BF16)

    qkv[...] = product(normed[...], weight[...]).astype(BF16)


def project_cross_kernel(
    scalars, both, theirs, normed_cross, weight, encoded, ckv, cross_queries
):
    step = pl.program_id(0)

    @pl.when(step == 0)
    def _():
        put_together(scalars[1], both, theirs, encoded)

    @pl.when(step == 1)
    def _():
        cross_queries[...] = product(normed_cross[...], weight[...]).astype(BF16)

    @pl.when(step != 1)
    def _():
        ckv[...] = product(encoded[...], weight[...]).astype(BF16)


def self_forward_kernel(
    blocks,
    seg_row,
    seg_col,
    hidden,
    gain_rows,
    q_ref,
    k_ref,
    v_ref,
    w_o,
    attended,
    lse_ref,
    after_self,
    normed_cross,
    bias,
    lse_cols,
    mixed,
):
    @pl.when(pl.program_id(0) == 0)
    def _():
        bias[...] = masked_bias(seg_col, seg_row, False)
        lse_cols[...] = jnp.zeros_like(lse_cols)

    pair_forward(
        blocks,
        lambda start, end, first, last: bias[start:end, first:last],
        q_ref,
        k_ref,
        v_ref,
        mixed,
        lse_ref,
        lse_cols,
    )
    place = pl.multiple_of(pl.program_id(0) * LANES, LANES)
    attended[:, pl.ds(place, LANES)] = mixed[...]

    @pl.when(pl.program_id(0) == pl.num_programs(0) - 1)
    def _():
        values = hidden[...].astype(F32) + product(attended[...], w_o[...])
        after_self[...] = values
        normed_cross[...] = (values * inverse_rms(values) * gain_rows[1:2, :]).astype(BF16)


def cross_forward_kernel(
    blocks,
    count,
    after_self,
    gain_rows,
    q_ref,
    k_ref,
    v_ref,
    w_co,
    attended,
    lse_ref,
    after_cross,
    normed_ffn,
    lse_cols,
    mixed,
):
    @pl.when(pl.program_id(0) == 0)
    def _():
        lse_cols[...] = jnp.zeros_like(lse_cols)

    places = lax.broadcasted_iota(jnp.int32, (1, k_ref.shape[0]), 1)
    bias = jnp.where(places < count[0], 0.0, NEG)
    pair_forward(
        blocks,
        lambda start, end, first, last: bias,
        q_ref,
        k_ref,
        v_ref,
        mixed,
        lse_ref,
        lse_cols,
    )
    place = pl.multiple_of(pl.program_id(0) * LANES, LANES)
    attended[:, pl.ds(place, LANES)] = mixed[...]

    @pl.when(pl.program_id(0) == pl.num_programs(0) - 1)
    def _():
        values = after_self[...] + product(attended[...], w_co[...])
        after_cross[...] = values
        normed_ffn[...] = (values * inverse_rms(values) * gain_rows[2:3, :]).astype(BF16)


def ffn_kernel(
    scalars,
    normed,
    both,
    theirs,
    after_cross,
    gain_rows,
    w_in,
    w_out,
    out_mine,
    out_theirs,
    d_after_cross,
    grad_in,
    kept_out,
    sent_out,
    out_acc,
    dn_acc,
    normed_t,
    branch,
):
    step = pl.program_id(0)

    @pl.when(step == 0)
    def _():
        put_together(scalars[1], both, theirs, branch)
        normed_t[...] = jnp.transpose(normed[...])
        out_acc[...] = after_cross[...]
        dn_acc[...] = jnp.zeros_like(dn_acc)

    width = normed.shape[1]
    up = w_in[...].reshape(width, -1)
    down = w_out[...]
    pre = product(normed[...], up)
    bent = jnp.tanh(GELU_RATE * (pre + GELU_CUBIC * pre * pre * pre))
    half = 0.5 * (1.0 + bent)
    hidden_act = (pre * half).astype(BF16)
    slope = half + 0.5 * pre * (1.0 - bent * bent) * GELU_RATE * (
        1.0 + 3.0 * GELU_CUBIC * pre * pre
    )
    out_acc[...] += product(hidden_act, down)
    d_pre = (right_transposed(branch[...], down) * slope).astype(BF16)
    grad_out = row_outer(hidden_act, branch[...]).astype(BF16)
    store_halves(scalars[1], kept_out, sent_out, 0, grad_out)
    grad_in[...] = product(normed_t[...], d_pre).astype(BF16)
    dn_acc[...] += right_transposed(d_pre, up)

    @pl.when(step == pl.num_programs(0) - 1)
    def _():
        store_rows(scalars[1], out_mine, out_theirs, out_acc[...].astype(BF16))
        values = after_cross[...]
        d_values = norm_backward(values, inverse_rms(values), gain_rows[2:3, :], dn_acc[...])
        d_after_cross[...] = branch[...].astype(F32) + d_values


def attended_gradient(branch, w_out, d_att):
    d_mixed = right_transposed(branch, w_out[...]).astype(BF16)
    for pair in range(d_att.shape[0]):
        d_att[pair] = d_mixed[:, pair * LANES : (pair + 1) * LANES]


def cross_branch_kernel(d_after, w_out, d_att):
    attended_gradient(d_after[...].astype(BF16), w_out, d_att)


def cross_backward_kernel(
    blocks,
    scalars,
    q_ref,
    k_ref,
    v_ref,
    d_att,
    lse_ref,
    d_after_cross,
    after_self,
    normed_cross,
    cross_attended,
    self_attended,
    encoded,
    gain_rows,
    w_cq,
    w_ck,
    w_cv,
    w_o,
    d_after_self,
    d_att_self,
    kept,
    sent,
    encoded_mine,
    encoded_theirs,
    dq_all,
    dkv_all,
    dk_acc,
    dv_acc,
):
    step = pl.program_id(0)
    width = d_after_cross.shape[1]
    half = width // 2
    places = lax.broadcasted_iota(jnp.int32, (k_ref.shape[0], 1), 0)
    bias = jnp.where(places < scalars[0], 0.0, NEG)
    d_queries = pair_backward(
        blocks,
        lambda start, end, first, last: bias,
        q_ref,
        k_ref,
        v_ref,
        d_att.at[0],
        lse_ref,
        dk_acc,
        dv_acc,
    )
    place = pl.multiple_of(step * LANES, LANES)
    for start, end, d_query in d_queries:
        dq_all[start:end, pl.ds(place, LANES)] = d_query.astype(BF16)
    dkv_all[:, pl.ds(place, LANES)] = dk_acc[...].astype(BF16)
    dkv_all[:, pl.ds(width + place, LANES)] = dv_acc[...].astype(BF16)

    @pl.when(step == pl.num_programs(0) - 1)
    def _():
        dq = dq_all[...]
        grad_query = row_outer(normed_cross[...], dq).astype(BF16)
        grad_kv = row_outer(encoded[...], dkv_all[...]).astype(BF16)
        store_halves(scalars[1], kept, sent, 0, grad_query)
        store_halves(scalars[1], kept, sent, half, grad_kv[:, :width])
        store_halves(scalars[1], kept, sent, 2 * half, grad_kv[:, width:])
        grad_out = row_outer(cross_attended[...], d_after_cross[...].astype(BF16))
        store_halves(scalars[1], kept, sent, 3 * half, grad_out.astype(BF16))
        grad_encoded = right_transposed(dkv_all[:, :width], w_ck[...]) + right_transposed(
            dkv_all[:, width:], w_cv[...]
        )
        store_rows(scalars[1], encoded_mine, encoded_theirs, grad_encoded)
        values = after_self[...]
        d_values = norm_backward(
            values,
            inverse_rms(values),
            gain_rows[1:2, :],
            right_transposed(dq, w_cq[...]),
        )
        d_values = d_after_cross[...] + d_values
        d_after_self[...] = d_values
        branch = d_values.astype(BF16)
        attended_gradient(branch, w_o, d_att_self)
        grad_out = row_outer(self_attended[...], branch)
        store_halves(scalars[1], kept, sent, 4 * half, grad_out.astype(BF16))


def self_backward_pairs(
    blocks, seg_row, seg_col, q_ref, k_ref, v_ref, d_att, lse_ref, d_all, bias, dk_acc, dv_acc, first
):
    @pl.when(pl.program_id(0) == 0)
    def _():
        bias[...] = masked_bias(seg_col, seg_row, True)

    d_queries = pair_backward(
        blocks,
        lambda start, end, first_key, last_key: bias[first_key:last_key, start:end],
        q_ref,
        k_ref,
        v_ref,
        d_att.at[0],
        lse_ref,
        dk_acc,
        dv_acc,
        first,
    )
    place = pl.multiple_of(pl.program_id(0) * LANES, LANES)
    for start, end, d_query in d_queries:
        d_all[0, start:end, pl.ds(place, LANES)] = d_query.astype(BF16)
    d_all[1, :, pl.ds(place, LANES)] = dk_acc[...].astype(BF16)
    d_all[2, :, pl.ds(place, LANES)] = dv_acc[...].astype(BF16)


def self_backward_first_kernel(
    blocks, seg_row, seg_col, q_ref, k_ref, v_ref, d_att, lse_ref, d_all, bias, dk_acc, dv_acc
):
    self_backward_pairs(
        blocks, seg_row, seg_col, q_ref, k_ref, v_ref, d_att, lse_ref, d_all, bias, dk_acc, dv_acc, 0
    )


def self_backward_last_kernel(
    blocks,
    first,
    scalars,
    seg_row,
    seg_col,
    q_ref,
    k_ref,
    v_ref,
    d_att,
    lse_ref,
    d_first,
    normed_self,
    kept_q,
    kept_k,
    kept_v,
    sent_q,
    sent_k,
    sent_v,
    d_last,
    bias,
    dk_acc,
    dv_acc,
):
    self_backward_pairs(
        blocks,
        seg_row,
        seg_col,
        q_ref,
        k_ref,
        v_ref,
        d_att,
        lse_ref,
        d_last,
        bias,
        dk_acc,
        dv_acc,
        first,
    )

    @pl.when(pl.program_id(0) == pl.num_programs(0) - 1)
    def _():
        normed_t = jnp.transpose(normed_self[...])
        for i, (kept, sent) in enumerate(
            ((kept_q, sent_q), (kept_k, sent_k), (kept_v, sent_v))
        ):
            grad = product(normed_t, jnp.concatenate([d_first[i], d_last[i]], axis=1))
            store_halves(scalars[1], kept, sent, 0, grad.astype(BF16))


def self_input_kernel(
    scalars, d_first, d_last, d_after_self, hidden, gain_rows, w_q, w_k, w_v, mine, theirs
):
    d_normed = None
    for i, weight_ref in enumerate((w_q, w_k, w_v)):
        d_out = jnp.concatenate([d_first[i], d_last[i]], axis=1)
        part = right_transposed(d_out, weight_ref[...])
        d_normed = part if d_normed is None else d_normed + part
    values = hidden[...].astype(F32)
    d_values = norm_backward(values, inverse_rms(values), gain_rows[0:1, :], d_normed)
    store_rows(scalars[1], mine, theirs, d_after_self[...] + d_values)


def columns(rows, offset):
    return pl.BlockSpec((rows, LANES), lambda step: (0, offset + step))


def whole(shape, place=None):
    place = (0,) * len(shape) if place is None else place
    return pl.BlockSpec(shape, lambda step: place)


def like(*shapes):
    return [jax.ShapeDtypeStruct(shape, dtype) for shape, dtype in shapes]


def call(kernel, name, steps, in_specs, out_specs, out_shape, scratch, flops, args, grant=56):
    size = sum(int(a.size) * a.dtype.itemsize for a in args)
    return pl.pallas_call(
        kernel,
        grid=(steps,),
        in_specs=in_specs,
        out_specs=out_specs,
        out_shape=out_shape,
        scratch_shapes=scratch,
        compiler_params=pltpu.CompilerParams(
            dimension_semantics=("arbitrary",), vmem_limit_bytes=grant << 20
        ),
        cost_estimate=pl.CostEstimate(flops=flops, bytes_accessed=size, transcendentals=0),
        name=name,
    )(*args)


QUERY, VALUE, KEY, OUT = range(4)
CROSS_KEY, CROSS_QUERY, CROSS_VALUE, CROSS_OUT = range(4)


def weight(width, place):
    return pl.BlockSpec((None, width, width), lambda step: (place, 0, 0))


def project(scalars, both, theirs, gains, self_set):
    cores, half_length, width = both.shape
    length = cores * half_length
    shape = (length, width)
    return call(
        project_kernel,
        "project",
        3,
        [
            pl.BlockSpec(memory_space=pltpu.SMEM),
            whole(both.shape),
            whole(theirs.shape),
            whole(gains.shape),
            pl.BlockSpec((None, width, width), lambda step: (2 * step % 3, 0, 0)),
        ],
        [
            whole(shape),
            whole(shape),
            pl.BlockSpec((length, width), lambda step: (0, step)),
            whole((8, width)),
        ],
        like((shape, BF16), (shape, BF16), ((length, 3 * width), BF16), ((8, width), F32)),
        [],
        6 * length * width * width,
        (scalars, both, theirs, gains, self_set),
    )


def project_cross(scalars, both, theirs, normed_cross, cross_set):
    length, width = normed_cross.shape
    keys = both.shape[0] * both.shape[1]
    return call(
        project_cross_kernel,
        "project_cross",
        3,
        [
            pl.BlockSpec(memory_space=pltpu.SMEM),
            whole(both.shape),
            whole(theirs.shape),
            whole(normed_cross.shape),
            pl.BlockSpec((None, width, width), lambda step: (step, 0, 0)),
        ],
        [
            whole((keys, width)),
            pl.BlockSpec((keys, width), lambda step: (0, step // 2)),
            whole(normed_cross.shape),
        ],
        like(((keys, width), BF16), ((keys, 2 * width), BF16), (normed_cross.shape, BF16)),
        [],
        2 * width * width * (length + 2 * keys),
        (scalars, both, theirs, normed_cross, cross_set),
    )


def self_forward(qkv, seg_row, seg_col, hidden, gain_rows, self_set):
    length, width = hidden.shape
    pairs = width // LANES
    return call(
        functools.partial(self_forward_kernel, self_blocks(length)),
        "self_forward",
        pairs,
        [
            whole(seg_row.shape),
            whole(seg_col.shape),
            whole(hidden.shape),
            whole(gain_rows.shape),
            columns(length, 0),
            columns(length, pairs),
            columns(length, 2 * pairs),
            weight(width, OUT),
        ],
        [
            whole(hidden.shape),
            whole((16, length)),
            whole(hidden.shape),
            whole(hidden.shape),
        ],
        like(
            (hidden.shape, BF16),
            ((16, length), F32),
            (hidden.shape, F32),
            (hidden.shape, BF16),
        ),
        [
            pltpu.VMEM((length, length), F32),
            pltpu.VMEM((length, LANES), F32),
            pltpu.VMEM((length, LANES), BF16),
        ],
        4 * length * width * (length + width),
        (
            seg_row,
            seg_col,
            hidden,
            gain_rows,
            qkv,
            qkv,
            qkv,
            self_set,
        ),
    )


def cross_forward(queries, ckv, count, after_self, gain_rows, cross_set):
    length, width = queries.shape
    keys = ckv.shape[0]
    pairs = width // LANES
    return call(
        functools.partial(cross_forward_kernel, cross_blocks(length, keys)),
        "cross_forward",
        pairs,
        [
            pl.BlockSpec(memory_space=pltpu.SMEM),
            whole(queries.shape),
            whole(gain_rows.shape),
            columns(length, 0),
            columns(keys, 0),
            columns(keys, pairs),
            weight(width, CROSS_OUT),
        ],
        [
            whole(queries.shape),
            whole((16, length)),
            whole(queries.shape),
            whole(queries.shape),
        ],
        like(
            (queries.shape, BF16),
            ((16, length), F32),
            (queries.shape, F32),
            (queries.shape, BF16),
        ),
        [pltpu.VMEM((length, LANES), F32), pltpu.VMEM((length, LANES), BF16)],
        2 * length * width * (2 * keys + width),
        (count, after_self, gain_rows, queries, ckv, ckv, cross_set),
    )


def feed_forward(scalars, normed, both, theirs, after_cross, gain_rows, ffn_set, w_in):
    length, width = normed.shape
    groups, steps, rows, _ = w_in.shape
    block = pl.BlockSpec((groups, 1, rows, width), lambda step: (0, step, 0, 0))
    half_rows = pl.BlockSpec((width, width // 2), lambda step: (step, 0))
    half_out = ((steps * width, width // 2), BF16)
    half_length = (length // both.shape[0], width)
    return call(
        ffn_kernel,
        "feed_forward",
        steps,
        [
            pl.BlockSpec(memory_space=pltpu.SMEM),
            whole(normed.shape),
            whole(both.shape),
            whole(theirs.shape),
            whole(normed.shape),
            whole(gain_rows.shape),
            block,
            pl.BlockSpec((width, width), lambda step: (step, 1)),
        ],
        [
            whole(half_length),
            whole(half_length),
            whole(normed.shape),
            pl.BlockSpec((width, width), lambda step: (0, step)),
            half_rows,
            half_rows,
        ],
        like(
            (half_length, BF16),
            (half_length, BF16),
            (normed.shape, F32),
            ((width, steps * width), BF16),
            half_out,
            half_out,
        ),
        [
            pltpu.VMEM(normed.shape, F32),
            pltpu.VMEM(normed.shape, F32),
            pltpu.VMEM((width, length), BF16),
            pltpu.VMEM((length, width), BF16),
        ],
        12 * length * width * width * steps,
        (scalars, normed, both, theirs, after_cross, gain_rows, w_in, ffn_set),
        grant=56,
    )


def cross_branch(d_after, cross_set):
    length, width = d_after.shape
    shape = (width // LANES, length, LANES)
    return call(
        cross_branch_kernel,
        "cross_branch",
        1,
        [whole(d_after.shape), weight(width, CROSS_OUT)],
        whole(shape),
        jax.ShapeDtypeStruct(shape, BF16),
        [],
        2 * length * width * width,
        (d_after, cross_set),
    )


def pair_block(length, first):
    return pl.BlockSpec((1, length, LANES), lambda step: (first + step, 0, 0))


def cross_backward(
    scalars,
    queries,
    ckv,
    d_att,
    lse,
    d_after_cross,
    after_self,
    normed_cross,
    cross_attended,
    self_attended,
    encoded,
    gain_rows,
    cross_set,
    self_set,
):
    length, width = queries.shape
    keys = ckv.shape[0]
    pairs = width // LANES
    halves = (width, 5 * width // 2)
    half_keys = (keys // 2, width)
    return call(
        functools.partial(cross_backward_kernel, cross_blocks(length, keys)),
        "cross_backward",
        pairs,
        [
            pl.BlockSpec(memory_space=pltpu.SMEM),
            columns(length, 0),
            columns(keys, 0),
            columns(keys, pairs),
            pair_block(length, 0),
            whole(lse.shape),
            whole(queries.shape),
            whole(queries.shape),
            whole(queries.shape),
            whole(queries.shape),
            whole(queries.shape),
            whole(encoded.shape),
            whole(gain_rows.shape),
            weight(width, CROSS_QUERY),
            weight(width, CROSS_KEY),
            weight(width, CROSS_VALUE),
            weight(width, OUT),
        ],
        [
            whole(queries.shape),
            whole((pairs, length, LANES)),
            whole(halves),
            whole(halves),
            whole(half_keys),
            whole(half_keys),
        ],
        like(
            (queries.shape, F32),
            ((pairs, length, LANES), BF16),
            (halves, BF16),
            (halves, BF16),
            (half_keys, F32),
            (half_keys, F32),
        ),
        [
            pltpu.VMEM((length, width), BF16),
            pltpu.VMEM((keys, 2 * width), BF16),
            pltpu.VMEM((keys, LANES), F32),
            pltpu.VMEM((keys, LANES), F32),
        ],
        2 * length * width * (5 * keys + 7 * width),
        (
            scalars,
            queries,
            ckv,
            ckv,
            d_att,
            lse,
            d_after_cross,
            after_self,
            normed_cross,
            cross_attended,
            self_attended,
            encoded,
            gain_rows,
            cross_set,
            cross_set,
            cross_set,
            self_set,
        ),
    )


def self_backward_first(seg_row, seg_col, qkv, d_att, lse):
    length, width = qkv.shape[0], qkv.shape[1] // 3
    pairs = width // LANES
    done = pairs // 2
    return call(
        functools.partial(self_backward_first_kernel, self_blocks(length)),
        "self_backward_first",
        done,
        [
            whole(seg_row.shape),
            whole(seg_col.shape),
            columns(length, 0),
            columns(length, pairs),
            columns(length, 2 * pairs),
            pair_block(length, 0),
            whole(lse.shape),
        ],
        whole((3, length, done * LANES)),
        jax.ShapeDtypeStruct((3, length, done * LANES), BF16),
        [
            pltpu.VMEM((length, length), F32),
            pltpu.VMEM((length, LANES), F32),
            pltpu.VMEM((length, LANES), F32),
        ],
        120 * length * width * length,
        (seg_row, seg_col, qkv, qkv, qkv, d_att, lse),
    )


def self_backward_last(scalars, seg_row, seg_col, qkv, d_att, lse, d_first, normed_self):
    length, width = normed_self.shape
    pairs = width // LANES
    done = d_first.shape[2] // LANES
    halves = (width, width // 2)
    d_last = (3, length, (pairs - done) * LANES)
    return call(
        functools.partial(self_backward_last_kernel, self_blocks(length), done),
        "self_backward_last",
        pairs - done,
        [
            pl.BlockSpec(memory_space=pltpu.SMEM),
            whole(seg_row.shape),
            whole(seg_col.shape),
            columns(length, done),
            columns(length, pairs + done),
            columns(length, 2 * pairs + done),
            pair_block(length, done),
            whole(lse.shape),
            whole(d_first.shape),
            whole(normed_self.shape),
        ],
        [whole(halves)] * 6 + [whole(d_last)],
        like(*[(halves, BF16)] * 6, (d_last, BF16)),
        [
            pltpu.VMEM((length, length), F32),
            pltpu.VMEM((length, LANES), F32),
            pltpu.VMEM((length, LANES), F32),
        ],
        2 * length * width * (length + 3 * width),
        (scalars, seg_row, seg_col, qkv, qkv, qkv, d_att, lse, d_first, normed_self),
    )


def self_input(scalars, d_first, d_last, d_after_self, hidden, gain_rows, self_set):
    length, width = hidden.shape
    half_length = (length // 2, width)
    return call(
        self_input_kernel,
        "self_input",
        1,
        [
            pl.BlockSpec(memory_space=pltpu.SMEM),
            whole(d_first.shape),
            whole(d_last.shape),
            whole(hidden.shape),
            whole(hidden.shape),
            whole(gain_rows.shape),
            weight(width, QUERY),
            weight(width, KEY),
            weight(width, VALUE),
        ],
        [whole(half_length), whole(half_length)],
        like((half_length, F32), (half_length, F32)),
        [],
        6 * length * width * width,
        (scalars, d_first, d_last, d_after_self, hidden, gain_rows)
        + (self_set, self_set, self_set),
    )


def grid_of(chips):
    side = 1
    while 2 * side**3 < chips:
        side += 1
    return (2 * side, side, side) if 2 * side**3 == chips else (1, 1, chips)


def axis_stride(grid, axis):
    stride = 1
    for extent in grid[axis + 1 :]:
        stride *= extent
    return stride


def coordinate(grid, axis):
    return lax.axis_index("dp") // axis_stride(grid, axis) % grid[axis]


def shifted(values, grid, axis, shift):
    stride, extent = axis_stride(grid, axis), grid[axis]
    chips = grid[0] * grid[1] * grid[2]
    pairs = []
    for chip in range(chips):
        at = chip // stride % extent
        pairs.append((chip, chip + ((at + shift) % extent - at) * stride))
    return lax.ppermute(values, "dp", pairs)


def swapped(values):
    cores = lax.axis_size("seq")
    return lax.ppermute(values, "seq", [(i, (i + 1) % cores) for i in range(cores)])


def total(parts):
    result = parts[0].astype(F32)
    for part in parts[1:]:
        result = result + part.astype(F32)
    return result


def pieces_kernel(plan, *refs):
    outputs = refs[len(refs) - len(plan) :]
    at = 1
    for output, sources in zip(outputs, plan):
        for start, end, count in sources:
            value = total([refs[at + i][:, 0] for i in range(count)])
            output[:, :, :, start:end] = value.astype(BF16)
            at += count


def pieces(groups):
    outers = []
    for sources, dim, _, _ in groups:
        outer = 1
        for n in sources[0][0][0].shape[:dim]:
            outer *= n
        outers.append(outer)
    steps = 1 if any(outer % 2 for outer in outers) else 2
    plan, args, in_specs, out_specs, out_shape, finals, all_places = [], [], [], [], [], [], []
    size = 0
    for (sources, dim, places, (share, shares)), outer in zip(groups, outers):
        shape = sources[0][0][0].shape
        before, extent, after = shape[:dim], shape[dim], shape[dim + 1 : -2]
        rows = shape[-2] // shares
        inner = 1
        for n in after:
            inner *= n
        lead = outer // steps
        for place in places:
            width, spans = 0, []
            for parts, columns_, block in sources:
                spans.append((width, width + columns_, len(parts)))
                width += columns_
                for part in parts:
                    args.append(part.reshape(outer, extent, inner, *part.shape[-2:]))
                    in_specs.append(
                        pl.BlockSpec(
                            (lead, 1, inner, rows, columns_),
                            lambda g, at, o=len(all_places), share=share, block=block: (
                                g,
                                at[o],
                                0,
                                share,
                                block,
                            ),
                        )
                    )
                    size += outer * inner * rows * columns_
            plan.append(spans)
            all_places.append(place)
            out_specs.append(
                pl.BlockSpec((lead, inner, rows, width), lambda g, at: (g, 0, 0, 0))
            )
            out_shape.append(jax.ShapeDtypeStruct((outer, inner, rows, width), BF16))
            finals.append(before + after + (rows, width))
            size += outer * inner * rows * width
    result = pl.pallas_call(
        functools.partial(pieces_kernel, plan),
        grid_spec=pltpu.PrefetchScalarGridSpec(
            num_scalar_prefetch=1, grid=(steps,), in_specs=in_specs, out_specs=out_specs
        ),
        out_shape=out_shape,
        compiler_params=pltpu.CompilerParams(
            dimension_semantics=("arbitrary",), vmem_limit_bytes=max(16 << 20, 6 * size)
        ),
        cost_estimate=pl.CostEstimate(flops=0, bytes_accessed=2 * size, transcendentals=0),
        name="pieces",
    )(jnp.stack(all_places).astype(jnp.int32), *args)
    return [r.reshape(final) for r, final in zip(result, finals)]


def scattered(grid, *groups):
    wanted = []
    for sources, axis, dim, share in groups:
        here, extent = coordinate(grid, axis), grid[axis]
        wanted.append((sources, dim, [(here + shift) % extent for shift in range(extent)], share))
    taken = pieces(wanted)
    results = []
    for _, axis, _, _ in groups:
        own, *others = taken[: grid[axis]]
        taken = taken[grid[axis] :]
        results.append(
            [own]
            + [shifted(other, grid, axis, shift) for shift, other in enumerate(others, start=1)]
        )
    return results


def assemble_kernel(count, chips, *refs):
    inputs, (weights, gains) = refs[: 2 * 2 * count], refs[2 * 2 * count :]
    core = chips[chips.shape[0] - 1]
    width = weights.shape[-1]
    for which in range(2):
        place = core if which == 0 else 1 - core
        at = 0
        for number in range(2 * count):
            source = inputs[which * 2 * count + number]
            second = number >= count
            for i in range(source.shape[0]):
                for k in range(source.shape[1]):
                    chip = chips[at]
                    at += 1
                    if second:
                        weights[2 + place, chip] = source[i, k, :, :width]
                        if which == 0 and gains is not None:
                            gains[chip] = source[i, k, :, width:]
                    else:
                        weights[place, chip] = source[i, k]


def along(values, grid, axis):
    return [values] + [shifted(values, grid, axis, shift) for shift in range(1, grid[axis])]


def gather_z(matrices, grid):
    every = along(jnp.concatenate(matrices, axis=1), grid, 0)
    stacked, at = [], 0
    for matrix in matrices:
        end = at + matrix.shape[1]
        stacked.append(jnp.stack([values[:, at:end] for values in every]))
        at = end
    return stacked


def gather_near(first, second, grid):
    return jnp.stack(along(first, grid, 1)), jnp.stack(along(second, grid, 2))


def gather_far(first, second, grid):
    return along(first, grid, 2), along(second, grid, 1)


def gather_end(mine, other, grid):
    first_sets, second_sets = mine
    mine, other = first_sets + second_sets, other[0] + other[1]
    rows, width = first_sets[0].shape[-2:]
    chips = grid[0] * grid[1] * grid[2]
    here = [coordinate(grid, axis) for axis in range(3)]
    places = []
    for outer, inner in ((2, 1), (1, 2)):
        for far in range(grid[outer]):
            for near in range(grid[inner]):
                for deep in range(grid[0]):
                    at = [None, None, None]
                    at[outer] = (here[outer] - far) % grid[outer]
                    at[inner] = (here[inner] - near) % grid[inner]
                    at[0] = (here[0] - deep) % grid[0]
                    places.append((at[0] * grid[1] + at[1]) * grid[2] + at[2])
    places.append(lax.axis_index("seq"))
    assert len(first_sets) == len(second_sets)
    extra = second_sets[0].shape[-1] - width
    out_shape = [pltpu.HBM((4, chips, rows, width), BF16)]
    if extra:
        out_shape.append(pltpu.HBM((chips, rows, extra), BF16))
    in_vmem = pl.BlockSpec(memory_space=pltpu.VMEM)

    def kernel(places, *refs):
        assemble_kernel(len(first_sets), places, *(refs if extra else refs + (None,)))

    result = pl.pallas_call(
        kernel,
        in_specs=[pl.BlockSpec(memory_space=pltpu.SMEM)] + [in_vmem] * (2 * len(mine)),
        out_specs=[in_vmem] * len(out_shape),
        out_shape=out_shape,
        compiler_params=pltpu.CompilerParams(vmem_limit_bytes=48 << 20),
        cost_estimate=pl.CostEstimate(
            flops=0, bytes_accessed=16 * chips * rows * width, transcendentals=0
        ),
        name="assemble",
    )(jnp.stack(places).astype(jnp.int32), *mine, *other)
    weights = result[0].reshape(4, chips * rows, width)
    return weights, result[1].reshape(chips * rows, extra) if extra else None


def on_device(
    hidden_in,
    encoder_out,
    segment_ids,
    passage_counts,
    cotangent,
    w_query,
    w_key,
    w_value,
    w_out,
    w_cross_query,
    w_cross_key,
    w_cross_value,
    w_cross_out,
    w_ffn_in,
    w_ffn_out,
    gain_self,
    gain_cross,
    gain_ffn,
):
    cores = lax.axis_size("seq")
    core = lax.axis_index("seq")
    chips = lax.axis_size("dp")
    grid = grid_of(chips)
    width = hidden_in.shape[-1]
    half = width // 2
    ratio = w_ffn_in.shape[1] // width
    rows = w_query.shape[0]
    joint = ("dp", "seq")

    def own_rows(values):
        part = values.shape[0] // cores
        return lax.dynamic_slice_in_dim(values, core * part, part, 0)

    def in_order(mine, other, axis):
        first = jnp.where(core == 0, mine, other)
        second = jnp.where(core == 0, other, mine)
        return jnp.concatenate([first, second], axis=axis)

    ffn_in_rows = jnp.concatenate(
        [w_ffn_in[:, i * width : (i + 1) * width] for i in range(ratio)], axis=0
    )
    ffn_rows = own_rows(jnp.concatenate([ffn_in_rows, w_ffn_out], axis=1))
    gains = jnp.stack([gain_self, gain_cross, gain_ffn], axis=1)
    gains = jnp.pad(gains, ((0, 0), (0, LANES - gains.shape[1])))

    def by_core(here, there):
        return jnp.where(core == 0, here, there)

    def tied(value, others):
        return lax.optimization_barrier((value, others))

    def sent(values):
        return swapped(lax.dynamic_index_in_dim(values, 1 - core, 0, keepdims=False))

    def returned(mine, theirs):
        return in_order(mine[None, None], theirs[None, None], 0)

    def exchanged(sets):
        return tuple([swapped(values) for values in one] for one in sets)

    hidden_both, encoded_both, branch_both = hidden_in[:, 0], encoder_out[:, 0], cotangent[:, 0]
    hidden_theirs, encoded_theirs, branch_theirs = (
        sent(hidden_both),
        sent(encoded_both),
        sent(branch_both),
    )
    segments = in_order(
        lax.dynamic_index_in_dim(segment_ids[:, 0], core, 0, keepdims=False),
        sent(segment_ids[:, 0]),
        0,
    )
    count = lax.dynamic_index_in_dim(passage_counts[:, 0], core, 0, keepdims=False)
    scalars = jnp.stack([count, core.astype(jnp.int32)])
    seg_row = segments[None, :]
    seg_col = segments[:, None]

    stacked = gather_z(
        [
            by_core(w_query, w_value),
            jnp.concatenate([by_core(w_key, w_out), gains], axis=1),
            by_core(w_cross_key, w_cross_query),
            by_core(w_cross_value, w_cross_out),
        ],
        grid,
    )
    self_rows, cross_rows = stacked[:2], stacked[2:]
    ffn_rows, self_rows = tied(ffn_rows, self_rows)
    ffn_set = lax.all_gather(ffn_rows, joint, axis=0, tiled=True)
    self_rows = gather_near(*self_rows, grid)
    self_near = [[values] for values in self_rows]
    self_far = [values[1:] for values in gather_far(*self_rows, grid)]
    self_other = exchanged(self_near)
    self_far, _ = tied(self_far, (self_other, scalars, seg_row, seg_col, hidden_theirs))
    cross_rows, self_far = tied(cross_rows, self_far)
    self_set, gains = gather_end(
        [near + far for near, far in zip(self_near, self_far)],
        [near + far for near, far in zip(self_other, exchanged(self_far))],
        grid,
    )
    cross_rows = along(cross_rows[0], grid, 1), along(cross_rows[1], grid, 2)

    w_in = ffn_set.reshape(chips, ratio, rows, 2 * width)
    if rows % 16:
        w_in = w_in[:, :, :, :width].transpose(1, 0, 2, 3).reshape(1, ratio, width, width)

    hidden, normed_self, qkv, gain_rows = project(
        scalars, hidden_both, hidden_theirs, gains, self_set
    )
    cross_rows, qkv = tied(cross_rows, qkv)
    cross_rows = [jnp.stack(values) for values in cross_rows]
    cross_near = [[values] for values in cross_rows]
    cross_far = [values[1:] for values in gather_far(*cross_rows, grid)]
    cross_other = exchanged(cross_near)
    qkv, (cross_near, cross_other) = tied(qkv, (cross_near, cross_other))
    attended, self_lse, after_self, normed_cross = self_forward(
        qkv, seg_row, seg_col, hidden, gain_rows, self_set
    )
    normed_cross, cross_far = tied(normed_cross, cross_far)
    cross_set, _ = gather_end(
        [near + far for near, far in zip(cross_near, cross_far)],
        [near + far for near, far in zip(cross_other, exchanged(cross_far))],
        grid,
    )
    encoded, ckv, cross_queries = project_cross(
        scalars, encoded_both, encoded_theirs, normed_cross, cross_set
    )
    cross_attended, cross_lse, after_cross, normed_ffn = cross_forward(
        cross_queries, ckv, scalars, after_self, gain_rows, cross_set
    )
    out_mine, out_theirs, d_after_cross, grad_in, kept_out, sent_out = feed_forward(
        scalars, normed_ffn, branch_both, branch_theirs, after_cross, gain_rows, ffn_set, w_in
    )
    grad_in = lax.psum_scatter(grad_in, joint, scatter_dimension=0, tiled=True)

    def by_chip(values):
        return values.reshape(grid + (-1, values.shape[-1]))

    def pair_parts(kept, sent):
        return [by_chip(kept), by_chip(swapped(sent))]

    def whole_source(parts):
        return (parts, parts[0].shape[-1], 0)

    every = (0, 1)

    def along_first(first, second, first_share=every, second_share=every):
        return scattered(grid, (first, 2, 2, first_share), (second, 1, 1, second_share))

    def along_second(first, second):
        return scattered(
            grid, ([whole_source(first)], 1, 1, every), ([whole_source(second)], 2, 1, every)
        )

    def along_z(first, second):
        return scattered(grid, ([whole_source(first), whole_source(second)], 0, 0, every))[0]

    ffn_out = pair_parts(kept_out, sent_out)
    d_att = cross_branch(d_after_cross, cross_set)
    d_att, ffn_out = tied(d_att, ffn_out)
    by_rows = ratio * rows // 2 % 16 == 0
    if by_rows:
        ffn_first, ffn_second = along_first(
            [(ffn_out, half, 0)], [(ffn_out, half, 0)], (0, 2), (1, 2)
        )
    else:
        ffn_first, ffn_second = along_first(
            [(ffn_out, 2 * LANES, 0)], [(ffn_out, half - 2 * LANES, 2)]
        )
    d_att, _ = tied(d_att, (ffn_first[0], ffn_second[0]))
    d_after_self, d_att, kept_c, sent_c, encoded_mine, encoded_their = cross_backward(
        scalars,
        cross_queries,
        ckv,
        d_att,
        cross_lse,
        d_after_cross,
        after_self,
        normed_cross,
        cross_attended,
        attended,
        encoded,
        gain_rows,
        cross_set,
        self_set,
    )
    d_att, (ffn_first, ffn_second) = tied(d_att, (ffn_first, ffn_second))
    ffn_first, ffn_second = along_second(ffn_first, ffn_second)
    d_att, _ = tied(d_att, (ffn_first[0], ffn_second[0]))
    cross_all = pair_parts(kept_c, sent_c)
    d_first = self_backward_first(seg_row, seg_col, qkv, d_att, self_lse)
    out_theirs, encoded_their = swapped(out_theirs), swapped(encoded_their)
    d_first, (ffn_first, ffn_second, cross_all, out_theirs, encoded_their) = tied(
        d_first, (ffn_first, ffn_second, cross_all, out_theirs, encoded_their)
    )
    cross_first, cross_second = along_first(
        [(cross_all, half, 3), (cross_all, half, 0), (cross_all, half, 4)],
        [(cross_all, half, 1), (cross_all, half, 2)],
    )
    ffn_parts = along_z(ffn_first, ffn_second)
    d_first, _ = tied(d_first, (ffn_parts[0], cross_first[0], cross_second[0]))
    *self_grads, d_last = self_backward_last(
        scalars, seg_row, seg_col, qkv, d_att, self_lse, d_first, normed_self
    )
    self_grads, ffn_parts = tied(self_grads, ffn_parts)
    self_qkv = [pair_parts(self_grads[i], self_grads[3 + i]) for i in range(3)]
    d_last, (cross_first, cross_second) = tied(d_last, (cross_first, cross_second))
    cross_first, cross_second = along_second(cross_first, cross_second)
    self_qkv, _ = tied(self_qkv, (cross_first[0], cross_second[0]))
    self_first, self_second = along_first(
        [(self_qkv[0], half, 0), (self_qkv[2], 2 * LANES, 0)],
        [(self_qkv[1], half, 0), (self_qkv[2], half - 2 * LANES, 2)],
    )
    d_last, _ = tied(d_last, (self_first[0], self_second[0]))
    hidden_mine, hidden_their = self_input(
        scalars, d_first, d_last, d_after_self, hidden, gain_rows, self_set
    )
    def matrices(mine, places):
        other = swapped(mine)
        results = []
        for spans in places:
            halves = [
                jnp.concatenate([values[:, start:end] for start, end in spans], axis=1)
                for values in (mine, other)
            ]
            results.append(in_order(*halves, 1))
        return results

    def gain_gradient(gain, *pairs):
        weighed = [weight_rows.astype(F32) * grad for weight_rows, grad in pairs]
        return jnp.sum(total(weighed), axis=1) / gain.astype(F32)

    hidden_their, (self_first, self_second, cross_first, cross_second) = tied(
        hidden_their, (self_first, self_second, cross_first, cross_second)
    )
    ffn_sum = total(ffn_parts)
    if by_rows:
        ffn_sum = jnp.concatenate([ffn_sum[:, :half], ffn_sum[:, half:]], axis=0)
    (grad_ffn_out,) = matrices(ffn_sum, [[(0, half)]])
    (cross_first, cross_second), grad_ffn_out = tied((cross_first, cross_second), grad_ffn_out)
    cross_parts = along_z(cross_first, cross_second)
    (self_first, self_second), _ = tied((self_first, self_second), cross_parts[0])
    self_first, self_second = along_second(self_first, self_second)
    (cross_parts, hidden_their, grad_in), _ = tied(
        (cross_parts, hidden_their, grad_in), (self_first[0], self_second[0])
    )
    self_parts = along_z(self_first, self_second)
    cross_grads = matrices(total(cross_parts), [[(i * half, (i + 1) * half)] for i in range(5)])
    grad_co, grad_cq, grad_o, grad_ck, grad_cv = cross_grads
    grad_in = lax.all_gather(grad_in, "seq", axis=0, tiled=True).astype(F32)
    done = (
        returned(out_mine, out_theirs),
        returned(hidden_mine, swapped(hidden_their)),
        returned(encoded_mine, encoded_their),
        gain_gradient(gain_cross, (w_cross_query, grad_cq)),
        gain_gradient(gain_ffn, (w_ffn_in, grad_in)),
    )
    self_parts, (done, cross_grads, grad_in) = tied(self_parts, (done, cross_grads, grad_in))
    grad_co, grad_cq, grad_o, grad_ck, grad_cv = cross_grads
    split = half + 2 * LANES
    grad_q, grad_k, grad_v = matrices(
        total(self_parts),
        [
            [(0, half)],
            [(split, split + half)],
            [(half, split), (split + half, 3 * half)],
        ],
    )
    return done[:3] + (
        grad_q,
        grad_k,
        grad_v,
        grad_o,
        grad_cq,
        grad_ck,
        grad_cv,
        grad_co,
        grad_in,
        grad_ffn_out,
        gain_gradient(gain_self, (w_query, grad_q), (w_key, grad_k), (w_value, grad_v)),
    ) + done[3:]


def solution(mesh):
    tokens = P(None, "dp", "seq", None)
    rows = P("dp", None)
    gain = P("dp")
    return jax.shard_map(
        on_device,
        mesh=mesh,
        in_specs=(tokens, tokens, P(None, "dp", "seq"), P(None, "dp"), tokens)
        + (rows,) * 10
        + (gain,) * 3,
        out_specs=(tokens,) * 3 + (rows,) * 10 + (gain,) * 3,
        check_vma=False,
    )
```

```python
import functools

import jax
import jax.numpy as jnp
from jax import lax
from jax.experimental import pallas as pl
from jax.experimental.pallas import tpu as pltpu
from jax.sharding import PartitionSpec as P

HEAD_DIM = 64
LANES = 128
SEGMENT_LIMIT = 384
SELF_BLOCK = 256
CROSS_BLOCK = 768
EPS = 1e-06
NEG = -1e30
GELU_RATE = 0.7978845608
GELU_CUBIC = 0.044715
BF16 = jnp.bfloat16
F32 = jnp.float32


def product(left, right):
    return jnp.dot(left, right, preferred_element_type=F32)


def row_outer(left, right):
    return lax.dot_general(left, right, (((0,), (0,)), ((), ())), preferred_element_type=F32)


def right_transposed(left, right):
    return lax.dot_general(left, right, (((1,), (1,)), ((), ())), preferred_element_type=F32)


def inverse_rms(values):
    return lax.rsqrt(jnp.mean(values * values, axis=-1, keepdims=True) + EPS)


def norm_backward(values, scale, gain, d_normed):
    scaled = gain * d_normed
    d_values = scale * scaled - values * (scale * scale * scale) * jnp.mean(
        values * scaled, axis=-1, keepdims=True
    )
    return d_values


def self_blocks(length):
    blocks = []
    for start in range(0, length, SELF_BLOCK):
        end = min(start + SELF_BLOCK, length)
        first = max(0, start - SEGMENT_LIMIT + 1) // LANES * LANES
        blocks.append((start, end, first, end))
    return blocks


def cross_blocks(length, keys):
    return [
        (start, min(start + CROSS_BLOCK, length), 0, keys)
        for start in range(0, length, CROSS_BLOCK)
    ]


def of_head(values, head):
    lanes = lax.broadcasted_iota(jnp.int32, values.shape, 1)
    return jnp.where(lanes // HEAD_DIM == head, values, jnp.zeros_like(values))


def ahead(first_step, items):
    coming = first_step(*items[0])
    for at, item in enumerate(items):
        result = coming
        if at + 1 < len(items):
            coming = first_step(*items[at + 1])
        yield item, result


def pair_forward(blocks, bias_of, q_ref, k_ref, v_ref, o_ref, lse_ref, lse_cols):
    pair = pl.program_id(0)
    lane = lax.broadcasted_iota(jnp.int32, (1, LANES), 1)

    def scores_of(block, head):
        start, end, first, last = block
        query_head = of_head(q_ref[start:end, :], head)
        return right_transposed(query_head, k_ref[first:last, :]) + bias_of(*block)

    mixed = []
    items = [(block, head) for block in blocks for head in range(2)]
    for ((start, end, first, last), head), scores in ahead(scores_of, items):
        row_max = jnp.max(scores, axis=-1, keepdims=True)
        exponents = jnp.exp(scores - row_max)
        totals = jnp.sum(exponents, axis=-1, keepdims=True)
        mixed.append(product(exponents.astype(BF16), v_ref[first:last, :]) / totals)
        lse_cols[start:end, :] = jnp.where(
            lane == 2 * pair + head, row_max + jnp.log(totals), lse_cols[start:end, :]
        )
        if head == 1:
            o_ref[start:end, :] = jnp.where(lane < HEAD_DIM, mixed[-2], mixed[-1]).astype(BF16)

    @pl.when(pair == pl.num_programs(0) - 1)
    def _():
        lse_ref[...] = jnp.transpose(lse_cols[...])[: lse_ref.shape[0], :]


def pair_backward(
    blocks, bias_of, q_ref, k_ref, v_ref, d_ref, lse_ref, dk_acc, dv_acc, first_pair=0
):
    pair = first_pair + pl.program_id(0)

    def products_of(block, head):
        start, end, first, last = block
        query_head = of_head(q_ref[start:end, :], head)
        d_head = of_head(d_ref[start:end, :], head)
        scores = right_transposed(k_ref[first:last, :], query_head)
        d_probs = right_transposed(v_ref[first:last, :], d_head)
        return query_head, d_head, scores, d_probs

    dk_acc[...] = jnp.zeros_like(dk_acc)
    dv_acc[...] = jnp.zeros_like(dv_acc)
    d_queries, rows = [], []
    items = [(block, head) for block in blocks for head in range(2)]
    for (block, head), (query_head, d_head, scores, d_probs) in ahead(products_of, items):
        start, end, first, last = block
        log_totals = lse_ref[pl.ds(2 * pair + head, 1), start:end]
        exact = jnp.exp(scores + (bias_of(*block) - log_totals))
        inner = jnp.sum(exact * d_probs, axis=0, keepdims=True)
        d_scores = (exact * (d_probs - inner)).astype(BF16)
        dv_acc[first:last, :] += product(exact.astype(BF16), d_head)
        dk_acc[first:last, :] += product(d_scores, query_head)
        rows.append(row_outer(d_scores, of_head(k_ref[first:last, :], head)))
        if head == 1:
            d_queries.append((start, end, rows[-2] + rows[-1]))
    return d_queries


def store_halves(core, kept, sent, place, value):
    half = value.shape[-1] // 2
    there = slice(place, place + half)

    @pl.when(core == 0)
    def _():
        kept[..., there] = value[..., :half]
        sent[..., there] = value[..., half:]

    @pl.when(core != 0)
    def _():
        kept[..., there] = value[..., half:]
        sent[..., there] = value[..., :half]


def store_rows(core, mine, theirs, value):
    length = mine.shape[0]

    @pl.when(core == 0)
    def _():
        mine[...] = value[:length, :]
        theirs[...] = value[length:, :]

    @pl.when(core != 0)
    def _():
        mine[...] = value[length:, :]
        theirs[...] = value[:length, :]


def masked_bias(seg_col, seg_row, keys_first):
    shape = (seg_col.shape[0], seg_row.shape[1])
    rows = lax.broadcasted_iota(jnp.int32, shape, 0)
    lanes = lax.broadcasted_iota(jnp.int32, shape, 1)
    ordered = rows <= lanes if keys_first else lanes <= rows
    return jnp.where(ordered & (seg_col[...] == seg_row[...]), 0.0, NEG)


def put_together(core, both, theirs, whole_rows):
    length = theirs.shape[0]

    @pl.when(core == 0)
    def _():
        whole_rows[:length, :] = both[0]
        whole_rows[length:, :] = theirs[...]

    @pl.when(core != 0)
    def _():
        whole_rows[:length, :] = theirs[...]
        whole_rows[length:, :] = both[1]


def project_kernel(scalars, both, theirs, gains, weight, hidden, normed, qkv, gain_rows):
    @pl.when(pl.program_id(0) == 0)
    def _():
        put_together(scalars[1], both, theirs, hidden)
        rows = jnp.transpose(gains[...].astype(F32))[: gain_rows.shape[0], :]
        gain_rows[...] = rows
        values = hidden[...].astype(F32)
        normed[...] = (values * inverse_rms(values) * rows[0:1, :]).astype(BF16)

    qkv[...] = product(normed[...], weight[...]).astype(BF16)


def project_cross_kernel(
    scalars, both, theirs, normed_cross, weight, encoded, ckv, cross_queries
):
    step = pl.program_id(0)

    @pl.when(step == 0)
    def _():
        put_together(scalars[1], both, theirs, encoded)

    @pl.when(step == 1)
    def _():
        cross_queries[...] = product(normed_cross[...], weight[...]).astype(BF16)

    @pl.when(step != 1)
    def _():
        ckv[...] = product(encoded[...], weight[...]).astype(BF16)


def self_forward_kernel(
    blocks,
    seg_row,
    seg_col,
    hidden,
    gain_rows,
    q_ref,
    k_ref,
    v_ref,
    w_o,
    attended,
    lse_ref,
    after_self,
    normed_cross,
    bias,
    lse_cols,
    mixed,
):
    @pl.when(pl.program_id(0) == 0)
    def _():
        bias[...] = masked_bias(seg_col, seg_row, False)
        lse_cols[...] = jnp.zeros_like(lse_cols)

    pair_forward(
        blocks,
        lambda start, end, first, last: bias[start:end, first:last],
        q_ref,
        k_ref,
        v_ref,
        mixed,
        lse_ref,
        lse_cols,
    )
    place = pl.multiple_of(pl.program_id(0) * LANES, LANES)
    attended[:, pl.ds(place, LANES)] = mixed[...]

    @pl.when(pl.program_id(0) == pl.num_programs(0) - 1)
    def _():
        values = hidden[...].astype(F32) + product(attended[...], w_o[...])
        after_self[...] = values
        normed_cross[...] = (values * inverse_rms(values) * gain_rows[1:2, :]).astype(BF16)


def cross_forward_kernel(
    blocks,
    count,
    after_self,
    gain_rows,
    q_ref,
    k_ref,
    v_ref,
    w_co,
    attended,
    lse_ref,
    after_cross,
    normed_ffn,
    lse_cols,
    mixed,
):
    @pl.when(pl.program_id(0) == 0)
    def _():
        lse_cols[...] = jnp.zeros_like(lse_cols)

    places = lax.broadcasted_iota(jnp.int32, (1, k_ref.shape[0]), 1)
    bias = jnp.where(places < count[0], 0.0, NEG)
    pair_forward(
        blocks,
        lambda start, end, first, last: bias,
        q_ref,
        k_ref,
        v_ref,
        mixed,
        lse_ref,
        lse_cols,
    )
    place = pl.multiple_of(pl.program_id(0) * LANES, LANES)
    attended[:, pl.ds(place, LANES)] = mixed[...]

    @pl.when(pl.program_id(0) == pl.num_programs(0) - 1)
    def _():
        values = after_self[...] + product(attended[...], w_co[...])
        after_cross[...] = values
        normed_ffn[...] = (values * inverse_rms(values) * gain_rows[2:3, :]).astype(BF16)


def ffn_kernel(
    scalars,
    normed,
    both,
    theirs,
    after_cross,
    gain_rows,
    w_in,
    w_out,
    out_mine,
    out_theirs,
    d_after_cross,
    grad_in,
    kept_out,
    sent_out,
    out_acc,
    dn_acc,
    normed_t,
    branch,
):
    step = pl.program_id(0)

    @pl.when(step == 0)
    def _():
        put_together(scalars[1], both, theirs, branch)
        normed_t[...] = jnp.transpose(normed[...])
        out_acc[...] = jnp.zeros_like(out_acc)
        dn_acc[...] = jnp.zeros_like(dn_acc)

    width = normed.shape[1]
    up = w_in[...].reshape(width, -1)
    down = w_out[...]
    pre = product(normed[...], up)
    d_act = right_transposed(branch[...], down)
    bent = jnp.tanh(GELU_RATE * (pre + GELU_CUBIC * pre * pre * pre))
    half = 0.5 * (1.0 + bent)
    hidden_act = (pre * half).astype(BF16)
    slope = half + 0.5 * pre * (1.0 - bent * bent) * GELU_RATE * (
        1.0 + 3.0 * GELU_CUBIC * pre * pre
    )
    out_acc[...] += product(hidden_act, down)
    d_pre = (d_act * slope).astype(BF16)
    grad_out = row_outer(hidden_act, branch[...]).astype(BF16)
    store_halves(scalars[1], kept_out, sent_out, 0, grad_out)
    grad_in[...] = product(normed_t[...], d_pre).astype(BF16)
    dn_acc[...] += right_transposed(d_pre, up)

    @pl.when(step == pl.num_programs(0) - 1)
    def _():
        values = after_cross[...]
        store_rows(scalars[1], out_mine, out_theirs, (values + out_acc[...]).astype(BF16))
        d_values = norm_backward(values, inverse_rms(values), gain_rows[2:3, :], dn_acc[...])
        d_after_cross[...] = branch[...].astype(F32) + d_values


def attended_gradient(branch, w_out, d_att):
    d_mixed = right_transposed(branch, w_out[...]).astype(BF16)
    for pair in range(d_att.shape[0]):
        d_att[pair] = d_mixed[:, pair * LANES : (pair + 1) * LANES]


def cross_branch_kernel(d_after, w_out, d_att):
    attended_gradient(d_after[...].astype(BF16), w_out, d_att)


def cross_backward_kernel(
    blocks,
    scalars,
    q_ref,
    k_ref,
    v_ref,
    d_att,
    lse_ref,
    d_after_cross,
    after_self,
    normed_cross,
    cross_attended,
    self_attended,
    encoded,
    gain_rows,
    w_cq,
    w_ck,
    w_cv,
    w_o,
    d_after_self,
    d_att_self,
    kept,
    sent,
    encoded_mine,
    encoded_theirs,
    dq_all,
    dkv_all,
    dk_acc,
    dv_acc,
):
    step = pl.program_id(0)
    width = d_after_cross.shape[1]
    half = width // 2
    places = lax.broadcasted_iota(jnp.int32, (k_ref.shape[0], 1), 0)
    bias = jnp.where(places < scalars[0], 0.0, NEG)
    d_queries = pair_backward(
        blocks,
        lambda start, end, first, last: bias,
        q_ref,
        k_ref,
        v_ref,
        d_att.at[0],
        lse_ref,
        dk_acc,
        dv_acc,
    )
    place = pl.multiple_of(step * LANES, LANES)
    for start, end, d_query in d_queries:
        dq_all[start:end, pl.ds(place, LANES)] = d_query.astype(BF16)
    dkv_all[:, pl.ds(place, LANES)] = dk_acc[...].astype(BF16)
    dkv_all[:, pl.ds(width + place, LANES)] = dv_acc[...].astype(BF16)

    @pl.when(step == pl.num_programs(0) - 1)
    def _():
        dq = dq_all[...]
        grad_query = row_outer(normed_cross[...], dq).astype(BF16)
        grad_kv = row_outer(encoded[...], dkv_all[...]).astype(BF16)
        store_halves(scalars[1], kept, sent, 0, grad_query)
        store_halves(scalars[1], kept, sent, half, grad_kv[:, :width])
        store_halves(scalars[1], kept, sent, 2 * half, grad_kv[:, width:])
        grad_out = row_outer(cross_attended[...], d_after_cross[...].astype(BF16))
        store_halves(scalars[1], kept, sent, 3 * half, grad_out.astype(BF16))
        grad_encoded = right_transposed(dkv_all[:, :width], w_ck[...]) + right_transposed(
            dkv_all[:, width:], w_cv[...]
        )
        store_rows(scalars[1], encoded_mine, encoded_theirs, grad_encoded)
        values = after_self[...]
        d_values = norm_backward(
            values,
            inverse_rms(values),
            gain_rows[1:2, :],
            right_transposed(dq, w_cq[...]),
        )
        d_values = d_after_cross[...] + d_values
        d_after_self[...] = d_values
        branch = d_values.astype(BF16)
        attended_gradient(branch, w_o, d_att_self)
        grad_out = row_outer(self_attended[...], branch)
        store_halves(scalars[1], kept, sent, 4 * half, grad_out.astype(BF16))


def self_backward_pairs(
    blocks, seg_row, seg_col, q_ref, k_ref, v_ref, d_att, lse_ref, d_all, bias, dk_acc, dv_acc, first
):
    @pl.when(pl.program_id(0) == 0)
    def _():
        bias[...] = masked_bias(seg_col, seg_row, True)

    d_queries = pair_backward(
        blocks,
        lambda start, end, first_key, last_key: bias[first_key:last_key, start:end],
        q_ref,
        k_ref,
        v_ref,
        d_att.at[0],
        lse_ref,
        dk_acc,
        dv_acc,
        first,
    )
    place = pl.multiple_of(pl.program_id(0) * LANES, LANES)
    for start, end, d_query in d_queries:
        d_all[0, start:end, pl.ds(place, LANES)] = d_query.astype(BF16)
    d_all[1, :, pl.ds(place, LANES)] = dk_acc[...].astype(BF16)
    d_all[2, :, pl.ds(place, LANES)] = dv_acc[...].astype(BF16)


def self_backward_first_kernel(
    blocks, seg_row, seg_col, q_ref, k_ref, v_ref, d_att, lse_ref, d_all, bias, dk_acc, dv_acc
):
    self_backward_pairs(
        blocks, seg_row, seg_col, q_ref, k_ref, v_ref, d_att, lse_ref, d_all, bias, dk_acc, dv_acc, 0
    )


def self_backward_last_kernel(
    blocks,
    first,
    scalars,
    seg_row,
    seg_col,
    q_ref,
    k_ref,
    v_ref,
    d_att,
    lse_ref,
    d_first,
    normed_self,
    kept_q,
    kept_k,
    kept_v,
    sent_q,
    sent_k,
    sent_v,
    d_last,
    bias,
    dk_acc,
    dv_acc,
):
    self_backward_pairs(
        blocks,
        seg_row,
        seg_col,
        q_ref,
        k_ref,
        v_ref,
        d_att,
        lse_ref,
        d_last,
        bias,
        dk_acc,
        dv_acc,
        first,
    )

    @pl.when(pl.program_id(0) == pl.num_programs(0) - 1)
    def _():
        normed_t = jnp.transpose(normed_self[...])
        for i, (kept, sent) in enumerate(
            ((kept_q, sent_q), (kept_k, sent_k), (kept_v, sent_v))
        ):
            grad = product(normed_t, jnp.concatenate([d_first[i], d_last[i]], axis=1))
            store_halves(scalars[1], kept, sent, 0, grad.astype(BF16))


def self_input_kernel(
    scalars, d_first, d_last, d_after_self, hidden, gain_rows, w_q, w_k, w_v, mine, theirs
):
    d_normed = None
    for i, weight_ref in enumerate((w_q, w_k, w_v)):
        d_out = jnp.concatenate([d_first[i], d_last[i]], axis=1)
        part = right_transposed(d_out, weight_ref[...])
        d_normed = part if d_normed is None else d_normed + part
    values = hidden[...].astype(F32)
    d_values = norm_backward(values, inverse_rms(values), gain_rows[0:1, :], d_normed)
    store_rows(scalars[1], mine, theirs, d_after_self[...] + d_values)


def columns(rows, offset):
    return pl.BlockSpec((rows, LANES), lambda step: (0, offset + step))


def whole(shape, place=None):
    place = (0,) * len(shape) if place is None else place
    return pl.BlockSpec(shape, lambda step: place)


def like(*shapes):
    return [jax.ShapeDtypeStruct(shape, dtype) for shape, dtype in shapes]


def with_late(kernel, late, steps):
    def run(*refs):
        sems, buffers = refs[-1], refs[-1 - len(late) : -1]
        refs = list(refs[: -1 - len(late)])
        copies = []
        for at, ((number, index), buffer) in enumerate(zip(late, buffers)):
            source = refs[number] if index is None else refs[number].at[index]
            copies.append(pltpu.make_async_copy(source, buffer, sems.at[at]))
            refs[number] = buffer

        @pl.when(pl.program_id(0) == 0)
        def _():
            for copy in copies:
                copy.start()

        @pl.when(pl.program_id(0) == steps - 1)
        def _():
            for copy in copies:
                copy.wait()

        kernel(*refs)

    return run


def call(
    kernel, name, steps, in_specs, out_specs, out_shape, scratch, flops, args, grant=56, late=()
):
    size = sum(int(a.size) * a.dtype.itemsize for a in args)
    if late:
        in_specs, scratch = list(in_specs), list(scratch)
        for number, index in late:
            shape = args[number].shape if index is None else args[number].shape[1:]
            in_specs[number] = pl.BlockSpec(memory_space=pl.ANY)
            scratch.append(pltpu.VMEM(shape, args[number].dtype))
        scratch.append(pltpu.SemaphoreType.DMA((len(late),)))
        kernel = with_late(kernel, late, steps)
    return pl.pallas_call(
        kernel,
        grid=(steps,),
        in_specs=in_specs,
        out_specs=out_specs,
        out_shape=out_shape,
        scratch_shapes=scratch,
        compiler_params=pltpu.CompilerParams(
            dimension_semantics=("arbitrary",), vmem_limit_bytes=grant << 20
        ),
        cost_estimate=pl.CostEstimate(flops=flops, bytes_accessed=size, transcendentals=0),
        name=name,
    )(*args)


QUERY, VALUE, KEY, OUT = range(4)
CROSS_KEY, CROSS_QUERY, CROSS_VALUE, CROSS_OUT = range(4)


def weight(width, place):
    return pl.BlockSpec((None, width, width), lambda step: (place, 0, 0))


def project(scalars, both, theirs, gains, self_set):
    cores, half_length, width = both.shape
    length = cores * half_length
    shape = (length, width)
    return call(
        project_kernel,
        "project",
        3,
        [
            pl.BlockSpec(memory_space=pltpu.SMEM),
            whole(both.shape),
            whole(theirs.shape),
            whole(gains.shape),
            pl.BlockSpec((None, width, width), lambda step: (2 * step % 3, 0, 0)),
        ],
        [
            whole(shape),
            whole(shape),
            pl.BlockSpec((length, width), lambda step: (0, step)),
            whole((8, width)),
        ],
        like((shape, BF16), (shape, BF16), ((length, 3 * width), BF16), ((8, width), F32)),
        [],
        6 * length * width * width,
        (scalars, both, theirs, gains, self_set),
    )


def project_cross(scalars, both, theirs, normed_cross, cross_set):
    length, width = normed_cross.shape
    keys = both.shape[0] * both.shape[1]
    return call(
        project_cross_kernel,
        "project_cross",
        3,
        [
            pl.BlockSpec(memory_space=pltpu.SMEM),
            whole(both.shape),
            whole(theirs.shape),
            whole(normed_cross.shape),
            pl.BlockSpec((None, width, width), lambda step: (step, 0, 0)),
        ],
        [
            whole((keys, width)),
            pl.BlockSpec((keys, width), lambda step: (0, step // 2)),
            whole(normed_cross.shape),
        ],
        like(((keys, width), BF16), ((keys, 2 * width), BF16), (normed_cross.shape, BF16)),
        [],
        2 * width * width * (length + 2 * keys),
        (scalars, both, theirs, normed_cross, cross_set),
    )


def self_forward(qkv, seg_row, seg_col, hidden, gain_rows, self_set):
    length, width = hidden.shape
    pairs = width // LANES
    return call(
        functools.partial(self_forward_kernel, self_blocks(length)),
        "self_forward",
        pairs,
        [
            whole(seg_row.shape),
            whole(seg_col.shape),
            whole(hidden.shape),
            whole(gain_rows.shape),
            columns(length, 0),
            columns(length, pairs),
            columns(length, 2 * pairs),
            weight(width, OUT),
        ],
        [
            whole(hidden.shape),
            whole((16, length)),
            whole(hidden.shape),
            whole(hidden.shape),
        ],
        like(
            (hidden.shape, BF16),
            ((16, length), F32),
            (hidden.shape, F32),
            (hidden.shape, BF16),
        ),
        [
            pltpu.VMEM((length, length), F32),
            pltpu.VMEM((length, LANES), F32),
            pltpu.VMEM((length, LANES), BF16),
        ],
        4 * length * width * (length + width),
        (
            seg_row,
            seg_col,
            hidden,
            gain_rows,
            qkv,
            qkv,
            qkv,
            self_set,
        ),
    )


def cross_forward(queries, ckv, count, after_self, gain_rows, cross_set):
    length, width = queries.shape
    keys = ckv.shape[0]
    pairs = width // LANES
    return call(
        functools.partial(cross_forward_kernel, cross_blocks(length, keys)),
        "cross_forward",
        pairs,
        [
            pl.BlockSpec(memory_space=pltpu.SMEM),
            whole(queries.shape),
            whole(gain_rows.shape),
            columns(length, 0),
            columns(keys, 0),
            columns(keys, pairs),
            weight(width, CROSS_OUT),
        ],
        [
            whole(queries.shape),
            whole((16, length)),
            whole(queries.shape),
            whole(queries.shape),
        ],
        like(
            (queries.shape, BF16),
            ((16, length), F32),
            (queries.shape, F32),
            (queries.shape, BF16),
        ),
        [pltpu.VMEM((length, LANES), F32), pltpu.VMEM((length, LANES), BF16)],
        2 * length * width * (2 * keys + width),
        (count, after_self, gain_rows, queries, ckv, ckv, cross_set),
    )


def feed_forward(scalars, normed, both, theirs, after_cross, gain_rows, ffn_set, w_in):
    length, width = normed.shape
    groups, steps, rows, _ = w_in.shape
    block = pl.BlockSpec((groups, 1, rows, width), lambda step: (0, step, 0, 0))
    half_rows = pl.BlockSpec((width, width // 2), lambda step: (step, 0))
    half_out = ((steps * width, width // 2), BF16)
    half_length = (length // both.shape[0], width)
    return call(
        ffn_kernel,
        "feed_forward",
        steps,
        [
            pl.BlockSpec(memory_space=pltpu.SMEM),
            whole(normed.shape),
            whole(both.shape),
            whole(theirs.shape),
            whole(normed.shape),
            whole(gain_rows.shape),
            block,
            pl.BlockSpec((width, width), lambda step: (step, 1)),
        ],
        [
            whole(half_length),
            whole(half_length),
            whole(normed.shape),
            pl.BlockSpec((width, width), lambda step: (0, step)),
            half_rows,
            half_rows,
        ],
        like(
            (half_length, BF16),
            (half_length, BF16),
            (normed.shape, F32),
            ((width, steps * width), BF16),
            half_out,
            half_out,
        ),
        [
            pltpu.VMEM(normed.shape, F32),
            pltpu.VMEM(normed.shape, F32),
            pltpu.VMEM((width, length), BF16),
            pltpu.VMEM((length, width), BF16),
        ],
        12 * length * width * width * steps,
        (scalars, normed, both, theirs, after_cross, gain_rows, w_in, ffn_set),
        grant=56,
        late=[(4, None)],
    )


def cross_branch(d_after, cross_set):
    length, width = d_after.shape
    shape = (width // LANES, length, LANES)
    return call(
        cross_branch_kernel,
        "cross_branch",
        1,
        [whole(d_after.shape), weight(width, CROSS_OUT)],
        whole(shape),
        jax.ShapeDtypeStruct(shape, BF16),
        [],
        2 * length * width * width,
        (d_after, cross_set),
    )


def pair_block(length, first):
    return pl.BlockSpec((1, length, LANES), lambda step: (first + step, 0, 0))


def cross_backward(
    scalars,
    queries,
    ckv,
    d_att,
    lse,
    d_after_cross,
    after_self,
    normed_cross,
    cross_attended,
    self_attended,
    encoded,
    gain_rows,
    cross_set,
    self_set,
):
    length, width = queries.shape
    keys = ckv.shape[0]
    pairs = width // LANES
    halves = (width, 5 * width // 2)
    half_keys = (keys // 2, width)
    return call(
        functools.partial(cross_backward_kernel, cross_blocks(length, keys)),
        "cross_backward",
        pairs,
        [
            pl.BlockSpec(memory_space=pltpu.SMEM),
            columns(length, 0),
            columns(keys, 0),
            columns(keys, pairs),
            pair_block(length, 0),
            whole(lse.shape),
            whole(queries.shape),
            whole(queries.shape),
            whole(queries.shape),
            whole(queries.shape),
            whole(queries.shape),
            whole(encoded.shape),
            whole(gain_rows.shape),
            weight(width, CROSS_QUERY),
            weight(width, CROSS_KEY),
            weight(width, CROSS_VALUE),
            weight(width, OUT),
        ],
        [
            whole(queries.shape),
            whole((pairs, length, LANES)),
            whole(halves),
            whole(halves),
            whole(half_keys),
            whole(half_keys),
        ],
        like(
            (queries.shape, F32),
            ((pairs, length, LANES), BF16),
            (halves, BF16),
            (halves, BF16),
            (half_keys, F32),
            (half_keys, F32),
        ),
        [
            pltpu.VMEM((length, width), BF16),
            pltpu.VMEM((keys, 2 * width), BF16),
            pltpu.VMEM((keys, LANES), F32),
            pltpu.VMEM((keys, LANES), F32),
        ],
        2 * length * width * (5 * keys + 7 * width),
        (
            scalars,
            queries,
            ckv,
            ckv,
            d_att,
            lse,
            d_after_cross,
            after_self,
            normed_cross,
            cross_attended,
            self_attended,
            encoded,
            gain_rows,
            cross_set,
            cross_set,
            cross_set,
            self_set,
        ),
        late=[(number, None) for number in range(6, 12)]
        + [(13, CROSS_QUERY), (14, CROSS_KEY), (15, CROSS_VALUE), (16, OUT)],
    )


def self_backward_first(seg_row, seg_col, qkv, d_att, lse):
    length, width = qkv.shape[0], qkv.shape[1] // 3
    pairs = width // LANES
    done = pairs // 2
    return call(
        functools.partial(self_backward_first_kernel, self_blocks(length)),
        "self_backward_first",
        done,
        [
            whole(seg_row.shape),
            whole(seg_col.shape),
            columns(length, 0),
            columns(length, pairs),
            columns(length, 2 * pairs),
            pair_block(length, 0),
            whole(lse.shape),
        ],
        whole((3, length, done * LANES)),
        jax.ShapeDtypeStruct((3, length, done * LANES), BF16),
        [
            pltpu.VMEM((length, length), F32),
            pltpu.VMEM((length, LANES), F32),
            pltpu.VMEM((length, LANES), F32),
        ],
        120 * length * width * length,
        (seg_row, seg_col, qkv, qkv, qkv, d_att, lse),
    )


def self_backward_last(scalars, seg_row, seg_col, qkv, d_att, lse, d_first, normed_self):
    length, width = normed_self.shape
    pairs = width // LANES
    done = d_first.shape[2] // LANES
    halves = (width, width // 2)
    d_last = (3, length, (pairs - done) * LANES)
    return call(
        functools.partial(self_backward_last_kernel, self_blocks(length), done),
        "self_backward_last",
        pairs - done,
        [
            pl.BlockSpec(memory_space=pltpu.SMEM),
            whole(seg_row.shape),
            whole(seg_col.shape),
            columns(length, done),
            columns(length, pairs + done),
            columns(length, 2 * pairs + done),
            pair_block(length, done),
            whole(lse.shape),
            whole(d_first.shape),
            whole(normed_self.shape),
        ],
        [whole(halves)] * 6 + [whole(d_last)],
        like(*[(halves, BF16)] * 6, (d_last, BF16)),
        [
            pltpu.VMEM((length, length), F32),
            pltpu.VMEM((length, LANES), F32),
            pltpu.VMEM((length, LANES), F32),
        ],
        2 * length * width * (length + 3 * width),
        (scalars, seg_row, seg_col, qkv, qkv, qkv, d_att, lse, d_first, normed_self),
        late=[(8, None), (9, None)],
    )


def self_input(scalars, d_first, d_last, d_after_self, hidden, gain_rows, self_set):
    length, width = hidden.shape
    half_length = (length // 2, width)
    return call(
        self_input_kernel,
        "self_input",
        1,
        [
            pl.BlockSpec(memory_space=pltpu.SMEM),
            whole(d_first.shape),
            whole(d_last.shape),
            whole(hidden.shape),
            whole(hidden.shape),
            whole(gain_rows.shape),
            weight(width, QUERY),
            weight(width, KEY),
            weight(width, VALUE),
        ],
        [whole(half_length), whole(half_length)],
        like((half_length, F32), (half_length, F32)),
        [],
        6 * length * width * width,
        (scalars, d_first, d_last, d_after_self, hidden, gain_rows)
        + (self_set, self_set, self_set),
    )


def grid_of(chips):
    side = 1
    while 2 * side**3 < chips:
        side += 1
    return (2 * side, side, side) if 2 * side**3 == chips else (1, 1, chips)


def axis_stride(grid, axis):
    stride = 1
    for extent in grid[axis + 1 :]:
        stride *= extent
    return stride


def coordinate(grid, axis):
    return lax.axis_index("dp") // axis_stride(grid, axis) % grid[axis]


def shifted(values, grid, axis, shift):
    stride, extent = axis_stride(grid, axis), grid[axis]
    chips = grid[0] * grid[1] * grid[2]
    pairs = []
    for chip in range(chips):
        at = chip // stride % extent
        pairs.append((chip, chip + ((at + shift) % extent - at) * stride))
    return lax.ppermute(values, "dp", pairs)


def swapped(values):
    cores = lax.axis_size("seq")
    return lax.ppermute(values, "seq", [(i, (i + 1) % cores) for i in range(cores)])


def total(parts):
    result = parts[0].astype(F32)
    for part in parts[1:]:
        result = result + part.astype(F32)
    return result


def pieces_kernel(plan, *refs):
    outputs = refs[len(refs) - len(plan) :]
    at = 1
    for output, sources in zip(outputs, plan):
        for start, end, count in sources:
            value = total([refs[at + i][:, 0] for i in range(count)])
            output[:, :, :, start:end] = value.astype(BF16)
            at += count


def pieces(groups):
    outers = []
    for sources, dim, _, _ in groups:
        outer = 1
        for n in sources[0][0][0].shape[:dim]:
            outer *= n
        outers.append(outer)
    steps = 1 if any(outer % 2 for outer in outers) else 2
    plan, args, in_specs, out_specs, out_shape, finals, all_places = [], [], [], [], [], [], []
    size = 0
    for (sources, dim, places, (share, shares)), outer in zip(groups, outers):
        shape = sources[0][0][0].shape
        before, extent, after = shape[:dim], shape[dim], shape[dim + 1 : -2]
        rows = shape[-2] // shares
        inner = 1
        for n in after:
            inner *= n
        lead = outer // steps
        for place in places:
            width, spans = 0, []
            for parts, columns_, block in sources:
                spans.append((width, width + columns_, len(parts)))
                width += columns_
                for part in parts:
                    args.append(part.reshape(outer, extent, inner, *part.shape[-2:]))
                    in_specs.append(
                        pl.BlockSpec(
                            (lead, 1, inner, rows, columns_),
                            lambda g, at, o=len(all_places), share=share, block=block: (
                                g,
                                at[o],
                                0,
                                share,
                                block,
                            ),
                        )
                    )
                    size += outer * inner * rows * columns_
            plan.append(spans)
            all_places.append(place)
            out_specs.append(
                pl.BlockSpec((lead, inner, rows, width), lambda g, at: (g, 0, 0, 0))
            )
            out_shape.append(jax.ShapeDtypeStruct((outer, inner, rows, width), BF16))
            finals.append(before + after + (rows, width))
            size += outer * inner * rows * width
    result = pl.pallas_call(
        functools.partial(pieces_kernel, plan),
        grid_spec=pltpu.PrefetchScalarGridSpec(
            num_scalar_prefetch=1, grid=(steps,), in_specs=in_specs, out_specs=out_specs
        ),
        out_shape=out_shape,
        compiler_params=pltpu.CompilerParams(
            dimension_semantics=("arbitrary",), vmem_limit_bytes=max(16 << 20, 6 * size)
        ),
        cost_estimate=pl.CostEstimate(flops=0, bytes_accessed=2 * size, transcendentals=0),
        name="pieces",
    )(jnp.stack(all_places).astype(jnp.int32), *args)
    return [r.reshape(final) for r, final in zip(result, finals)]


def scattered(grid, *groups):
    wanted = []
    for sources, axis, dim, share in groups:
        here, extent = coordinate(grid, axis), grid[axis]
        wanted.append((sources, dim, [(here + shift) % extent for shift in range(extent)], share))
    taken = pieces(wanted)
    results = []
    for _, axis, _, _ in groups:
        own, *others = taken[: grid[axis]]
        taken = taken[grid[axis] :]
        results.append(
            [own]
            + [shifted(other, grid, axis, shift) for shift, other in enumerate(others, start=1)]
        )
    return results


def assemble_kernel(count, chips, *refs):
    inputs, (weights, gains) = refs[: 2 * 2 * count], refs[2 * 2 * count :]
    core = chips[chips.shape[0] - 1]
    width = weights.shape[-1]
    for which in range(2):
        place = core if which == 0 else 1 - core
        at = 0
        for number in range(2 * count):
            source = inputs[which * 2 * count + number]
            second = number >= count
            for i in range(source.shape[0]):
                for k in range(source.shape[1]):
                    chip = chips[at]
                    at += 1
                    if second:
                        weights[2 + place, chip] = source[i, k, :, :width]
                        if which == 0 and gains is not None:
                            gains[chip] = source[i, k, :, width:]
                    else:
                        weights[place, chip] = source[i, k]


def along(values, grid, axis):
    return [values] + [shifted(values, grid, axis, shift) for shift in range(1, grid[axis])]


def pack_kernel(core, gains, *refs):
    packed = refs[-1]
    width = refs[0].shape[1]
    for which in range(2):

        @pl.when(core[0] == which)
        def _(which=which):
            at = 0
            for number in range(4):
                packed[:, at : at + width] = refs[2 * number + which][...]
                at += width
                if number == 1:
                    packed[:, at : at + LANES] = gains[...]
                    at += LANES


def pack(core, gains, pairs):
    rows, width = pairs[0][0].shape
    in_vmem = pl.BlockSpec(memory_space=pltpu.VMEM)
    return pl.pallas_call(
        pack_kernel,
        in_specs=[pl.BlockSpec(memory_space=pltpu.SMEM)] + [in_vmem] * 9,
        out_specs=in_vmem,
        out_shape=jax.ShapeDtypeStruct((rows, 4 * width + LANES), BF16),
        cost_estimate=pl.CostEstimate(
            flops=0, bytes_accessed=24 * rows * width, transcendentals=0
        ),
        name="pack",
    )(core.astype(jnp.int32)[None], gains, *[matrix for pair in pairs for matrix in pair])


def gather_z(packed, widths, grid):
    every = along(packed, grid, 0)
    stacked, at = [], 0
    for columns_ in widths:
        end = at + columns_
        stacked.append(jnp.stack([values[:, at:end] for values in every]))
        at = end
    return stacked


def gather_near(first, second, grid):
    return jnp.stack(along(first, grid, 1)), jnp.stack(along(second, grid, 2))


def gather_far(first, second, grid):
    return along(first, grid, 2), along(second, grid, 1)


def gather_end(mine, other, grid):
    first_sets, second_sets = mine
    mine, other = first_sets + second_sets, other[0] + other[1]
    rows, width = first_sets[0].shape[-2:]
    chips = grid[0] * grid[1] * grid[2]
    here = [coordinate(grid, axis) for axis in range(3)]
    places = []
    for outer, inner in ((2, 1), (1, 2)):
        for far in range(grid[outer]):
            for near in range(grid[inner]):
                for deep in range(grid[0]):
                    at = [None, None, None]
                    at[outer] = (here[outer] - far) % grid[outer]
                    at[inner] = (here[inner] - near) % grid[inner]
                    at[0] = (here[0] - deep) % grid[0]
                    places.append((at[0] * grid[1] + at[1]) * grid[2] + at[2])
    places.append(lax.axis_index("seq"))
    assert len(first_sets) == len(second_sets)
    extra = second_sets[0].shape[-1] - width
    out_shape = [pltpu.HBM((4, chips, rows, width), BF16)]
    if extra:
        out_shape.append(pltpu.HBM((chips, rows, extra), BF16))
    in_vmem = pl.BlockSpec(memory_space=pltpu.VMEM)

    def kernel(places, *refs):
        assemble_kernel(len(first_sets), places, *(refs if extra else refs + (None,)))

    result = pl.pallas_call(
        kernel,
        in_specs=[pl.BlockSpec(memory_space=pltpu.SMEM)] + [in_vmem] * (2 * len(mine)),
        out_specs=[in_vmem] * len(out_shape),
        out_shape=out_shape,
        compiler_params=pltpu.CompilerParams(vmem_limit_bytes=48 << 20),
        cost_estimate=pl.CostEstimate(
            flops=0, bytes_accessed=16 * chips * rows * width, transcendentals=0
        ),
        name="assemble",
    )(jnp.stack(places).astype(jnp.int32), *mine, *other)
    weights = result[0].reshape(4, chips * rows, width)
    return weights, result[1].reshape(chips * rows, extra) if extra else None


def on_device(
    hidden_in,
    encoder_out,
    segment_ids,
    passage_counts,
    cotangent,
    w_query,
    w_key,
    w_value,
    w_out,
    w_cross_query,
    w_cross_key,
    w_cross_value,
    w_cross_out,
    w_ffn_in,
    w_ffn_out,
    gain_self,
    gain_cross,
    gain_ffn,
):
    cores = lax.axis_size("seq")
    core = lax.axis_index("seq")
    chips = lax.axis_size("dp")
    grid = grid_of(chips)
    width = hidden_in.shape[-1]
    half = width // 2
    ratio = w_ffn_in.shape[1] // width
    rows = w_query.shape[0]
    joint = ("dp", "seq")

    def own_rows(values):
        part = values.shape[0] // cores
        return lax.dynamic_slice_in_dim(values, core * part, part, 0)

    def in_order(mine, other, axis):
        first = jnp.where(core == 0, mine, other)
        second = jnp.where(core == 0, other, mine)
        return jnp.concatenate([first, second], axis=axis)

    ffn_in_rows = jnp.concatenate(
        [w_ffn_in[:, i * width : (i + 1) * width] for i in range(ratio)], axis=0
    )
    ffn_rows = own_rows(jnp.concatenate([ffn_in_rows, w_ffn_out], axis=1))
    gains = jnp.stack([gain_self, gain_cross, gain_ffn], axis=1)
    gains = jnp.pad(gains, ((0, 0), (0, LANES - gains.shape[1])))

    def tied(value, others):
        return lax.optimization_barrier((value, others))

    def sent(values):
        return swapped(lax.dynamic_index_in_dim(values, 1 - core, 0, keepdims=False))

    def returned(mine, theirs):
        return in_order(mine[None, None], theirs[None, None], 0)

    def exchanged(sets):
        return tuple([swapped(values) for values in one] for one in sets)

    hidden_both, encoded_both, branch_both = hidden_in[:, 0], encoder_out[:, 0], cotangent[:, 0]
    hidden_theirs, encoded_theirs, branch_theirs = (
        sent(hidden_both),
        sent(encoded_both),
        sent(branch_both),
    )
    segments = in_order(
        lax.dynamic_index_in_dim(segment_ids[:, 0], core, 0, keepdims=False),
        sent(segment_ids[:, 0]),
        0,
    )
    count = lax.dynamic_index_in_dim(passage_counts[:, 0], core, 0, keepdims=False)
    scalars = jnp.stack([count, core.astype(jnp.int32)])
    seg_row = segments[None, :]
    seg_col = segments[:, None]

    packed = pack(
        core,
        gains,
        [
            (w_query, w_value),
            (w_key, w_out),
            (w_cross_key, w_cross_query),
            (w_cross_value, w_cross_out),
        ],
    )
    stacked = gather_z(packed, (width, width + LANES, width, width), grid)
    self_rows, cross_rows = stacked[:2], stacked[2:]
    ffn_rows, self_rows = tied(ffn_rows, self_rows)
    ffn_set = lax.all_gather(ffn_rows, joint, axis=0, tiled=True)
    self_rows = gather_near(*self_rows, grid)
    self_near = [[values] for values in self_rows]
    self_far = [values[1:] for values in gather_far(*self_rows, grid)]
    self_other = exchanged(self_near)
    self_far, _ = tied(self_far, (self_other, scalars, seg_row, seg_col, hidden_theirs))
    cross_rows, self_far = tied(cross_rows, self_far)
    self_set, gains = gather_end(
        [near + far for near, far in zip(self_near, self_far)],
        [near + far for near, far in zip(self_other, exchanged(self_far))],
        grid,
    )
    cross_rows = along(cross_rows[0], grid, 1), along(cross_rows[1], grid, 2)

    w_in = ffn_set.reshape(chips, ratio, rows, 2 * width)
    if rows % 16:
        w_in = w_in[:, :, :, :width].transpose(1, 0, 2, 3).reshape(1, ratio, width, width)

    hidden, normed_self, qkv, gain_rows = project(
        scalars, hidden_both, hidden_theirs, gains, self_set
    )
    cross_rows, qkv = tied(cross_rows, qkv)
    cross_rows = [jnp.stack(values) for values in cross_rows]
    cross_near = [[values] for values in cross_rows]
    cross_far = [values[1:] for values in gather_far(*cross_rows, grid)]
    cross_other = exchanged(cross_near)
    qkv, (cross_near, cross_other) = tied(qkv, (cross_near, cross_other))
    attended, self_lse, after_self, normed_cross = self_forward(
        qkv, seg_row, seg_col, hidden, gain_rows, self_set
    )
    normed_cross, cross_far = tied(normed_cross, cross_far)
    cross_set, _ = gather_end(
        [near + far for near, far in zip(cross_near, cross_far)],
        [near + far for near, far in zip(cross_other, exchanged(cross_far))],
        grid,
    )
    encoded, ckv, cross_queries = project_cross(
        scalars, encoded_both, encoded_theirs, normed_cross, cross_set
    )
    cross_attended, cross_lse, after_cross, normed_ffn = cross_forward(
        cross_queries, ckv, scalars, after_self, gain_rows, cross_set
    )
    out_mine, out_theirs, d_after_cross, grad_in, kept_out, sent_out = feed_forward(
        scalars, normed_ffn, branch_both, branch_theirs, after_cross, gain_rows, ffn_set, w_in
    )
    grad_in = lax.psum_scatter(grad_in, joint, scatter_dimension=0, tiled=True)

    def by_chip(values):
        return values.reshape(grid + (-1, values.shape[-1]))

    def pair_parts(kept, sent):
        return [by_chip(kept), by_chip(swapped(sent))]

    def whole_source(parts):
        return (parts, parts[0].shape[-1], 0)

    every = (0, 1)

    def along_first(first, second, first_share=every, second_share=every):
        return scattered(grid, (first, 2, 2, first_share), (second, 1, 1, second_share))

    def along_second(first, second):
        return scattered(
            grid, ([whole_source(first)], 1, 1, every), ([whole_source(second)], 2, 1, every)
        )

    def along_z(first, second):
        return scattered(grid, ([whole_source(first), whole_source(second)], 0, 0, every))[0]

    ffn_out = pair_parts(kept_out, sent_out)
    d_att = cross_branch(d_after_cross, cross_set)
    d_att, ffn_out = tied(d_att, ffn_out)
    by_rows = ratio * rows // 2 % 16 == 0
    if by_rows:
        ffn_first, ffn_second = along_first(
            [(ffn_out, half, 0)], [(ffn_out, half, 0)], (0, 2), (1, 2)
        )
    else:
        ffn_first, ffn_second = along_first(
            [(ffn_out, 2 * LANES, 0)], [(ffn_out, half - 2 * LANES, 2)]
        )
    d_att, _ = tied(d_att, (ffn_first[0], ffn_second[0]))
    d_after_self, d_att, kept_c, sent_c, encoded_mine, encoded_their = cross_backward(
        scalars,
        cross_queries,
        ckv,
        d_att,
        cross_lse,
        d_after_cross,
        after_self,
        normed_cross,
        cross_attended,
        attended,
        encoded,
        gain_rows,
        cross_set,
        self_set,
    )
    d_att, (ffn_first, ffn_second) = tied(d_att, (ffn_first, ffn_second))
    ffn_first, ffn_second = along_second(ffn_first, ffn_second)
    d_att, _ = tied(d_att, (ffn_first[0], ffn_second[0]))
    cross_all = pair_parts(kept_c, sent_c)
    d_first = self_backward_first(seg_row, seg_col, qkv, d_att, self_lse)
    out_theirs, encoded_their = swapped(out_theirs), swapped(encoded_their)
    d_first, (ffn_first, ffn_second, cross_all, out_theirs, encoded_their) = tied(
        d_first, (ffn_first, ffn_second, cross_all, out_theirs, encoded_their)
    )
    cross_first, cross_second = along_first(
        [(cross_all, half, 3), (cross_all, half, 0), (cross_all, half, 4)],
        [(cross_all, half, 1), (cross_all, half, 2)],
    )
    ffn_parts = along_z(ffn_first, ffn_second)
    d_first, _ = tied(d_first, (ffn_parts[0], cross_first[0], cross_second[0]))
    *self_grads, d_last = self_backward_last(
        scalars, seg_row, seg_col, qkv, d_att, self_lse, d_first, normed_self
    )
    self_grads, ffn_parts = tied(self_grads, ffn_parts)
    self_qkv = [pair_parts(self_grads[i], self_grads[3 + i]) for i in range(3)]
    d_last, (cross_first, cross_second) = tied(d_last, (cross_first, cross_second))
    cross_first, cross_second = along_second(cross_first, cross_second)
    self_qkv, _ = tied(self_qkv, (cross_first[0], cross_second[0]))
    self_first, self_second = along_first(
        [(self_qkv[0], half, 0), (self_qkv[2], 2 * LANES, 0)],
        [(self_qkv[1], half, 0), (self_qkv[2], half - 2 * LANES, 2)],
    )
    d_last, _ = tied(d_last, (self_first[0], self_second[0]))
    hidden_mine, hidden_their = self_input(
        scalars, d_first, d_last, d_after_self, hidden, gain_rows, self_set
    )
    def matrices(mine, places):
        other = swapped(mine)
        results = []
        for spans in places:
            halves = [
                jnp.concatenate([values[:, start:end] for start, end in spans], axis=1)
                for values in (mine, other)
            ]
            results.append(in_order(*halves, 1))
        return results

    def gain_gradient(gain, *pairs):
        weighed = [weight_rows.astype(F32) * grad for weight_rows, grad in pairs]
        return jnp.sum(total(weighed), axis=1) / gain.astype(F32)

    hidden_their, (self_first, self_second, cross_first, cross_second) = tied(
        hidden_their, (self_first, self_second, cross_first, cross_second)
    )
    ffn_sum = total(ffn_parts)
    if by_rows:
        ffn_sum = jnp.concatenate([ffn_sum[:, :half], ffn_sum[:, half:]], axis=0)
    (grad_ffn_out,) = matrices(ffn_sum, [[(0, half)]])
    (cross_first, cross_second), grad_ffn_out = tied((cross_first, cross_second), grad_ffn_out)
    cross_parts = along_z(cross_first, cross_second)
    (self_first, self_second), _ = tied((self_first, self_second), cross_parts[0])
    self_first, self_second = along_second(self_first, self_second)
    (cross_parts, hidden_their, grad_in), _ = tied(
        (cross_parts, hidden_their, grad_in), (self_first[0], self_second[0])
    )
    self_parts = along_z(self_first, self_second)
    cross_grads = matrices(total(cross_parts), [[(i * half, (i + 1) * half)] for i in range(5)])
    grad_co, grad_cq, grad_o, grad_ck, grad_cv = cross_grads
    grad_in = lax.all_gather(grad_in, "seq", axis=0, tiled=True).astype(F32)
    done = (
        returned(out_mine, out_theirs),
        returned(hidden_mine, swapped(hidden_their)),
        returned(encoded_mine, encoded_their),
        gain_gradient(gain_cross, (w_cross_query, grad_cq)),
        gain_gradient(gain_ffn, (w_ffn_in, grad_in)),
    )
    self_parts, (done, cross_grads, grad_in) = tied(self_parts, (done, cross_grads, grad_in))
    grad_co, grad_cq, grad_o, grad_ck, grad_cv = cross_grads
    split = half + 2 * LANES
    grad_q, grad_k, grad_v = matrices(
        total(self_parts),
        [
            [(0, half)],
            [(split, split + half)],
            [(half, split), (split + half, 3 * half)],
        ],
    )
    return done[:3] + (
        grad_q,
        grad_k,
        grad_v,
        grad_o,
        grad_cq,
        grad_ck,
        grad_cv,
        grad_co,
        grad_in,
        grad_ffn_out,
        gain_gradient(gain_self, (w_query, grad_q), (w_key, grad_k), (w_value, grad_v)),
    ) + done[3:]


def solution(mesh):
    tokens = P(None, "dp", "seq", None)
    rows = P("dp", None)
    gain = P("dp")
    return jax.shard_map(
        on_device,
        mesh=mesh,
        in_specs=(tokens, tokens, P(None, "dp", "seq"), P(None, "dp"), tokens)
        + (rows,) * 10
        + (gain,) * 3,
        out_specs=(tokens,) * 3 + (rows,) * 10 + (gain,) * 3,
        check_vma=False,
    )
```

```python
import functools

import jax
import jax.numpy as jnp
from jax import lax
from jax.experimental import pallas as pl
from jax.experimental.pallas import tpu as pltpu
from jax.sharding import PartitionSpec as P

HEAD_DIM = 64
LANES = 128
SEGMENT_LIMIT = 384
SELF_BLOCK = 256
CROSS_BLOCK = 768
EPS = 1e-06
NEG = -1e30
GELU_RATE = 0.7978845608
GELU_CUBIC = 0.044715
QUERY, VALUE, KEY, OUT = range(4)
CROSS_KEY, CROSS_QUERY, CROSS_VALUE, CROSS_OUT = range(4)
BF16 = jnp.bfloat16
F32 = jnp.float32


def product(left, right):
    return jnp.dot(left, right, preferred_element_type=F32)


def row_outer(left, right):
    return lax.dot_general(left, right, (((0,), (0,)), ((), ())), preferred_element_type=F32)


def right_transposed(left, right):
    return lax.dot_general(left, right, (((1,), (1,)), ((), ())), preferred_element_type=F32)


def inverse_rms(values):
    return lax.rsqrt(jnp.mean(values * values, axis=-1, keepdims=True) + EPS)


def norm_backward(values, scale, gain, d_normed):
    scaled = gain * d_normed
    d_values = scale * scaled - values * (scale * scale * scale) * jnp.mean(
        values * scaled, axis=-1, keepdims=True
    )
    return d_values


def self_blocks(length):
    blocks = []
    for start in range(0, length, SELF_BLOCK):
        end = min(start + SELF_BLOCK, length)
        first = max(0, start - SEGMENT_LIMIT + 1) // LANES * LANES
        blocks.append((start, end, first, end))
    return blocks


def cross_blocks(length, keys):
    return [
        (start, min(start + CROSS_BLOCK, length), 0, keys)
        for start in range(0, length, CROSS_BLOCK)
    ]


def of_head(values, head):
    lanes = lax.broadcasted_iota(jnp.int32, values.shape, 1)
    return jnp.where(lanes // HEAD_DIM == head, values, jnp.zeros_like(values))


def ahead(first_step, items):
    coming = first_step(*items[0])
    for at, item in enumerate(items):
        result = coming
        if at + 1 < len(items):
            coming = first_step(*items[at + 1])
        yield item, result


def pair_forward(blocks, bias_of, q_ref, k_ref, v_ref, o_ref, lse_ref, lse_cols):
    pair = pl.program_id(0)
    lane = lax.broadcasted_iota(jnp.int32, (1, LANES), 1)

    def scores_of(block, head):
        start, end, first, last = block
        query_head = of_head(q_ref[start:end, :], head)
        return right_transposed(query_head, k_ref[first:last, :]) + bias_of(*block)

    mixed = []
    items = [(block, head) for block in blocks for head in range(2)]
    for ((start, end, first, last), head), scores in ahead(scores_of, items):
        row_max = jnp.max(scores, axis=-1, keepdims=True)
        exponents = jnp.exp(scores - row_max)
        totals = jnp.sum(exponents, axis=-1, keepdims=True)
        mixed.append(product(exponents.astype(BF16), v_ref[first:last, :]) / totals)
        lse_cols[start:end, :] = jnp.where(
            lane == 2 * pair + head, row_max + jnp.log(totals), lse_cols[start:end, :]
        )
        if head == 1:
            o_ref[start:end, :] = jnp.where(lane < HEAD_DIM, mixed[-2], mixed[-1]).astype(BF16)

    @pl.when(pair == pl.num_programs(0) - 1)
    def _():
        lse_ref[...] = jnp.transpose(lse_cols[...])[: lse_ref.shape[0], :]


def pair_backward(
    blocks, bias_of, q_ref, k_ref, v_ref, d_ref, lse_ref, dk_acc, dv_acc, first_pair=0
):
    pair = first_pair + pl.program_id(0)

    def products_of(block, head):
        start, end, first, last = block
        query_head = of_head(q_ref[start:end, :], head)
        d_head = of_head(d_ref[start:end, :], head)
        scores = right_transposed(k_ref[first:last, :], query_head)
        d_probs = right_transposed(v_ref[first:last, :], d_head)
        return query_head, d_head, scores, d_probs

    dk_acc[...] = jnp.zeros_like(dk_acc)
    dv_acc[...] = jnp.zeros_like(dv_acc)
    d_queries, rows = [], []
    items = [(block, head) for block in blocks for head in range(2)]
    for (block, head), (query_head, d_head, scores, d_probs) in ahead(products_of, items):
        start, end, first, last = block
        log_totals = lse_ref[pl.ds(2 * pair + head, 1), start:end]
        exact = jnp.exp(scores + (bias_of(*block) - log_totals))
        inner = jnp.sum(exact * d_probs, axis=0, keepdims=True)
        d_scores = (exact * (d_probs - inner)).astype(BF16)
        dv_acc[first:last, :] += product(exact.astype(BF16), d_head)
        dk_acc[first:last, :] += product(d_scores, query_head)
        rows.append(row_outer(d_scores, of_head(k_ref[first:last, :], head)))
        if head == 1:
            d_queries.append((start, end, rows[-2] + rows[-1]))
    return d_queries


def store_halves(core, kept, sent, place, value):
    half = value.shape[-1] // 2
    there = slice(place, place + half)

    @pl.when(core == 0)
    def _():
        kept[..., there] = value[..., :half]
        sent[..., there] = value[..., half:]

    @pl.when(core != 0)
    def _():
        kept[..., there] = value[..., half:]
        sent[..., there] = value[..., :half]


def store_rows(core, mine, theirs, value):
    length = mine.shape[0]

    @pl.when(core == 0)
    def _():
        mine[...] = value[:length, :]
        theirs[...] = value[length:, :]

    @pl.when(core != 0)
    def _():
        mine[...] = value[length:, :]
        theirs[...] = value[:length, :]


def masked_bias(seg_col, seg_row, keys_first):
    shape = (seg_col.shape[0], seg_row.shape[1])
    rows = lax.broadcasted_iota(jnp.int32, shape, 0)
    lanes = lax.broadcasted_iota(jnp.int32, shape, 1)
    ordered = rows <= lanes if keys_first else lanes <= rows
    return jnp.where(ordered & (seg_col[...] == seg_row[...]), 0.0, NEG)


def put_together(core, both, theirs, whole_rows):
    length = theirs.shape[0]

    @pl.when(core == 0)
    def _():
        whole_rows[:length, :] = both[0]
        whole_rows[length:, :] = theirs[...]

    @pl.when(core != 0)
    def _():
        whole_rows[:length, :] = theirs[...]
        whole_rows[length:, :] = both[1]


def project_kernel(scalars, both, theirs, gains, weight, hidden, normed, qkv, gain_rows):
    @pl.when(pl.program_id(0) == 0)
    def _():
        put_together(scalars[1], both, theirs, hidden)
        rows = jnp.transpose(gains[...].astype(F32))[: gain_rows.shape[0], :]
        gain_rows[...] = rows
        values = hidden[...].astype(F32)
        normed[...] = (values * inverse_rms(values) * rows[0:1, :]).astype(BF16)

    qkv[...] = product(normed[...], weight[...]).astype(BF16)


def project_cross_kernel(
    scalars, both, theirs, normed_cross, weight, encoded, ckv, cross_queries
):
    step = pl.program_id(0)

    @pl.when(step == 0)
    def _():
        put_together(scalars[1], both, theirs, encoded)

    @pl.when(step == 1)
    def _():
        cross_queries[...] = product(normed_cross[...], weight[...]).astype(BF16)

    @pl.when(step != 1)
    def _():
        ckv[...] = product(encoded[...], weight[...]).astype(BF16)


def self_forward_kernel(
    blocks,
    seg_row,
    seg_col,
    hidden,
    gain_rows,
    q_ref,
    k_ref,
    v_ref,
    w_o,
    attended,
    lse_ref,
    after_self,
    normed_cross,
    bias,
    lse_cols,
    mixed,
):
    @pl.when(pl.program_id(0) == 0)
    def _():
        bias[...] = masked_bias(seg_col, seg_row, False)
        lse_cols[...] = jnp.zeros_like(lse_cols)

    pair_forward(
        blocks,
        lambda start, end, first, last: bias[start:end, first:last],
        q_ref,
        k_ref,
        v_ref,
        mixed,
        lse_ref,
        lse_cols,
    )
    place = pl.multiple_of(pl.program_id(0) * LANES, LANES)
    attended[:, pl.ds(place, LANES)] = mixed[...]

    @pl.when(pl.program_id(0) == pl.num_programs(0) - 1)
    def _():
        values = hidden[...].astype(F32) + product(attended[...], w_o[...])
        after_self[...] = values
        normed_cross[...] = (values * inverse_rms(values) * gain_rows[1:2, :]).astype(BF16)


def cross_forward_kernel(
    blocks,
    count,
    after_self,
    gain_rows,
    q_ref,
    k_ref,
    v_ref,
    w_co,
    attended,
    lse_ref,
    after_cross,
    normed_ffn,
    lse_cols,
    mixed,
):
    @pl.when(pl.program_id(0) == 0)
    def _():
        lse_cols[...] = jnp.zeros_like(lse_cols)

    places = lax.broadcasted_iota(jnp.int32, (1, k_ref.shape[0]), 1)
    bias = jnp.where(places < count[0], 0.0, NEG)
    pair_forward(
        blocks,
        lambda start, end, first, last: bias,
        q_ref,
        k_ref,
        v_ref,
        mixed,
        lse_ref,
        lse_cols,
    )
    place = pl.multiple_of(pl.program_id(0) * LANES, LANES)
    attended[:, pl.ds(place, LANES)] = mixed[...]

    @pl.when(pl.program_id(0) == pl.num_programs(0) - 1)
    def _():
        values = after_self[...] + product(attended[...], w_co[...])
        after_cross[...] = values
        normed_ffn[...] = (values * inverse_rms(values) * gain_rows[2:3, :]).astype(BF16)


def ffn_kernel(
    scalars,
    normed,
    both,
    theirs,
    after_cross,
    gain_rows,
    w_in,
    w_out,
    out_mine,
    out_theirs,
    d_after_cross,
    grad_in,
    kept_out,
    sent_out,
    out_acc,
    dn_acc,
    normed_t,
    branch,
):
    step = pl.program_id(0)

    @pl.when(step == 0)
    def _():
        put_together(scalars[1], both, theirs, branch)
        normed_t[...] = jnp.transpose(normed[...])
        out_acc[...] = jnp.zeros_like(out_acc)
        dn_acc[...] = jnp.zeros_like(dn_acc)

    width = normed.shape[1]
    up = w_in[...].reshape(width, -1)
    down = w_out[...]
    pre = product(normed[...], up)
    d_act = right_transposed(branch[...], down)
    bent = jnp.tanh(GELU_RATE * (pre + GELU_CUBIC * pre * pre * pre))
    half = 0.5 * (1.0 + bent)
    hidden_act = (pre * half).astype(BF16)
    slope = half + 0.5 * pre * (1.0 - bent * bent) * GELU_RATE * (
        1.0 + 3.0 * GELU_CUBIC * pre * pre
    )
    out_acc[...] += product(hidden_act, down)
    d_pre = (d_act * slope).astype(BF16)
    grad_out = row_outer(hidden_act, branch[...]).astype(BF16)
    store_halves(scalars[1], kept_out, sent_out, 0, grad_out)
    grad_in[...] = product(normed_t[...], d_pre).astype(BF16)
    dn_acc[...] += right_transposed(d_pre, up)

    @pl.when(step == pl.num_programs(0) - 1)
    def _():
        values = after_cross[...]
        store_rows(scalars[1], out_mine, out_theirs, (values + out_acc[...]).astype(BF16))
        d_values = norm_backward(values, inverse_rms(values), gain_rows[2:3, :], dn_acc[...])
        d_after_cross[...] = branch[...].astype(F32) + d_values


def attended_gradient(branch, w_out, d_att):
    d_mixed = right_transposed(branch, w_out[...]).astype(BF16)
    for pair in range(d_att.shape[0]):
        d_att[pair] = d_mixed[:, pair * LANES : (pair + 1) * LANES]


def cross_branch_kernel(d_after, w_out, d_att):
    attended_gradient(d_after[...].astype(BF16), w_out, d_att)


def cross_backward_kernel(
    blocks,
    scalars,
    q_ref,
    k_ref,
    v_ref,
    d_att,
    lse_ref,
    d_after_cross,
    after_self,
    normed_cross,
    cross_attended,
    self_attended,
    encoded,
    gain_rows,
    w_cq,
    w_ck,
    w_cv,
    w_o,
    d_after_self,
    d_att_self,
    kept,
    sent,
    encoded_mine,
    encoded_theirs,
    dq_all,
    dkv_all,
    dk_acc,
    dv_acc,
):
    step = pl.program_id(0)
    width = d_after_cross.shape[1]
    half = width // 2
    places = lax.broadcasted_iota(jnp.int32, (k_ref.shape[0], 1), 0)
    bias = jnp.where(places < scalars[0], 0.0, NEG)
    d_queries = pair_backward(
        blocks,
        lambda start, end, first, last: bias,
        q_ref,
        k_ref,
        v_ref,
        d_att.at[0],
        lse_ref,
        dk_acc,
        dv_acc,
    )
    place = pl.multiple_of(step * LANES, LANES)
    for start, end, d_query in d_queries:
        dq_all[start:end, pl.ds(place, LANES)] = d_query.astype(BF16)
    dkv_all[:, pl.ds(place, LANES)] = dk_acc[...].astype(BF16)
    dkv_all[:, pl.ds(width + place, LANES)] = dv_acc[...].astype(BF16)

    @pl.when(step == pl.num_programs(0) - 1)
    def _():
        dq = dq_all[...]
        grad_query = row_outer(normed_cross[...], dq).astype(BF16)
        grad_kv = row_outer(encoded[...], dkv_all[...]).astype(BF16)
        store_halves(scalars[1], kept, sent, 0, grad_query)
        store_halves(scalars[1], kept, sent, half, grad_kv[:, :width])
        store_halves(scalars[1], kept, sent, 2 * half, grad_kv[:, width:])
        grad_out = row_outer(cross_attended[...], d_after_cross[...].astype(BF16))
        store_halves(scalars[1], kept, sent, 3 * half, grad_out.astype(BF16))
        grad_encoded = right_transposed(dkv_all[:, :width], w_ck[...]) + right_transposed(
            dkv_all[:, width:], w_cv[...]
        )
        store_rows(scalars[1], encoded_mine, encoded_theirs, grad_encoded)
        values = after_self[...]
        d_values = norm_backward(
            values,
            inverse_rms(values),
            gain_rows[1:2, :],
            right_transposed(dq, w_cq[...]),
        )
        d_values = d_after_cross[...] + d_values
        d_after_self[...] = d_values
        branch = d_values.astype(BF16)
        attended_gradient(branch, w_o, d_att_self)
        grad_out = row_outer(self_attended[...], branch)
        store_halves(scalars[1], kept, sent, 4 * half, grad_out.astype(BF16))


def self_backward_pairs(
    blocks, seg_row, seg_col, q_ref, k_ref, v_ref, d_att, lse_ref, d_all, bias, dk_acc, dv_acc, first
):
    @pl.when(pl.program_id(0) == 0)
    def _():
        bias[...] = masked_bias(seg_col, seg_row, True)

    d_queries = pair_backward(
        blocks,
        lambda start, end, first_key, last_key: bias[first_key:last_key, start:end],
        q_ref,
        k_ref,
        v_ref,
        d_att.at[0],
        lse_ref,
        dk_acc,
        dv_acc,
        first,
    )
    place = pl.multiple_of(pl.program_id(0) * LANES, LANES)
    for start, end, d_query in d_queries:
        d_all[0, start:end, pl.ds(place, LANES)] = d_query.astype(BF16)
    d_all[1, :, pl.ds(place, LANES)] = dk_acc[...].astype(BF16)
    d_all[2, :, pl.ds(place, LANES)] = dv_acc[...].astype(BF16)


def self_backward_first_kernel(
    blocks, seg_row, seg_col, q_ref, k_ref, v_ref, d_att, lse_ref, d_all, bias, dk_acc, dv_acc
):
    self_backward_pairs(
        blocks, seg_row, seg_col, q_ref, k_ref, v_ref, d_att, lse_ref, d_all, bias, dk_acc, dv_acc, 0
    )


def self_backward_last_kernel(
    blocks,
    first,
    scalars,
    seg_row,
    seg_col,
    q_ref,
    k_ref,
    v_ref,
    d_att,
    lse_ref,
    d_first,
    normed_self,
    kept_q,
    kept_k,
    kept_v,
    sent_q,
    sent_k,
    sent_v,
    d_last,
    bias,
    dk_acc,
    dv_acc,
):
    self_backward_pairs(
        blocks,
        seg_row,
        seg_col,
        q_ref,
        k_ref,
        v_ref,
        d_att,
        lse_ref,
        d_last,
        bias,
        dk_acc,
        dv_acc,
        first,
    )

    @pl.when(pl.program_id(0) == pl.num_programs(0) - 1)
    def _():
        normed_t = jnp.transpose(normed_self[...])
        for i, (kept, sent) in enumerate(
            ((kept_q, sent_q), (kept_k, sent_k), (kept_v, sent_v))
        ):
            grad = product(normed_t, jnp.concatenate([d_first[i], d_last[i]], axis=1))
            store_halves(scalars[1], kept, sent, 0, grad.astype(BF16))


def self_input_kernel(
    scalars,
    d_first,
    d_last,
    d_after_self,
    hidden,
    gain_rows,
    self_set,
    mine,
    theirs,
    first,
    last,
    weights,
    after,
    held,
    sems,
):
    copies = []
    for i, place in enumerate((QUERY, KEY, VALUE)):
        copies.append(pltpu.make_async_copy(d_first.at[i], first.at[i], sems.at[3 * i]))
        copies.append(pltpu.make_async_copy(d_last.at[i], last.at[i], sems.at[3 * i + 1]))
        copies.append(
            pltpu.make_async_copy(self_set.at[place], weights.at[i], sems.at[3 * i + 2])
        )
    copies.append(pltpu.make_async_copy(hidden, held, sems.at[9]))
    copies.append(pltpu.make_async_copy(d_after_self, after, sems.at[10]))
    for copy in copies:
        copy.start()
    d_normed = None
    for i in range(3):
        for copy in copies[3 * i : 3 * i + 3]:
            copy.wait()
        d_out = jnp.concatenate([first[i], last[i]], axis=1)
        part = right_transposed(d_out, weights[i])
        d_normed = part if d_normed is None else d_normed + part
    for copy in copies[9:]:
        copy.wait()
    values = held[...].astype(F32)
    d_values = norm_backward(values, inverse_rms(values), gain_rows[0:1, :], d_normed)
    store_rows(scalars[1], mine, theirs, after[...] + d_values)


def columns(rows, offset):
    return pl.BlockSpec((rows, LANES), lambda step: (0, offset + step))


def whole(shape, place=None):
    place = (0,) * len(shape) if place is None else place
    return pl.BlockSpec(shape, lambda step: place)


def like(*shapes):
    return [jax.ShapeDtypeStruct(shape, dtype) for shape, dtype in shapes]


def with_late(kernel, late, steps):
    def run(*refs):
        sems, buffers = refs[-1], refs[-1 - len(late) : -1]
        refs = list(refs[: -1 - len(late)])
        copies = []
        for at, ((number, index), buffer) in enumerate(zip(late, buffers)):
            source = refs[number] if index is None else refs[number].at[index]
            copies.append(pltpu.make_async_copy(source, buffer, sems.at[at]))
            refs[number] = buffer

        @pl.when(pl.program_id(0) == 0)
        def _():
            for copy in copies:
                copy.start()

        @pl.when(pl.program_id(0) == steps - 1)
        def _():
            for copy in copies:
                copy.wait()

        kernel(*refs)

    return run


def call(
    kernel, name, steps, in_specs, out_specs, out_shape, scratch, flops, args, grant=56, late=()
):
    size = sum(int(a.size) * a.dtype.itemsize for a in args)
    if late:
        in_specs, scratch = list(in_specs), list(scratch)
        for number, index in late:
            shape = args[number].shape if index is None else args[number].shape[1:]
            in_specs[number] = pl.BlockSpec(memory_space=pl.ANY)
            scratch.append(pltpu.VMEM(shape, args[number].dtype))
        scratch.append(pltpu.SemaphoreType.DMA((len(late),)))
        kernel = with_late(kernel, late, steps)
    return pl.pallas_call(
        kernel,
        grid=(steps,),
        in_specs=in_specs,
        out_specs=out_specs,
        out_shape=out_shape,
        scratch_shapes=scratch,
        compiler_params=pltpu.CompilerParams(
            dimension_semantics=("arbitrary",), vmem_limit_bytes=grant << 20
        ),
        cost_estimate=pl.CostEstimate(flops=flops, bytes_accessed=size, transcendentals=0),
        name=name,
    )(*args)


def weight(width, place):
    return pl.BlockSpec((None, width, width), lambda step: (place, 0, 0))


def project(scalars, both, theirs, gains, self_set):
    cores, half_length, width = both.shape
    length = cores * half_length
    shape = (length, width)
    return call(
        project_kernel,
        "project",
        3,
        [
            pl.BlockSpec(memory_space=pltpu.SMEM),
            whole(both.shape),
            whole(theirs.shape),
            whole(gains.shape),
            pl.BlockSpec((None, width, width), lambda step: (2 * step % 3, 0, 0)),
        ],
        [
            whole(shape),
            whole(shape),
            pl.BlockSpec((length, width), lambda step: (0, step)),
            whole((8, width)),
        ],
        like((shape, BF16), (shape, BF16), ((length, 3 * width), BF16), ((8, width), F32)),
        [],
        6 * length * width * width,
        (scalars, both, theirs, gains, self_set),
    )


def project_cross(scalars, both, theirs, normed_cross, cross_set):
    length, width = normed_cross.shape
    keys = both.shape[0] * both.shape[1]
    return call(
        project_cross_kernel,
        "project_cross",
        3,
        [
            pl.BlockSpec(memory_space=pltpu.SMEM),
            whole(both.shape),
            whole(theirs.shape),
            whole(normed_cross.shape),
            pl.BlockSpec((None, width, width), lambda step: (step, 0, 0)),
        ],
        [
            whole((keys, width)),
            pl.BlockSpec((keys, width), lambda step: (0, step // 2)),
            whole(normed_cross.shape),
        ],
        like(((keys, width), BF16), ((keys, 2 * width), BF16), (normed_cross.shape, BF16)),
        [],
        2 * width * width * (length + 2 * keys),
        (scalars, both, theirs, normed_cross, cross_set),
    )


def self_forward(qkv, seg_row, seg_col, hidden, gain_rows, self_set):
    length, width = hidden.shape
    pairs = width // LANES
    return call(
        functools.partial(self_forward_kernel, self_blocks(length)),
        "self_forward",
        pairs,
        [
            whole(seg_row.shape),
            whole(seg_col.shape),
            whole(hidden.shape),
            whole(gain_rows.shape),
            columns(length, 0),
            columns(length, pairs),
            columns(length, 2 * pairs),
            weight(width, OUT),
        ],
        [
            whole(hidden.shape),
            whole((16, length)),
            whole(hidden.shape),
            whole(hidden.shape),
        ],
        like(
            (hidden.shape, BF16),
            ((16, length), F32),
            (hidden.shape, F32),
            (hidden.shape, BF16),
        ),
        [
            pltpu.VMEM((length, length), F32),
            pltpu.VMEM((length, LANES), F32),
            pltpu.VMEM((length, LANES), BF16),
        ],
        4 * length * width * (length + width),
        (
            seg_row,
            seg_col,
            hidden,
            gain_rows,
            qkv,
            qkv,
            qkv,
            self_set,
        ),
    )


def cross_forward(queries, ckv, count, after_self, gain_rows, cross_set):
    length, width = queries.shape
    keys = ckv.shape[0]
    pairs = width // LANES
    return call(
        functools.partial(cross_forward_kernel, cross_blocks(length, keys)),
        "cross_forward",
        pairs,
        [
            pl.BlockSpec(memory_space=pltpu.SMEM),
            whole(queries.shape),
            whole(gain_rows.shape),
            columns(length, 0),
            columns(keys, 0),
            columns(keys, pairs),
            weight(width, CROSS_OUT),
        ],
        [
            whole(queries.shape),
            whole((16, length)),
            whole(queries.shape),
            whole(queries.shape),
        ],
        like(
            (queries.shape, BF16),
            ((16, length), F32),
            (queries.shape, F32),
            (queries.shape, BF16),
        ),
        [pltpu.VMEM((length, LANES), F32), pltpu.VMEM((length, LANES), BF16)],
        2 * length * width * (2 * keys + width),
        (count, after_self, gain_rows, queries, ckv, ckv, cross_set),
    )


def feed_forward(scalars, normed, both, theirs, after_cross, gain_rows, ffn_set, w_in):
    length, width = normed.shape
    groups, steps, rows, _ = w_in.shape
    block = pl.BlockSpec((groups, 1, rows, width), lambda step: (0, step, 0, 0))
    half_rows = pl.BlockSpec((width, width // 2), lambda step: (step, 0))
    half_out = ((steps * width, width // 2), BF16)
    half_length = (length // both.shape[0], width)
    return call(
        ffn_kernel,
        "feed_forward",
        steps,
        [
            pl.BlockSpec(memory_space=pltpu.SMEM),
            whole(normed.shape),
            whole(both.shape),
            whole(theirs.shape),
            whole(normed.shape),
            whole(gain_rows.shape),
            block,
            pl.BlockSpec((width, width), lambda step: (step, 1)),
        ],
        [
            whole(half_length),
            whole(half_length),
            whole(normed.shape),
            pl.BlockSpec((width, width), lambda step: (0, step)),
            half_rows,
            half_rows,
        ],
        like(
            (half_length, BF16),
            (half_length, BF16),
            (normed.shape, F32),
            ((width, steps * width), BF16),
            half_out,
            half_out,
        ),
        [
            pltpu.VMEM(normed.shape, F32),
            pltpu.VMEM(normed.shape, F32),
            pltpu.VMEM((width, length), BF16),
            pltpu.VMEM((length, width), BF16),
        ],
        12 * length * width * width * steps,
        (scalars, normed, both, theirs, after_cross, gain_rows, w_in, ffn_set),
        grant=56,
        late=[(4, None)],
    )


def cross_branch(d_after, cross_set):
    length, width = d_after.shape
    shape = (width // LANES, length, LANES)
    return call(
        cross_branch_kernel,
        "cross_branch",
        1,
        [whole(d_after.shape), weight(width, CROSS_OUT)],
        whole(shape),
        jax.ShapeDtypeStruct(shape, BF16),
        [],
        2 * length * width * width,
        (d_after, cross_set),
    )


def pair_block(length, first):
    return pl.BlockSpec((1, length, LANES), lambda step: (first + step, 0, 0))


def cross_backward(
    scalars,
    queries,
    ckv,
    d_att,
    lse,
    d_after_cross,
    after_self,
    normed_cross,
    cross_attended,
    self_attended,
    encoded,
    gain_rows,
    cross_set,
    self_set,
):
    length, width = queries.shape
    keys = ckv.shape[0]
    pairs = width // LANES
    halves = (width, 5 * width // 2)
    half_keys = (keys // 2, width)
    return call(
        functools.partial(cross_backward_kernel, cross_blocks(length, keys)),
        "cross_backward",
        pairs,
        [
            pl.BlockSpec(memory_space=pltpu.SMEM),
            columns(length, 0),
            columns(keys, 0),
            columns(keys, pairs),
            pair_block(length, 0),
            whole(lse.shape),
            whole(queries.shape),
            whole(queries.shape),
            whole(queries.shape),
            whole(queries.shape),
            whole(queries.shape),
            whole(encoded.shape),
            whole(gain_rows.shape),
            weight(width, CROSS_QUERY),
            weight(width, CROSS_KEY),
            weight(width, CROSS_VALUE),
            weight(width, OUT),
        ],
        [
            whole(queries.shape),
            whole((pairs, length, LANES)),
            whole(halves),
            whole(halves),
            whole(half_keys),
            whole(half_keys),
        ],
        like(
            (queries.shape, F32),
            ((pairs, length, LANES), BF16),
            (halves, BF16),
            (halves, BF16),
            (half_keys, F32),
            (half_keys, F32),
        ),
        [
            pltpu.VMEM((length, width), BF16),
            pltpu.VMEM((keys, 2 * width), BF16),
            pltpu.VMEM((keys, LANES), F32),
            pltpu.VMEM((keys, LANES), F32),
        ],
        2 * length * width * (5 * keys + 7 * width),
        (
            scalars,
            queries,
            ckv,
            ckv,
            d_att,
            lse,
            d_after_cross,
            after_self,
            normed_cross,
            cross_attended,
            self_attended,
            encoded,
            gain_rows,
            cross_set,
            cross_set,
            cross_set,
            self_set,
        ),
        late=[(number, None) for number in range(6, 12)]
        + [(13, CROSS_QUERY), (14, CROSS_KEY), (15, CROSS_VALUE), (16, OUT)],
    )


def self_backward_first(seg_row, seg_col, qkv, d_att, lse):
    length, width = qkv.shape[0], qkv.shape[1] // 3
    pairs = width // LANES
    done = pairs // 2
    return call(
        functools.partial(self_backward_first_kernel, self_blocks(length)),
        "self_backward_first",
        done,
        [
            whole(seg_row.shape),
            whole(seg_col.shape),
            columns(length, 0),
            columns(length, pairs),
            columns(length, 2 * pairs),
            pair_block(length, 0),
            whole(lse.shape),
        ],
        whole((3, length, done * LANES)),
        jax.ShapeDtypeStruct((3, length, done * LANES), BF16),
        [
            pltpu.VMEM((length, length), F32),
            pltpu.VMEM((length, LANES), F32),
            pltpu.VMEM((length, LANES), F32),
        ],
        120 * length * width * length,
        (seg_row, seg_col, qkv, qkv, qkv, d_att, lse),
    )


def self_backward_last(scalars, seg_row, seg_col, qkv, d_att, lse, d_first, normed_self):
    length, width = normed_self.shape
    pairs = width // LANES
    done = d_first.shape[2] // LANES
    halves = (width, width // 2)
    d_last = (3, length, (pairs - done) * LANES)
    return call(
        functools.partial(self_backward_last_kernel, self_blocks(length), done),
        "self_backward_last",
        pairs - done,
        [
            pl.BlockSpec(memory_space=pltpu.SMEM),
            whole(seg_row.shape),
            whole(seg_col.shape),
            columns(length, done),
            columns(length, pairs + done),
            columns(length, 2 * pairs + done),
            pair_block(length, done),
            whole(lse.shape),
            whole(d_first.shape),
            whole(normed_self.shape),
        ],
        [whole(halves)] * 6 + [whole(d_last)],
        like(*[(halves, BF16)] * 6, (d_last, BF16)),
        [
            pltpu.VMEM((length, length), F32),
            pltpu.VMEM((length, LANES), F32),
            pltpu.VMEM((length, LANES), F32),
        ],
        2 * length * width * (length + 3 * width),
        (scalars, seg_row, seg_col, qkv, qkv, qkv, d_att, lse, d_first, normed_self),
        late=[(8, None), (9, None)],
    )


def self_input(scalars, d_first, d_last, d_after_self, hidden, gain_rows, self_set):
    length, width = hidden.shape
    half_length = (length // 2, width)
    return call(
        self_input_kernel,
        "self_input",
        1,
        [pl.BlockSpec(memory_space=pltpu.SMEM)]
        + [pl.BlockSpec(memory_space=pl.ANY)] * 4
        + [whole(gain_rows.shape), pl.BlockSpec(memory_space=pl.ANY)],
        [whole(half_length), whole(half_length)],
        like((half_length, F32), (half_length, F32)),
        [
            pltpu.VMEM(d_first.shape, BF16),
            pltpu.VMEM(d_last.shape, BF16),
            pltpu.VMEM((3, width, width), BF16),
            pltpu.VMEM(hidden.shape, F32),
            pltpu.VMEM(hidden.shape, BF16),
            pltpu.SemaphoreType.DMA((11,)),
        ],
        6 * length * width * width,
        (scalars, d_first, d_last, d_after_self, hidden, gain_rows, self_set),
    )


def grid_of(chips):
    side = 1
    while 2 * side**3 < chips:
        side += 1
    return (2 * side, side, side) if 2 * side**3 == chips else (1, 1, chips)


def axis_stride(grid, axis):
    stride = 1
    for extent in grid[axis + 1 :]:
        stride *= extent
    return stride


def coordinate(grid, axis):
    return lax.axis_index("dp") // axis_stride(grid, axis) % grid[axis]


def shifted(values, grid, axis, shift):
    stride, extent = axis_stride(grid, axis), grid[axis]
    chips = grid[0] * grid[1] * grid[2]
    pairs = []
    for chip in range(chips):
        at = chip // stride % extent
        pairs.append((chip, chip + ((at + shift) % extent - at) * stride))
    return lax.ppermute(values, "dp", pairs)


def swapped(values):
    cores = lax.axis_size("seq")
    return lax.ppermute(values, "seq", [(i, (i + 1) % cores) for i in range(cores)])


def total(parts):
    result = parts[0].astype(F32)
    for part in parts[1:]:
        result = result + part.astype(F32)
    return result


def pieces_kernel(plan, *refs):
    outputs = refs[len(refs) - len(plan) :]
    at = 1
    for output, sources in zip(outputs, plan):
        for start, end, count in sources:
            value = total([refs[at + i][:, 0] for i in range(count)])
            output[:, :, :, start:end] = value.astype(BF16)
            at += count


def pieces(groups):
    outers = []
    for sources, dim, _, _ in groups:
        outer = 1
        for n in sources[0][0][0].shape[:dim]:
            outer *= n
        outers.append(outer)
    steps = 1 if any(outer % 2 for outer in outers) else 2
    plan, args, in_specs, out_specs, out_shape, finals, all_places = [], [], [], [], [], [], []
    size = 0
    for (sources, dim, places, (share, shares)), outer in zip(groups, outers):
        shape = sources[0][0][0].shape
        before, extent, after = shape[:dim], shape[dim], shape[dim + 1 : -2]
        rows = shape[-2] // shares
        inner = 1
        for n in after:
            inner *= n
        lead = outer // steps
        for place in places:
            width, spans = 0, []
            for parts, columns_, block in sources:
                spans.append((width, width + columns_, len(parts)))
                width += columns_
                for part in parts:
                    args.append(part.reshape(outer, extent, inner, *part.shape[-2:]))
                    in_specs.append(
                        pl.BlockSpec(
                            (lead, 1, inner, rows, columns_),
                            lambda g, at, o=len(all_places), share=share, block=block: (
                                g,
                                at[o],
                                0,
                                share,
                                block,
                            ),
                        )
                    )
                    size += outer * inner * rows * columns_
            plan.append(spans)
            all_places.append(place)
            out_specs.append(
                pl.BlockSpec((lead, inner, rows, width), lambda g, at: (g, 0, 0, 0))
            )
            out_shape.append(jax.ShapeDtypeStruct((outer, inner, rows, width), BF16))
            finals.append(before + after + (rows, width))
            size += outer * inner * rows * width
    result = pl.pallas_call(
        functools.partial(pieces_kernel, plan),
        grid_spec=pltpu.PrefetchScalarGridSpec(
            num_scalar_prefetch=1, grid=(steps,), in_specs=in_specs, out_specs=out_specs
        ),
        out_shape=out_shape,
        compiler_params=pltpu.CompilerParams(
            dimension_semantics=("arbitrary",), vmem_limit_bytes=max(16 << 20, 6 * size)
        ),
        cost_estimate=pl.CostEstimate(flops=0, bytes_accessed=2 * size, transcendentals=0),
        name="pieces",
    )(jnp.stack(all_places).astype(jnp.int32), *args)
    return [r.reshape(final) for r, final in zip(result, finals)]


def scattered(grid, *groups):
    wanted = []
    for sources, axis, dim, share in groups:
        here, extent = coordinate(grid, axis), grid[axis]
        wanted.append((sources, dim, [(here + shift) % extent for shift in range(extent)], share))
    taken = pieces(wanted)
    results = []
    for _, axis, _, _ in groups:
        own, *others = taken[: grid[axis]]
        taken = taken[grid[axis] :]
        results.append(
            [own]
            + [shifted(other, grid, axis, shift) for shift, other in enumerate(others, start=1)]
        )
    return results


def assemble_kernel(count, chips, *refs):
    inputs, (weights, gains) = refs[: 2 * 2 * count], refs[2 * 2 * count :]
    core = chips[chips.shape[0] - 1]
    width = weights.shape[-1]
    for which in range(2):
        place = core if which == 0 else 1 - core
        at = 0
        for number in range(2 * count):
            source = inputs[which * 2 * count + number]
            second = number >= count
            for i in range(source.shape[0]):
                for k in range(source.shape[1]):
                    chip = chips[at]
                    at += 1
                    if second:
                        weights[2 + place, chip] = source[i, k, :, :width]
                        if which == 0 and gains is not None:
                            gains[chip] = source[i, k, :, width:]
                    else:
                        weights[place, chip] = source[i, k]


def along(values, grid, axis):
    return [values] + [shifted(values, grid, axis, shift) for shift in range(1, grid[axis])]


def pack_kernel(core, gains, *refs):
    packed = refs[-1]
    width = refs[0].shape[1]
    for which in range(2):

        @pl.when(core[0] == which)
        def _(which=which):
            at = 0
            for number in range(4):
                packed[:, at : at + width] = refs[2 * number + which][...]
                at += width
                if number == 1:
                    packed[:, at : at + LANES] = gains[...]
                    at += LANES


def pack(core, gains, pairs):
    rows, width = pairs[0][0].shape
    in_vmem = pl.BlockSpec(memory_space=pltpu.VMEM)
    return pl.pallas_call(
        pack_kernel,
        in_specs=[pl.BlockSpec(memory_space=pltpu.SMEM)] + [in_vmem] * 9,
        out_specs=in_vmem,
        out_shape=jax.ShapeDtypeStruct((rows, 4 * width + LANES), BF16),
        cost_estimate=pl.CostEstimate(
            flops=0, bytes_accessed=24 * rows * width, transcendentals=0
        ),
        name="pack",
    )(core.astype(jnp.int32)[None], gains, *[matrix for pair in pairs for matrix in pair])


def gather_z(packed, widths, grid):
    every = along(packed, grid, 0)
    stacked, at = [], 0
    for columns_ in widths:
        end = at + columns_
        stacked.append(jnp.stack([values[:, at:end] for values in every]))
        at = end
    return stacked


def gather_near(first, second, grid):
    return jnp.stack(along(first, grid, 1)), jnp.stack(along(second, grid, 2))


def gather_far(first, second, grid):
    return along(first, grid, 2), along(second, grid, 1)


def gather_end(mine, other, grid):
    first_sets, second_sets = mine
    mine, other = first_sets + second_sets, other[0] + other[1]
    rows, width = first_sets[0].shape[-2:]
    chips = grid[0] * grid[1] * grid[2]
    here = [coordinate(grid, axis) for axis in range(3)]
    places = []
    for outer, inner in ((2, 1), (1, 2)):
        for far in range(grid[outer]):
            for near in range(grid[inner]):
                for deep in range(grid[0]):
                    at = [None, None, None]
                    at[outer] = (here[outer] - far) % grid[outer]
                    at[inner] = (here[inner] - near) % grid[inner]
                    at[0] = (here[0] - deep) % grid[0]
                    places.append((at[0] * grid[1] + at[1]) * grid[2] + at[2])
    places.append(lax.axis_index("seq"))
    assert len(first_sets) == len(second_sets)
    extra = second_sets[0].shape[-1] - width
    out_shape = [pltpu.HBM((4, chips, rows, width), BF16)]
    if extra:
        out_shape.append(pltpu.HBM((chips, rows, extra), BF16))
    in_vmem = pl.BlockSpec(memory_space=pltpu.VMEM)

    def kernel(places, *refs):
        assemble_kernel(len(first_sets), places, *(refs if extra else refs + (None,)))

    result = pl.pallas_call(
        kernel,
        in_specs=[pl.BlockSpec(memory_space=pltpu.SMEM)] + [in_vmem] * (2 * len(mine)),
        out_specs=[in_vmem] * len(out_shape),
        out_shape=out_shape,
        compiler_params=pltpu.CompilerParams(vmem_limit_bytes=48 << 20),
        cost_estimate=pl.CostEstimate(
            flops=0, bytes_accessed=16 * chips * rows * width, transcendentals=0
        ),
        name="assemble",
    )(jnp.stack(places).astype(jnp.int32), *mine, *other)
    weights = result[0].reshape(4, chips * rows, width)
    return weights, result[1].reshape(chips * rows, extra) if extra else None


def on_device(
    hidden_in,
    encoder_out,
    segment_ids,
    passage_counts,
    cotangent,
    w_query,
    w_key,
    w_value,
    w_out,
    w_cross_query,
    w_cross_key,
    w_cross_value,
    w_cross_out,
    w_ffn_in,
    w_ffn_out,
    gain_self,
    gain_cross,
    gain_ffn,
):
    cores = lax.axis_size("seq")
    core = lax.axis_index("seq")
    chips = lax.axis_size("dp")
    grid = grid_of(chips)
    width = hidden_in.shape[-1]
    half = width // 2
    ratio = w_ffn_in.shape[1] // width
    rows = w_query.shape[0]
    joint = ("dp", "seq")

    def own_rows(values):
        part = values.shape[0] // cores
        return lax.dynamic_slice_in_dim(values, core * part, part, 0)

    def in_order(mine, other, axis):
        first = jnp.where(core == 0, mine, other)
        second = jnp.where(core == 0, other, mine)
        return jnp.concatenate([first, second], axis=axis)

    ffn_in_rows = jnp.concatenate(
        [w_ffn_in[:, i * width : (i + 1) * width] for i in range(ratio)], axis=0
    )
    ffn_rows = own_rows(jnp.concatenate([ffn_in_rows, w_ffn_out], axis=1))
    gains = jnp.stack([gain_self, gain_cross, gain_ffn], axis=1)
    gains = jnp.pad(gains, ((0, 0), (0, LANES - gains.shape[1])))

    def tied(value, others):
        return lax.optimization_barrier((value, others))

    def sent(values):
        return swapped(lax.dynamic_index_in_dim(values, 1 - core, 0, keepdims=False))

    def returned(mine, theirs):
        return in_order(mine[None, None], theirs[None, None], 0)

    def exchanged(sets):
        return tuple([swapped(values) for values in one] for one in sets)

    hidden_both, encoded_both, branch_both = hidden_in[:, 0], encoder_out[:, 0], cotangent[:, 0]
    hidden_theirs, encoded_theirs, branch_theirs = (
        sent(hidden_both),
        sent(encoded_both),
        sent(branch_both),
    )
    segments = in_order(
        lax.dynamic_index_in_dim(segment_ids[:, 0], core, 0, keepdims=False),
        sent(segment_ids[:, 0]),
        0,
    )
    count = lax.dynamic_index_in_dim(passage_counts[:, 0], core, 0, keepdims=False)
    scalars = jnp.stack([count, core.astype(jnp.int32)])
    seg_row = segments[None, :]
    seg_col = segments[:, None]

    packed = pack(
        core,
        gains,
        [
            (w_query, w_value),
            (w_key, w_out),
            (w_cross_key, w_cross_query),
            (w_cross_value, w_cross_out),
        ],
    )
    stacked = gather_z(packed, (width, width + LANES, width, width), grid)
    self_rows, cross_rows = stacked[:2], stacked[2:]
    ffn_rows, self_rows = tied(ffn_rows, self_rows)
    ffn_set = lax.all_gather(ffn_rows, joint, axis=0, tiled=True)
    self_rows = gather_near(*self_rows, grid)
    self_near = [[values] for values in self_rows]
    self_far = [values[1:] for values in gather_far(*self_rows, grid)]
    self_other = exchanged(self_near)
    self_far, _ = tied(self_far, (self_other, scalars, seg_row, seg_col, hidden_theirs))
    cross_rows, self_far = tied(cross_rows, self_far)
    self_set, gains = gather_end(
        [near + far for near, far in zip(self_near, self_far)],
        [near + far for near, far in zip(self_other, exchanged(self_far))],
        grid,
    )
    cross_rows = along(cross_rows[0], grid, 1), along(cross_rows[1], grid, 2)

    w_in = ffn_set.reshape(chips, ratio, rows, 2 * width)
    if rows % 16:
        w_in = w_in[:, :, :, :width].transpose(1, 0, 2, 3).reshape(1, ratio, width, width)

    hidden, normed_self, qkv, gain_rows = project(
        scalars, hidden_both, hidden_theirs, gains, self_set
    )
    cross_rows, qkv = tied(cross_rows, qkv)
    cross_rows = [jnp.stack(values) for values in cross_rows]
    cross_near = [[values] for values in cross_rows]
    cross_far = [values[1:] for values in gather_far(*cross_rows, grid)]
    cross_other = exchanged(cross_near)
    qkv, (cross_near, cross_other) = tied(qkv, (cross_near, cross_other))
    attended, self_lse, after_self, normed_cross = self_forward(
        qkv, seg_row, seg_col, hidden, gain_rows, self_set
    )
    normed_cross, cross_far = tied(normed_cross, cross_far)
    cross_set, _ = gather_end(
        [near + far for near, far in zip(cross_near, cross_far)],
        [near + far for near, far in zip(cross_other, exchanged(cross_far))],
        grid,
    )
    encoded, ckv, cross_queries = project_cross(
        scalars, encoded_both, encoded_theirs, normed_cross, cross_set
    )
    cross_attended, cross_lse, after_cross, normed_ffn = cross_forward(
        cross_queries, ckv, scalars, after_self, gain_rows, cross_set
    )
    out_mine, out_theirs, d_after_cross, grad_in, kept_out, sent_out = feed_forward(
        scalars, normed_ffn, branch_both, branch_theirs, after_cross, gain_rows, ffn_set, w_in
    )
    grad_in = lax.psum_scatter(grad_in, joint, scatter_dimension=0, tiled=True)

    def by_chip(values):
        return values.reshape(grid + (-1, values.shape[-1]))

    def pair_parts(kept, sent):
        return [by_chip(kept), by_chip(swapped(sent))]

    def whole_source(parts):
        return (parts, parts[0].shape[-1], 0)

    every = (0, 1)

    def along_first(first, second, first_share=every, second_share=every):
        return scattered(grid, (first, 2, 2, first_share), (second, 1, 1, second_share))

    def along_second(first, second):
        return scattered(
            grid, ([whole_source(first)], 1, 1, every), ([whole_source(second)], 2, 1, every)
        )

    def along_z(first, second):
        return scattered(grid, ([whole_source(first), whole_source(second)], 0, 0, every))[0]

    ffn_out = pair_parts(kept_out, sent_out)
    d_att = cross_branch(d_after_cross, cross_set)
    d_att, ffn_out = tied(d_att, ffn_out)
    by_rows = ratio * rows // 2 % 16 == 0
    if by_rows:
        ffn_first, ffn_second = along_first(
            [(ffn_out, half, 0)], [(ffn_out, half, 0)], (0, 2), (1, 2)
        )
    else:
        ffn_first, ffn_second = along_first(
            [(ffn_out, 2 * LANES, 0)], [(ffn_out, half - 2 * LANES, 2)]
        )
    d_att, _ = tied(d_att, (ffn_first[0], ffn_second[0]))
    d_after_self, d_att, kept_c, sent_c, encoded_mine, encoded_their = cross_backward(
        scalars,
        cross_queries,
        ckv,
        d_att,
        cross_lse,
        d_after_cross,
        after_self,
        normed_cross,
        cross_attended,
        attended,
        encoded,
        gain_rows,
        cross_set,
        self_set,
    )
    d_att, (ffn_first, ffn_second) = tied(d_att, (ffn_first, ffn_second))
    ffn_first, ffn_second = along_second(ffn_first, ffn_second)
    d_att, _ = tied(d_att, (ffn_first[0], ffn_second[0]))
    cross_all = pair_parts(kept_c, sent_c)
    d_first = self_backward_first(seg_row, seg_col, qkv, d_att, self_lse)
    out_theirs, encoded_their = swapped(out_theirs), swapped(encoded_their)
    d_first, (ffn_first, ffn_second, cross_all, out_theirs, encoded_their) = tied(
        d_first, (ffn_first, ffn_second, cross_all, out_theirs, encoded_their)
    )
    cross_first, cross_second = along_first(
        [(cross_all, half, 3), (cross_all, half, 0), (cross_all, half, 4)],
        [(cross_all, half, 1), (cross_all, half, 2)],
    )
    ffn_parts = along_z(ffn_first, ffn_second)
    d_first, _ = tied(d_first, (ffn_parts[0], cross_first[0], cross_second[0]))
    *self_grads, d_last = self_backward_last(
        scalars, seg_row, seg_col, qkv, d_att, self_lse, d_first, normed_self
    )
    self_grads, ffn_parts = tied(self_grads, ffn_parts)
    self_qkv = [pair_parts(self_grads[i], self_grads[3 + i]) for i in range(3)]
    d_last, (cross_first, cross_second) = tied(d_last, (cross_first, cross_second))
    cross_first, cross_second = along_second(cross_first, cross_second)
    self_qkv, _ = tied(self_qkv, (cross_first[0], cross_second[0]))
    self_first, self_second = along_first(
        [(self_qkv[0], half, 0), (self_qkv[2], 2 * LANES, 0)],
        [(self_qkv[1], half, 0), (self_qkv[2], half - 2 * LANES, 2)],
    )
    d_last, _ = tied(d_last, (self_first[0], self_second[0]))
    hidden_mine, hidden_their = self_input(
        scalars, d_first, d_last, d_after_self, hidden, gain_rows, self_set
    )
    def matrices(mine, places):
        other = swapped(mine)
        results = []
        for spans in places:
            halves = [
                jnp.concatenate([values[:, start:end] for start, end in spans], axis=1)
                for values in (mine, other)
            ]
            results.append(in_order(*halves, 1))
        return results

    def gain_gradient(gain, *pairs):
        weighed = [weight_rows.astype(F32) * grad for weight_rows, grad in pairs]
        return jnp.sum(total(weighed), axis=1) / gain.astype(F32)

    hidden_their, (self_first, self_second, cross_first, cross_second) = tied(
        hidden_their, (self_first, self_second, cross_first, cross_second)
    )
    ffn_sum = total(ffn_parts)
    if by_rows:
        ffn_sum = jnp.concatenate([ffn_sum[:, :half], ffn_sum[:, half:]], axis=0)
    (grad_ffn_out,) = matrices(ffn_sum, [[(0, half)]])
    (cross_first, cross_second), grad_ffn_out = tied((cross_first, cross_second), grad_ffn_out)
    cross_parts = along_z(cross_first, cross_second)
    (self_first, self_second), _ = tied((self_first, self_second), cross_parts[0])
    self_first, self_second = along_second(self_first, self_second)
    (cross_parts, hidden_their, grad_in), _ = tied(
        (cross_parts, hidden_their, grad_in), (self_first[0], self_second[0])
    )
    self_parts = along_z(self_first, self_second)
    cross_grads = matrices(total(cross_parts), [[(i * half, (i + 1) * half)] for i in range(5)])
    grad_co, grad_cq, grad_o, grad_ck, grad_cv = cross_grads
    grad_in = lax.all_gather(grad_in, "seq", axis=0, tiled=True).astype(F32)
    done = (
        returned(out_mine, out_theirs),
        returned(hidden_mine, swapped(hidden_their)),
        returned(encoded_mine, encoded_their),
        gain_gradient(gain_cross, (w_cross_query, grad_cq)),
        gain_gradient(gain_ffn, (w_ffn_in, grad_in)),
    )
    self_parts, (done, cross_grads, grad_in) = tied(self_parts, (done, cross_grads, grad_in))
    grad_co, grad_cq, grad_o, grad_ck, grad_cv = cross_grads
    split = half + 2 * LANES
    grad_q, grad_k, grad_v = matrices(
        total(self_parts),
        [
            [(0, half)],
            [(split, split + half)],
            [(half, split), (split + half, 3 * half)],
        ],
    )
    return done[:3] + (
        grad_q,
        grad_k,
        grad_v,
        grad_o,
        grad_cq,
        grad_ck,
        grad_cv,
        grad_co,
        grad_in,
        grad_ffn_out,
        gain_gradient(gain_self, (w_query, grad_q), (w_key, grad_k), (w_value, grad_v)),
    ) + done[3:]


def solution(mesh):
    tokens = P(None, "dp", "seq", None)
    rows = P("dp", None)
    gain = P("dp")
    return jax.shard_map(
        on_device,
        mesh=mesh,
        in_specs=(tokens, tokens, P(None, "dp", "seq"), P(None, "dp"), tokens)
        + (rows,) * 10
        + (gain,) * 3,
        out_specs=(tokens,) * 3 + (rows,) * 10 + (gain,) * 3,
        check_vma=False,
    )
```
